32 devices in a mesh: rep: 8 (over y, x, core), shard: 4 (over z).
Axes of the slice: x: 2, y: 2, z: 4, core: 2. Of those that a mesh axis runs over, the one named last changes fastest.
Arguments:
- tokens: bfloat16 [2, 8, 2048, 1536], P(None, 'rep', 'shard'), may hold values from -6 to 6
- cotangent: bfloat16 [2, 8, 2048, 1536], P(None, 'rep', 'shard'), may hold values from -6 to 6
- routes: int32 [2, 8, 2048, 2], P(None, 'rep', 'shard'), may hold values from 0 to 3, all different within a row; in each aligned block of 512 rows (0 to 511, 512 to 1023, ..., all dimensions but the last counted through in order) at most 384 rows name the same one
- lengths: int32 [2, 8, 3], replicated, may hold values from 1 to 2046, as said below
- attn_gain: bfloat16 [1536], P('shard'), may hold values from 0.5 to 1.5
- w_query: bfloat16 [1536, 1536], P('shard'), may hold values from -0.15625 to 0.15625
- w_key: bfloat16 [1536, 512], P('shard'), may hold values from -0.15625 to 0.15625
- w_value: bfloat16 [1536, 512], P('shard'), may hold values from -0.15625 to 0.15625
- w_out: bfloat16 [1536, 1536], P('shard'), may hold values from -2.5 to 2.5
- moe_gain: bfloat16 [1536], P('shard'), may hold values from 0.5 to 1.5
- w_router: bfloat16 [1536, 4], P('shard'), may hold values from -0.109375 to 0.109375
- w_gate: bfloat16 [4, 1536, 1024], P(None, 'shard'), may hold values from -0.15625 to 0.15625
- w_up: bfloat16 [4, 1536, 1024], P(None, 'shard'), may hold values from -0.15625 to 0.15625
- w_down: bfloat16 [4, 1024, 1536], P(None, 'shard'), may hold values from -0.25 to 0.25
Outputs:
- block_out: bfloat16 [2, 8, 2048, 1536], P(None, 'rep', 'shard')
- input_grad: bfloat16 [2, 8, 2048, 1536], P(None, 'rep', 'shard')
- grad_attn_gain: float32 [1536], P('shard')
- grad_query: float32 [1536, 1536], P('shard')
- grad_key: float32 [1536, 512], P('shard')
- grad_value: float32 [1536, 512], P('shard')
- grad_out: float32 [1536, 1536], P('shard')
- grad_moe_gain: float32 [1536], P('shard')
- grad_router: float32 [1536, 4], P('shard')
- grad_gate: float32 [4, 1536, 1024], P(None, 'shard')
- grad_up: float32 [4, 1536, 1024], P(None, 'shard')
- grad_down: float32 [4, 1024, 1536], P(None, 'shard')
The draws below stay inside these ranges and needn't reach their ends.
Inputs may be any that keep to these rules, and one draw needn't show every extreme that they name: `routes`: each row names 2 different experts. Within the rows of one device for one micro-batch (aligned blocks of 512 rows) no expert is named more than 384 times, a bound that some block reaches. Each row holds 3 document lengths in order that sum to 2048; its largest is 2048 / 3 or more, and some row's largest is 2046.
All inputs are finite; a program needn't handle non-finite values.
Results may differ from the reference program's by a relative error of at most 0.023.
Values may be sent and summed in bfloat16 or wider, within the bound.
No kernel may reach another device: no remote copies, remote signals or barrier semaphores. Data moves between devices by JAX's collectives and lax.ppermute only.
A program may use at most 384 MiB of HBM per device.

```python
import math
from functools import partial
import jax
import jax.numpy as jnp
import numpy as np
from jax import lax

D = 1536
HEADS = 24
KV_HEADS = 8
HEAD = 64
GROUP = 3
FF = 1024
EXPERTS = 4
TOP = 2
MB = 2
DOCS = 3
STREAM = 2048
TOK_DEV = 512
CAP = 384
N_REP = 8


def draw_lengths(key, part):
    row_count = MB * N_REP
    key_large, key_split, key_turn = jax.random.split(key, 3)
    least_large = (STREAM + DOCS - 1) // DOCS
    most_large = STREAM - DOCS + 1
    largest = jax.random.randint(key_large, (row_count,), least_large, most_large + 1)
    largest = largest.at[0].set(most_large)
    rest = STREAM - largest
    lower = jnp.maximum(1, rest - largest)
    upper = jnp.minimum(largest, rest - 1)
    spread = jax.random.randint(key_split, (row_count,), 0, 1048576)
    first = lower + spread % (upper - lower + 1)
    second = rest - first
    table = jnp.stack([largest, first, second], axis=1)
    turn = jax.random.randint(key_turn, (row_count,), 0, 3)
    order = (jnp.arange(3, dtype=jnp.int32)[None, :] + turn[:, None]) % 3
    placed = jnp.take_along_axis(table, order, axis=1)
    return placed.reshape(MB, N_REP, DOCS).astype(jnp.int32)


def block_levels(own_key, extent, shards, smallest, high):
    loudness, own = 1.0, jax.random.fold_in(own_key, 6)
    for dim, shards_of in shards:
        heights = jnp.exp(jax.random.uniform(jax.random.fold_in(own, dim), (shards_of,), jnp.float32, smallest / len(shards), high / len(shards)))
        loudness = loudness * jnp.repeat(heights, extent[dim] // shards_of).reshape([-1 if axis == dim else 1 for axis in range(len(extent))])
    return loudness


def assign_block(rng, own, number, rows, amount, top, limit, slope):
    sequence = jax.random.permutation(rng, amount)
    heavy_load, usual = load_shares(amount, rows * top, limit, slope, True), load_shares(amount, rows * top, limit, slope, False)
    places = jnp.arange(amount)

    def named(tallies, offset_by):
        used = int((tallies > 0).sum())
        fixed = max(1, used // 4)
        shifted = fixed + (places - fixed + offset_by * (used - fixed)) % max(1, amount - fixed)
        return jnp.zeros((amount,), jnp.int32).at[sequence[jnp.where(places < fixed, places, shifted)]].set(jnp.asarray(tallies, jnp.int32))

    tallies = jnp.where(number % 4 == 0, named(heavy_load, number // 4), named(usual, number - number // 4 - 1))
    mixed = jax.random.permutation(jax.random.fold_in(own, 3), amount)
    giver, taker = mixed[0:amount // 2 * 2:2], mixed[1:amount // 2 * 2:2]
    margin = jnp.minimum(tallies[giver] - 1, limit - tallies[taker]) // 2
    margin = jnp.where((giver == sequence[0]) | (taker == sequence[0]) | (tallies[taker] == 0), 0, jnp.maximum(margin, 0))
    shifted = jax.random.randint(jax.random.fold_in(own, 4), (amount // 2,), 0, 1 << 20) % (margin + 1)
    tallies = tallies.at[giver].add(-shifted).at[taker].add(shifted)
    items = jnp.searchsorted(jnp.cumsum(tallies), jnp.arange(rows * top), side="right").astype(jnp.int32)
    table = items.reshape(top, rows).T
    table = table[jax.random.permutation(jax.random.fold_in(own, 1), rows)]
    offset_by = jax.random.randint(jax.random.fold_in(own, 2), (rows, 1), 0, top)
    return jnp.take_along_axis(table, (jnp.arange(top)[None, :] + offset_by) % top, axis=1)


def load_shares(amount, total, reach, slope, full):
    portions = [(1 << 20) // math.isqrt(standing ** slope) + 1 for standing in range(1, amount + 1)]
    largest = reach if full else min(reach, max(-(-total // amount), total * portions[0] // sum(portions)))
    least = 1 if total - largest >= amount - 1 else 0
    holding, surplus = [largest] + [least] * (amount - 1), total - largest - least * (amount - 1)
    while surplus > 0:
        candidates = [i for i in range(1, amount) if holding[i] < largest] or [i for i in range(1, amount) if holding[i] < reach]
        whole, remaining = sum([portions[i] for i in candidates]), surplus
        for i in candidates:
            extra = min(reach - holding[i], max(1, remaining * portions[i] // whole), surplus)
            holding[i] = holding[i] + extra
            surplus = surplus - extra
    return np.array(holding)


def normal_values(stream_key, shape, scale, bound, cuts=(), kind=jnp.bfloat16):
    gain = block_levels(stream_key, shape, cuts, -0.22, 0.18) if cuts else 1.0
    drawn = jax.random.normal(stream_key, shape, jnp.float32) * scale * gain
    return jnp.minimum(jnp.maximum(drawn, -bound), bound).astype(kind)


def setup_inputs(seed: int = 0) -> dict:
    key_of = jax.random.split(jax.random.key(seed), 15)
    tokens = normal_values(key_of[0], (MB, N_REP, STREAM, D), 1.0, 6.0, ((1, 8), (2, 4)))
    cotangent = normal_values(key_of[1], (MB, N_REP, STREAM, D), 1.0, 6.0, ((1, 8), (2, 4)))
    routes_keys = jax.random.split(jax.random.fold_in(key_of[2], 1), MB * N_REP * STREAM // TOK_DEV)
    routes_turns = jax.random.permutation(jax.random.fold_in(key_of[2], 3), MB * N_REP * STREAM // TOK_DEV)
    routes = jax.vmap(lambda own, number: assign_block(jax.random.fold_in(key_of[2], 2), own, number, TOK_DEV, EXPERTS, TOP, CAP, 1))(routes_keys, routes_turns).reshape((MB, N_REP, STREAM, TOP))
    lengths = draw_lengths(jax.random.fold_in(key_of[14], 71), 0)
    attn_gain = jnp.clip(1.0 + 0.1 * jax.random.normal(key_of[4], (D,), jnp.float32), 0.5, 1.5).astype(jnp.bfloat16)
    w_query = normal_values(key_of[5], (D, HEADS * HEAD), D ** -0.5, 0.15625, ((0, 4),))
    w_key = normal_values(key_of[6], (D, KV_HEADS * HEAD), D ** -0.5, 0.15625, ((0, 4),))
    w_value = normal_values(key_of[7], (D, KV_HEADS * HEAD), D ** -0.5, 0.15625, ((0, 4),))
    w_out = normal_values(key_of[8], (HEADS * HEAD, D), 6 ** -0.5, 2.5, ((0, 4),))
    moe_gain = jnp.clip(1.0 + 0.1 * jax.random.normal(key_of[9], (D,), jnp.float32), 0.5, 1.5).astype(jnp.bfloat16)
    w_router = normal_values(key_of[10], (D, EXPERTS), (2 * D) ** -0.5, 0.109375, ((0, 4),))
    w_gate = normal_values(key_of[11], (EXPERTS, D, FF), D ** -0.5, 0.15625, ((1, 4),))
    w_up = normal_values(key_of[12], (EXPERTS, D, FF), D ** -0.5, 0.15625, ((1, 4),))
    w_down = normal_values(key_of[13], (EXPERTS, FF, D), (FF // 2) ** -0.5, 0.25, ((1, 4),))
    return dict(tokens=tokens, cotangent=cotangent, routes=routes, lengths=lengths, attn_gain=attn_gain, w_query=w_query, w_key=w_key, w_value=w_value, w_out=w_out, moe_gain=moe_gain, w_router=w_router, w_gate=w_gate, w_up=w_up, w_down=w_down)


@jax.custom_vjp
def low(v):
    return lax.optimization_barrier(v.astype(jnp.bfloat16)).astype(jnp.float32)

@jax.custom_vjp
def low_back(v):
    return v

def low_keep(v):
    return (low(v), None)

def low_pass(kept, grad):
    return (grad,)

def back_keep(v):
    return (v, None)

def back_low(kept, grad):
    return (low(grad),)
low.defvjp(low_keep, low_pass)
low_back.defvjp(back_keep, back_low)
EPSILON = 1e-05
NEGATIVE = -1e+30
PRECISE = lax.Precision.HIGHEST

def product(left, right):
    return jnp.dot(left, right, precision=PRECISE, preferred_element_type=jnp.float32)

def norm_rows(values, gain_row):
    row_scale = lax.rsqrt(lax.optimization_barrier(jnp.mean(values * values, axis=-1, keepdims=True)) + EPSILON)
    return values * row_scale * gain_row

def doc_mask(lengths_row):
    bounds = jnp.cumsum(lengths_row)[:-1]
    places = jnp.arange(STREAM, dtype=jnp.int32)
    doc_ids = lax.optimization_barrier(jnp.sum((places[:, None] >= bounds[None, :]).astype(jnp.int32), axis=1))
    return (doc_ids[:, None] == doc_ids[None, :]) & (places[:, None] >= places[None, :])

def head_attend(q_head, k_head, v_head, allowed):
    scores = jnp.einsum('tgc,sc->gts', q_head, k_head, precision=PRECISE) * HEAD ** (-0.5)
    scores = low_back(scores)
    scores = jnp.where(allowed[None], scores, NEGATIVE)
    weights = low(jax.nn.softmax(scores, axis=-1))
    return jnp.einsum('gts,sc->tgc', weights, v_head, precision=PRECISE)

def stream_forward(inputs, route_rows, allowed, weights):
    gain_one, w_query, w_key, w_value, w_out, gain_two, w_router, w_gate, w_up, w_down = weights
    normed = low(norm_rows(inputs, gain_one))
    queries = low_back(low(product(normed, w_query)))
    key_rows = low_back(low(product(normed, w_key)))
    value_rows = low_back(low(product(normed, w_value)))
    q_heads = jnp.transpose(queries.reshape(STREAM, KV_HEADS, GROUP, HEAD), (1, 0, 2, 3))
    k_heads = jnp.transpose(key_rows.reshape(STREAM, KV_HEADS, HEAD), (1, 0, 2))
    v_heads = jnp.transpose(value_rows.reshape(STREAM, KV_HEADS, HEAD), (1, 0, 2))
    attend = jax.checkpoint(partial(head_attend, allowed=allowed))
    head_mix = lax.map(lambda head_items: attend(head_items[0], head_items[1], head_items[2]), (q_heads, k_heads, v_heads))
    attn_rows = jnp.transpose(head_mix, (1, 0, 2, 3)).reshape(STREAM, HEADS * HEAD)
    attn_rows = low_back(low(attn_rows))
    branch = low_back(product(attn_rows, w_out))
    residual = inputs + branch
    normed_two = low(norm_rows(residual, gain_two))
    logits = low_back(product(normed_two, w_router))
    route_hot = jax.nn.one_hot(route_rows, EXPERTS, dtype=jnp.float32)
    chosen = lax.optimization_barrier(jnp.sum(logits[:, None, :] * route_hot, axis=2))
    gate_share = jax.nn.softmax(chosen, axis=1)
    shares = lax.optimization_barrier(jnp.sum(gate_share[:, :, None] * route_hot, axis=1))
    summed = residual
    for expert in range(EXPERTS):
        gate_rows = low_back(low(product(normed_two, w_gate[expert])))
        up_rows = low_back(low(product(normed_two, w_up[expert])))
        hidden = low(jax.nn.silu(gate_rows) * up_rows)
        expert_out = low_back(product(hidden, w_down[expert]))
        summed = summed + shares[:, expert:expert + 1] * expert_out
    return summed

def reference(tokens, cotangent, routes, lengths, attn_gain, w_query, w_key, w_value, w_out, moe_gain, w_router, w_gate, w_up, w_down):
    weights = tuple((weight.astype(jnp.float32) for weight in (attn_gain, w_query, w_key, w_value, w_out, moe_gain, w_router, w_gate, w_up, w_down)))
    count = MB * N_REP
    stream_inputs = tokens.reshape(count, STREAM, D)
    stream_grads = cotangent.reshape(count, STREAM, D)
    stream_routes = routes.reshape(count, STREAM, TOP)
    stream_lengths = lengths.reshape(count, DOCS)

    def advance(totals, stream_item):
        inputs_row, grads_row, route_row, length_row = stream_item
        allowed = doc_mask(length_row)

        def forward(inputs_in, weights_in):
            return stream_forward(inputs_in, route_row, allowed, weights_in)
        output, pullback = jax.vjp(forward, inputs_row.astype(jnp.float32), weights)
        grad_in, grad_weights = pullback(grads_row.astype(jnp.float32))
        totals = jax.tree.map(jnp.add, totals, grad_weights)
        return (totals, (output.astype(jnp.bfloat16), grad_in.astype(jnp.bfloat16)))
    zeros = jax.tree.map(jnp.zeros_like, weights)
    totals, (outputs, grad_inputs) = lax.scan(advance, zeros, (stream_inputs, stream_grads, stream_routes, stream_lengths))
    block_out = outputs.reshape(MB, N_REP, STREAM, D)
    input_grad = grad_inputs.reshape(MB, N_REP, STREAM, D)
    return (block_out, input_grad, totals[0], totals[1], totals[2], totals[3], totals[4], totals[5], totals[6], totals[7], totals[8], totals[9])
```

```python
import functools
import math

import jax
import jax.numpy as jnp
from jax import lax
from jax.experimental import pallas as pl
from jax.experimental.pallas import tpu as pltpu
from jax.sharding import PartitionSpec as P

HEAD = 64
EPSILON = 1e-05
NEGATIVE = -1e30
F32 = jnp.float32
BF16 = jnp.bfloat16
LOG2_SCALE = HEAD ** (-0.5) * math.log2(math.e)
SCALE = HEAD ** (-0.5)
BOTH = ("rep", "shard")


def dot(left, right, left_dim, right_dim, kind=F32):
    return lax.dot_general(
        left, right, (((left_dim,), (right_dim,)), ((), ())), preferred_element_type=F32
    ).astype(kind)


def block_counts(length):
    return min(512, length), min(256, length)


def visible_mask(index, width, first_key, first_query, starts):
    rows = first_key + lax.broadcasted_iota(jnp.int32, (width, starts.shape[1]), 0)
    columns = first_query + lax.broadcasted_iota(jnp.int32, (1, starts.shape[1]), 1)
    return (rows >= starts) & (rows <= columns)


def side_by_side(block, group):
    return jnp.concatenate([block[g * HEAD : (g + 1) * HEAD, :] for g in range(group)], axis=1)


def three_loops(ranges, place, step, carry):
    low, full_low, full_high, high = (ranges[place, n] for n in range(4))
    carry = lax.fori_loop(low, full_low, functools.partial(step, True), carry)
    carry = lax.fori_loop(full_low, full_high, functools.partial(step, False), carry)
    return lax.fori_loop(full_high, high, functools.partial(step, True), carry)


def forward_kernel(ranges, q_ref, k_ref, v_ref, starts_ref, o_ref, stat_ref, k_rows, *, group, wide):
    place = pl.program_id(1)
    q_width = q_ref.shape[1]

    @pl.when(place == 0)
    def _():
        k_rows[...] = k_ref[...].T

    queries = side_by_side(q_ref[...], group)
    starts = starts_ref[...]

    def step(masked, index, carry):
        high, total, mixed = carry
        first = pl.multiple_of(index * wide, wide)
        scores = (
            jnp.dot(k_rows[pl.ds(first, wide), :], queries, preferred_element_type=F32)
            * LOG2_SCALE
        )
        if masked:
            seen = visible_mask(index, wide, first, place * q_width, starts)
            scores = jnp.where(jnp.concatenate([seen] * group, axis=1), scores, NEGATIVE)
        new_high = jnp.maximum(high, jnp.max(scores, axis=0, keepdims=True))
        weights = jnp.exp2(scores - new_high)
        fade = jnp.exp2(high - new_high)
        total = total * fade + jnp.sum(weights, axis=0, keepdims=True)
        mixed = mixed * fade + jnp.dot(
            v_ref[:, pl.ds(first, wide)], weights.astype(BF16), preferred_element_type=F32
        )
        return new_high, total, mixed

    columns = group * q_width
    high, total, mixed = three_loops(
        ranges,
        place,
        step,
        (
            jnp.full((1, columns), NEGATIVE, F32),
            jnp.zeros((1, columns), F32),
            jnp.zeros((HEAD, columns), F32),
        ),
    )
    mixed = (mixed / total).astype(BF16)
    stat = high + jnp.log2(total)
    for g in range(group):
        span = slice(g * q_width, (g + 1) * q_width)
        o_ref[g * HEAD : (g + 1) * HEAD, :] = mixed[:, span]
        stat_ref[0, g : g + 1, :] = stat[:, span]


def backward_kernel(
    ranges, q_ref, k_ref, v_ref, o_ref, g_ref, stat_ref, starts_ref,
    dq_ref, dk_ref, dv_ref, k_rows, v_rows, dk_sum, dv_sum, *, group, wide,
):
    place = pl.program_id(1)
    q_width = q_ref.shape[1]

    @pl.when(place == 0)
    def _():
        k_rows[...] = k_ref[...].T
        v_rows[...] = v_ref[...].T
        dk_sum[...] = jnp.zeros_like(dk_sum)
        dv_sum[...] = jnp.zeros_like(dv_sum)

    queries = side_by_side(q_ref[...], group)
    grads = side_by_side(g_ref[...], group)
    outs = side_by_side(o_ref[...], group)
    inner = jnp.sum(grads.astype(F32) * outs.astype(F32), axis=0, keepdims=True)
    stat = jnp.concatenate([stat_ref[0, g : g + 1, :] for g in range(group)], axis=1)
    starts = starts_ref[...]

    def step(masked, index, dq):
        first = pl.multiple_of(index * wide, wide)
        span = pl.ds(first, wide)
        scores = jnp.dot(k_rows[span, :], queries, preferred_element_type=F32) * LOG2_SCALE
        chances = jnp.exp2(scores - stat)
        if masked:
            seen = visible_mask(index, wide, first, place * q_width, starts)
            chances = jnp.where(jnp.concatenate([seen] * group, axis=1), chances, 0.0)
        slopes = jnp.dot(v_rows[span, :], grads, preferred_element_type=F32)
        pull = (chances * (slopes - inner)).astype(BF16)
        dv_sum[:, span] += dot(grads, chances.astype(BF16), 1, 1)
        dk_sum[:, span] += dot(queries, pull, 1, 1)
        return dq + jnp.dot(k_ref[:, span], pull, preferred_element_type=F32)

    dq = three_loops(ranges, place, step, jnp.zeros((HEAD, group * q_width), F32))
    dq = (dq * SCALE).astype(BF16)
    for g in range(group):
        dq_ref[g * HEAD : (g + 1) * HEAD, :] = dq[:, g * q_width : (g + 1) * q_width]

    @pl.when(place == pl.num_programs(1) - 1)
    def _():
        dk_ref[...] = (dk_sum[...] * SCALE).astype(BF16)
        dv_ref[...] = dv_sum[...].astype(BF16)


def block_ranges(starts, q_width, wide):
    length = starts.shape[1]
    count = length // q_width
    first_query = jnp.arange(count, dtype=jnp.int32) * q_width
    low = starts[0, ::q_width] // wide
    full_low = (starts[0, q_width - 1 :: q_width] + wide - 1) // wide
    full_high = (first_query + 1) // wide
    full_high = first_query // wide
    high = (first_query + q_width) // wide
    full_low = jnp.clip(full_low, low, jnp.maximum(full_high, low))
    full_high = jnp.maximum(full_high, full_low)
    return jnp.stack([low, full_low, full_high, high], axis=1)


def attention_specs(heads, group, length, q_width):
    per_query = pl.BlockSpec((group * HEAD, q_width), lambda h, i, r: (h, i))
    per_head = pl.BlockSpec((HEAD, length), lambda h, i, r: (h, 0))
    stat = pl.BlockSpec((1, group, q_width), lambda h, i, r: (h, 0, i))
    starts = pl.BlockSpec((1, q_width), lambda h, i, r: (0, i))
    return per_query, per_head, stat, starts


def attend_forward(q_t, k_t, v_t, starts):
    length = q_t.shape[1]
    heads = k_t.shape[0] // HEAD
    group = q_t.shape[0] // k_t.shape[0]
    q_width, wide = block_counts(length)
    per_query, per_head, stat, start_spec = attention_specs(heads, group, length, q_width)
    pairs = heads * group * length * length // 2
    return pl.pallas_call(
        functools.partial(forward_kernel, group=group, wide=wide),
        out_shape=(
            jax.ShapeDtypeStruct(q_t.shape, BF16),
            jax.ShapeDtypeStruct((heads, group, length), F32),
        ),
        grid_spec=pltpu.PrefetchScalarGridSpec(
            num_scalar_prefetch=1,
            grid=(heads, length // q_width),
            in_specs=[per_query, per_head, per_head, start_spec],
            out_specs=(per_query, stat),
            scratch_shapes=[pltpu.VMEM((length, HEAD), BF16)],
        ),
        compiler_params=pltpu.CompilerParams(
            dimension_semantics=("arbitrary", "arbitrary"), vmem_limit_bytes=48 << 20
        ),
        cost_estimate=pl.CostEstimate(
            flops=pairs * HEAD * 4 * 4, transcendentals=pairs, bytes_accessed=q_t.size * 8
        ),
        name="attend_forward",
    )(block_ranges(starts, q_width, wide), q_t, k_t, v_t, starts)


def attend_backward(q_t, k_t, v_t, o_t, g_t, stat_rows, starts):
    length = q_t.shape[1]
    heads = k_t.shape[0] // HEAD
    group = q_t.shape[0] // k_t.shape[0]
    q_width, wide = block_counts(length)
    per_query, per_head, stat, start_spec = attention_specs(heads, group, length, q_width)
    pairs = heads * group * length * length // 2
    return pl.pallas_call(
        functools.partial(backward_kernel, group=group, wide=wide),
        out_shape=(
            jax.ShapeDtypeStruct(q_t.shape, BF16),
            jax.ShapeDtypeStruct(k_t.shape, BF16),
            jax.ShapeDtypeStruct(k_t.shape, BF16),
        ),
        grid_spec=pltpu.PrefetchScalarGridSpec(
            num_scalar_prefetch=1,
            grid=(heads, length // q_width),
            in_specs=[per_query, per_head, per_head, per_query, per_query, stat, start_spec],
            out_specs=(per_query, per_head, per_head),
            scratch_shapes=[
                pltpu.VMEM((length, HEAD), BF16),
                pltpu.VMEM((length, HEAD), BF16),
                pltpu.VMEM((HEAD, length), F32),
                pltpu.VMEM((HEAD, length), F32),
            ],
        ),
        compiler_params=pltpu.CompilerParams(
            dimension_semantics=("arbitrary", "arbitrary"), vmem_limit_bytes=48 << 20
        ),
        cost_estimate=pl.CostEstimate(
            flops=pairs * HEAD * 10 * 4, transcendentals=pairs, bytes_accessed=q_t.size * 16
        ),
        name="attend_backward",
    )(block_ranges(starts, q_width, wide), q_t, k_t, v_t, o_t, g_t, stat_rows, starts)


class Place:
    def __init__(self):
        self.reps = lax.axis_size("rep")
        self.shards = lax.axis_size("shard")
        self.quarters = self.reps // 2
        self.chips = self.shards // 4
        rep = lax.axis_index("rep")
        self.core = rep % 2
        self.quarter = rep // 2
        self.shard = lax.axis_index("shard")
        self.stream = self.shard // self.chips
        self.batch = self.stream // 2
        self.source = self.quarter * 2 + self.stream % 2
        self.chip = self.shard % self.chips

    def across(self, array, bit):
        return lax.ppermute(array, "rep", [(i, i ^ bit) for i in range(self.reps)])

    def swap(self, array):
        return self.across(array, 1)

    def moves(self, turn, home):
        pairs = []
        for quarter in range(self.quarters):
            for core in range(2):
                for shard in range(self.shards):
                    batch = turn ^ (shard & 1)
                    member = shard // 2
                    stream = 2 * batch + core
                    start = (quarter * 2 + core) * self.shards + shard
                    end = (
                        (quarter * 2 + member % 2) * self.shards
                        + stream * self.chips
                        + member // 2
                    )
                    pairs.append((end, start) if home else (start, end))
        return pairs

    def to_streams(self, array):
        odd = self.shard % 2 == 1
        got = [
            lax.ppermute(
                jnp.where(odd, array[1 - turn], array[turn]), BOTH, self.moves(turn, False)
            )
            for turn in range(2)
        ]
        swapped = self.batch == 1
        return jnp.concatenate(
            [jnp.where(swapped, got[1], got[0]), jnp.where(swapped, got[0], got[1])], axis=0
        )

    def to_homes(self, array):
        half = array.shape[0] // 2
        swapped = self.batch == 1
        parts = [array[:half], array[half:]]
        got = [
            lax.ppermute(
                jnp.where(swapped, parts[1 - turn], parts[turn]), BOTH, self.moves(turn, True)
            )
            for turn in range(2)
        ]
        odd = self.shard % 2 == 1
        return jnp.stack([jnp.where(odd, got[1], got[0]), jnp.where(odd, got[0], got[1])])

    def ordered(self, mine, other, axis):
        return jnp.where(
            self.core == 0,
            jnp.concatenate([mine, other], axis=axis),
            jnp.concatenate([other, mine], axis=axis),
        )

    def halves(self, array, axis):
        size = array.shape[axis] // 2
        mine = lax.dynamic_slice_in_dim(array, self.core * size, size, axis)
        other = lax.dynamic_slice_in_dim(array, (1 - self.core) * size, size, axis)
        return mine, other

    def chip_exchange(self, array, split, join):
        if self.chips == 1:
            return array
        size = array.shape[split] // self.chips
        width = array.shape[join]
        shape = list(array.shape)
        shape[split] = size
        shape[join] = width * self.chips
        result = jnp.zeros(shape, array.dtype)
        for step in range(self.chips):
            other = self.chip ^ step
            piece = lax.dynamic_slice_in_dim(array, other * size, size, split)
            if step:
                piece = lax.ppermute(
                    piece, "shard", [(i, i ^ step) for i in range(self.shards)]
                )
            result = lax.dynamic_update_slice_in_dim(result, piece, other * width, join)
        return result

    def fetch(self, own, bits):
        piece = lax.dynamic_index_in_dim(own, self.quarter, 1, keepdims=False)
        count = self.shards
        ups, downs = [], []
        up = down = piece
        for step in range(1, count):
            up = lax.ppermute(up, "shard", [(i, i + 1) for i in range(step - 1, count - 1)])
            down = lax.ppermute(down, "shard", [(i, i - 1) for i in range(1, count - step + 1)])
            ups.append(up)
            downs.append(down)
        along = jnp.stack(
            [
                jnp.where(self.shard >= step, ups[step - 1], downs[count - step - 1])
                for step in range(1, count)
            ]
        )
        found = {0: along}
        for bit in bits:
            found.update(
                {key ^ bit: self.across(array, 2 * bit) for key, array in list(found.items())}
            )
        return [found[key] for key in range(self.quarters)]

    def assemble(self, own, found, swapped=None):
        parts, quarters, rows, columns = own.shape
        shards = self.shards
        sides = 1 if swapped is None else 2
        places = jnp.stack([self.shard, self.quarter, self.core]).astype(jnp.int32)

        def kernel(places_ref, *refs):
            out_ref, sem = refs[-2], refs[-1]
            shard, quarter, core = places_ref[0], places_ref[1], places_ref[2]
            copies = []
            for side in range(sides):
                own_ref = refs[side * (quarters + 1)]
                found_refs = refs[side * (quarters + 1) + 1 : (side + 1) * (quarters + 1)]
                if sides == 1:
                    span = slice(None)
                else:
                    at = core if side == 0 else 1 - core
                    span = pl.ds(pl.multiple_of(at * columns, 128), columns)
                for part in range(parts):
                    copies.append((own_ref.at[part], out_ref.at[part, shard, :, :, span]))
                    for key in range(quarters):
                        for step in range(1, shards):
                            end = out_ref.at[
                                part, (shard - step + shards) % shards, quarter ^ key, :, span
                            ]
                            copies.append((found_refs[key].at[step - 1, part], end))
            copies = [
                pltpu.make_async_copy(source, end, sem.at[n])
                for n, (source, end) in enumerate(copies)
            ]
            for copy in copies:
                copy.start()
            for copy in copies:
                copy.wait()

        operands = [own, *found]
        if swapped is not None:
            operands += [swapped[0], *swapped[1]]
        shape = (parts, shards, quarters, rows, sides * columns)
        total = parts * shards * quarters * rows * sides * columns
        return pl.pallas_call(
            kernel,
            out_shape=jax.ShapeDtypeStruct(shape, own.dtype),
            in_specs=[pl.BlockSpec(memory_space=pltpu.SMEM)]
            + [pl.BlockSpec(memory_space=pl.ANY)] * len(operands),
            out_specs=pl.BlockSpec(memory_space=pltpu.VMEM),
            scratch_shapes=[
                pltpu.SemaphoreType.DMA((sides * parts * (1 + quarters * (shards - 1)),))
            ],
            compiler_params=pltpu.CompilerParams(vmem_limit_bytes=24 << 20),
            cost_estimate=pl.CostEstimate(flops=0, transcendentals=0, bytes_accessed=total * 4),
            name="assemble",
        )(places, *operands)

    def reduce(self, grad, bits):
        parts, shards, quarters, rows, columns = grad.shape
        held = grad
        kept_bits = list(range(quarters.bit_length() - 1))
        shape = [2] * len(kept_bits)
        held = held.reshape(parts, shards, *shape, rows, columns)
        order = kept_bits[::-1]
        for bit in bits:
            number = bit.bit_length() - 1
            axis = 2 + order.index(number)
            mine = (self.quarter >> number) & 1
            keep = lax.dynamic_index_in_dim(held, mine, axis, keepdims=False)
            give = lax.dynamic_index_in_dim(held, 1 - mine, axis, keepdims=False)
            got = self.across(give.astype(BF16), 2 * bit)
            held = (keep.astype(F32) + got.astype(F32)).astype(BF16)
            order.remove(number)
        up = down = None
        for step in range(1, shards):
            index = jnp.minimum(self.shard + shards - step, shards - 1)
            send = lax.dynamic_index_in_dim(held, index, 1, keepdims=False)
            if up is not None:
                send = (send.astype(F32) + up.astype(F32)).astype(BF16)
            up = lax.ppermute(send, "shard", [(i, i + 1) for i in range(step)])
            index = jnp.maximum(self.shard - shards + step, 0)
            send = lax.dynamic_index_in_dim(held, index, 1, keepdims=False)
            if down is not None:
                send = (send.astype(F32) + down.astype(F32)).astype(BF16)
            down = lax.ppermute(
                send, "shard", [(i, i - 1) for i in range(shards - step, shards)]
            )
        own = lax.dynamic_index_in_dim(held, self.shard, 1, keepdims=False)
        total = (own.astype(F32) + up.astype(F32) + down.astype(F32)).astype(BF16)
        whole = lax.all_gather(total, "rep", axis=0, tiled=False)
        return whole.reshape(quarters, 2, parts, rows, columns)


def rms_scale(rows_in):
    return lax.rsqrt(jnp.mean(rows_in * rows_in, axis=-1, keepdims=True) + EPSILON)


def norm_back(rows_in, row_scale, gain_row, grad_normed):
    grad_gain = jnp.sum(grad_normed * rows_in * row_scale, axis=0)
    scaled = grad_normed * gain_row
    scale_cubed = row_scale * row_scale * row_scale
    grad_rows = row_scale * scaled - rows_in * scale_cubed * jnp.mean(
        scaled * rows_in, axis=-1, keepdims=True
    )
    return (grad_rows, grad_gain)


def local(
    tokens,
    cotangent,
    routes,
    lengths,
    attn_gain,
    w_query,
    w_key,
    w_value,
    w_out,
    moe_gain,
    w_router,
    w_gate,
    w_up,
    w_down,
):
    here = Place()
    core, shards, quarters = here.core, here.shards, here.quarters
    experts = w_gate.shape[0]
    features = tokens.shape[3]
    hidden_all = w_gate.shape[2]
    width_q = w_query.shape[1] // 2
    width_k = w_key.shape[1] // 2
    shard_rows = w_query.shape[0]
    rows_q = shard_rows // quarters
    hidden_part = hidden_all // shards // 2
    hidden_core = hidden_all // 2
    down_rows = hidden_part // quarters
    bit_list = [1 << n for n in range(quarters.bit_length() - 1)]
    bit_back = bit_list[::-1]

    x_own = here.to_streams(tokens[:, 0])
    rows = x_own.shape[0]

    def columns_of(weight, width):
        return lax.dynamic_slice_in_dim(weight, core * width, width, 1)

    def split(weight):
        return weight.reshape(1, quarters, rows_q, weight.shape[1])

    small = jnp.concatenate(
        [attn_gain[:, None], moe_gain[:, None], w_router], axis=1
    )
    small = jnp.pad(small, ((0, 0), (0, 128 - small.shape[1])))
    own_q = split(columns_of(w_query, width_q))
    own_kv = split(
        jnp.concatenate([columns_of(w_key, width_k), columns_of(w_value, width_k), small], axis=1)
    )
    own_out = split(columns_of(w_out, features // 2))

    def expert_columns(weight):
        parts = weight.reshape(experts, shard_rows, shards, 2, hidden_part)
        parts = lax.dynamic_index_in_dim(parts, core, 3, keepdims=False)
        return split(jnp.transpose(parts, (1, 0, 2, 3)).reshape(shard_rows, experts * hidden_core))

    own_gate = expert_columns(w_gate)
    own_up = expert_columns(w_up)
    own_down = lax.dynamic_slice_in_dim(w_down, core * hidden_part, hidden_part, 1).reshape(
        experts, quarters, down_rows, features
    )

    kv_w = here.assemble(own_kv, here.fetch(own_kv, bit_back)).reshape(features, -1)
    q_w = here.assemble(own_q, here.fetch(own_q, bit_list)).reshape(features, width_q)
    found_out = here.fetch(own_out, bit_back)
    out_w = here.assemble(
        own_out, found_out, (here.swap(own_out), [here.swap(part) for part in found_out])
    ).reshape(features, features)
    gate_w = here.assemble(own_gate, here.fetch(own_gate, bit_list)).reshape(features, -1)
    up_w = here.assemble(own_up, here.fetch(own_up, bit_back)).reshape(features, -1)
    down_w = here.assemble(own_down, here.fetch(own_down, bit_list)).reshape(-1, features)

    smalls = kv_w[:, 2 * width_k : 2 * width_k + 2 + experts].astype(F32)
    gain_one = smalls[:, 0][None, :]
    gain_two = smalls[:, 1][None, :]
    router_w = kv_w[:, 2 * width_k + 2 : 2 * width_k + 2 + experts]
    kv_w = kv_w[:, : 2 * width_k]

    x_wide = x_own.astype(F32)
    scale_one = rms_scale(x_wide)
    normed_own = (x_wide * scale_one * gain_one).astype(BF16)
    normed = here.ordered(normed_own, here.swap(normed_own), 0)
    q_t = dot(q_w, normed, 0, 1, BF16)
    kv_t = dot(kv_w, normed, 0, 1, BF16)
    k_t, v_t = kv_t[:width_k], kv_t[width_k:]
    q_t, k_t, v_t = (here.chip_exchange(part, 0, 1) for part in (q_t, k_t, v_t))
    length = q_t.shape[1]

    my_lengths = lax.dynamic_index_in_dim(
        lax.dynamic_index_in_dim(lengths, here.batch, 0, keepdims=False),
        here.source,
        0,
        keepdims=False,
    )
    ends = jnp.cumsum(my_lengths)[:-1]
    positions = jnp.arange(length, dtype=jnp.int32)
    starts = jnp.max(
        jnp.where(ends[:, None] <= positions[None, :], ends[:, None], 0), axis=0, keepdims=True
    ).astype(jnp.int32)
    o_t, stat = attend_forward(q_t, k_t, v_t, starts)
    o_back = here.chip_exchange(o_t, 1, 0)
    o_mine, o_other = here.halves(o_back, 1)
    o_own = here.ordered(o_mine, here.swap(o_other), 0)
    h_own = x_wide + dot(o_own, out_w, 0, 0)

    scale_two = rms_scale(h_own)
    b_own = (h_own * scale_two * gain_two).astype(BF16)
    b_all = jnp.concatenate([b_own, here.swap(b_own)], axis=0)
    route_own = here.to_streams(routes[:, 0])
    route_all = jnp.concatenate([route_own, here.swap(route_own)], axis=0)
    dy_own = here.to_streams(cotangent[:, 0])
    dy_all = jnp.concatenate([dy_own, here.swap(dy_own)], axis=0)

    logits = dot(b_all, router_w, 1, 0)
    route_hot = (
        route_all[:, :, None] == jnp.arange(experts, dtype=jnp.int32)[None, None, :]
    ).astype(F32)
    chosen = jnp.sum(logits[:, None, :] * route_hot, axis=2)
    gate_share = jax.nn.softmax(chosen, axis=1)
    shares = jnp.sum(gate_share[:, :, None] * route_hot, axis=1)
    share_wide = jnp.repeat(shares, hidden_core, axis=1)

    gate_v = dot(b_all, gate_w, 1, 0, BF16)
    up_v = dot(b_all, up_w, 1, 0, BF16)
    gate_f, up_f = gate_v.astype(F32), up_v.astype(F32)
    squashed = jax.nn.sigmoid(gate_f)
    mid = (gate_f * squashed * up_f * share_wide).astype(BF16)
    y_other = dot(mid[rows:], down_w, 1, 0, BF16)
    y_got = here.swap(y_other)
    y_own = dot(mid[:rows], down_w, 1, 0)
    block_own = (h_own + y_own + y_got.astype(F32)).astype(BF16)
    block_out = here.to_homes(block_own)

    slope = dot(dy_all, down_w, 1, 1)
    grad_down = dot(mid, dy_all, 0, 0, BF16)
    active = gate_f * squashed
    grad_share = jnp.sum((slope * active * up_f).reshape(2 * rows, experts, hidden_core), axis=2)
    scaled = slope * share_wide
    grad_gate_v = (scaled * up_f * squashed * (1.0 + gate_f * (1.0 - squashed))).astype(BF16)
    grad_up_v = (scaled * active).astype(BF16)
    share_got = here.swap(grad_share[rows:])
    grad_share = grad_share[:rows] + share_got
    db_other = (
        dot(grad_gate_v[rows:], gate_w, 1, 1) + dot(grad_up_v[rows:], up_w, 1, 1)
    ).astype(BF16)
    db_got = here.swap(db_other)
    db_own = dot(grad_gate_v[:rows], gate_w, 1, 1) + dot(grad_up_v[:rows], up_w, 1, 1)
    grad_gate = dot(b_all, grad_gate_v, 0, 0, BF16)
    grad_up = dot(b_all, grad_up_v, 0, 0, BF16)

    hot_own, share_own = route_hot[:rows], gate_share[:rows]
    grad_gates = jnp.sum(grad_share[:, None, :] * hot_own, axis=2)
    grad_chosen = share_own * (
        grad_gates - jnp.sum(share_own * grad_gates, axis=1, keepdims=True)
    )
    grad_logits = jnp.sum(grad_chosen[:, :, None] * hot_own, axis=1).astype(BF16)
    grad_router = dot(b_own, grad_logits, 0, 0)
    db = db_own + db_got.astype(F32) + dot(grad_logits, router_w, 1, 1)
    dh, grad_gain_two = norm_back(h_own, scale_two, gain_two, db)
    dh = dh + dy_own.astype(F32)
    dattn = dh.astype(BF16)

    do_t = dot(out_w, dattn, 1, 1, BF16)
    do_mine, do_other = here.halves(do_t, 0)
    do_t = here.ordered(do_mine, here.swap(do_other), 1)
    do_t = here.chip_exchange(do_t, 0, 1)
    grad_out = dot(o_own, dattn, 1, 0, BF16)
    out_mine, out_other = here.halves(grad_out, 1)
    grad_out = (out_mine.astype(F32) + here.swap(out_other).astype(F32)).astype(BF16)
    dq_t, dk_t, dv_t = attend_backward(q_t, k_t, v_t, o_t, do_t, stat, starts)
    dq_t, dk_t, dv_t = (here.chip_exchange(part, 1, 0) for part in (dq_t, dk_t, dv_t))
    back_t = jnp.concatenate([dq_t, dk_t, dv_t], axis=0)
    back_w = jnp.concatenate([q_w, kv_w], axis=1)
    back_w_got = here.swap(back_w)
    back_mine, back_other = here.halves(back_t, 1)
    back_got = here.swap(back_other)
    da = dot(back_mine, back_w, 0, 1) + dot(back_got, back_w_got, 0, 1)
    grad_qkv = dot(normed, back_t, 0, 1, BF16)
    dx, grad_gain_one = norm_back(x_wide, scale_one, gain_one, da)
    input_grad = here.to_homes((dx + dh).astype(BF16))

    def as_grad(grad, parts, part_rows):
        return grad.reshape(parts, shards, quarters, part_rows, grad.shape[-1])

    grad_small = jnp.concatenate(
        [grad_gain_one[:, None], grad_gain_two[:, None], grad_router], axis=1
    )
    grad_small = jnp.pad(grad_small, ((0, 0), (0, 128 - grad_small.shape[1]))).astype(BF16)
    sum_down = here.reduce(as_grad(grad_down, experts, down_rows), bit_list)
    sum_gate = here.reduce(as_grad(grad_gate, 1, rows_q), bit_back)
    sum_up = here.reduce(as_grad(grad_up, 1, rows_q), bit_list)
    sum_out = here.reduce(as_grad(grad_out, 1, rows_q), bit_back)
    sum_qkv = here.reduce(
        as_grad(jnp.concatenate([grad_qkv, grad_small], axis=1), 1, rows_q), bit_list
    )

    def both_cores(summed, first, width):
        piece = summed[:, :, 0, :, first : first + width].astype(F32)
        return jnp.transpose(piece, (0, 2, 1, 3)).reshape(shard_rows, 2 * width)

    out_query = both_cores(sum_qkv, 0, width_q)
    out_key = both_cores(sum_qkv, width_q, width_k)
    out_value = both_cores(sum_qkv, width_q + width_k, width_k)
    small_sum = sum_qkv[:, :, 0, :, width_q + 2 * width_k :].astype(F32).sum(axis=1)
    small_sum = small_sum.reshape(shard_rows, -1)
    out_out = both_cores(sum_out, 0, features // 2)

    def expert_grad(summed):
        piece = summed[:, :, 0].astype(F32)
        piece = piece.reshape(quarters, 2, rows_q, experts, shards, hidden_part)
        return jnp.transpose(piece, (3, 0, 2, 4, 1, 5)).reshape(experts, shard_rows, hidden_all)

    out_down = jnp.transpose(sum_down.astype(F32), (2, 1, 0, 3, 4)).reshape(
        experts, 2 * hidden_part, features
    )
    return (
        block_out[:, None],
        input_grad[:, None],
        small_sum[:, 0],
        out_query,
        out_key,
        out_value,
        out_out,
        small_sum[:, 1],
        small_sum[:, 2 : 2 + experts],
        expert_grad(sum_gate),
        expert_grad(sum_up),
        out_down,
    )


def solution(mesh):
    in_specs = (
        P(None, "rep", "shard", None),
        P(None, "rep", "shard", None),
        P(None, "rep", "shard", None),
        P(),
        P("shard"),
        P("shard", None),
        P("shard", None),
        P("shard", None),
        P("shard", None),
        P("shard"),
        P("shard", None),
        P(None, "shard", None),
        P(None, "shard", None),
        P(None, "shard", None),
    )
    out_specs = (
        P(None, "rep", "shard", None),
        P(None, "rep", "shard", None),
        P("shard"),
        P("shard", None),
        P("shard", None),
        P("shard", None),
        P("shard", None),
        P("shard"),
        P("shard", None),
        P(None, "shard", None),
        P(None, "shard", None),
        P(None, "shard", None),
    )
    return jax.shard_map(local, mesh=mesh, in_specs=in_specs, out_specs=out_specs, check_vma=False)
```

```python
import functools
import math

import jax
import jax.numpy as jnp
from jax import lax
from jax.experimental import pallas as pl
from jax.experimental.pallas import tpu as pltpu
from jax.sharding import PartitionSpec as P

HEAD = 64
EPSILON = 1e-05
NEGATIVE = -1e30
F32 = jnp.float32
BF16 = jnp.bfloat16
LOG2_SCALE = HEAD ** (-0.5) * math.log2(math.e)
SCALE = HEAD ** (-0.5)
PLANE = ("chip", "core")
BOTH = ("chip", "core", "shard")


def together(*arrays):
    return lax.optimization_barrier(arrays)


def dot(left, right, left_dim, right_dim, kind=F32):
    return lax.dot_general(
        left, right, (((left_dim,), (right_dim,)), ((), ())), preferred_element_type=F32
    ).astype(kind)


def forward_blocks(length):
    return min(512, length), min(512, length)


def backward_blocks(length):
    return min(512, length), min(256, length)


def visible_mask(index, width, first_key, first_query, starts):
    rows = first_key + lax.broadcasted_iota(jnp.int32, (width, starts.shape[1]), 0)
    columns = first_query + lax.broadcasted_iota(jnp.int32, (1, starts.shape[1]), 1)
    return (rows >= starts) & (rows <= columns)


def side_by_side(block, group):
    return jnp.concatenate([block[g * HEAD : (g + 1) * HEAD, :] for g in range(group)], axis=1)


def three_loops(ranges, place, step, carry):
    low, full_low, full_high, high = (ranges[place, n] for n in range(4))
    carry = lax.fori_loop(low, full_low, functools.partial(step, True), carry)
    carry = lax.fori_loop(full_low, full_high, functools.partial(step, False), carry)
    return lax.fori_loop(full_high, high, functools.partial(step, True), carry)


def forward_kernel(ranges, q_ref, k_ref, v_ref, starts_ref, o_ref, stat_ref, k_rows, *, group, wide):
    place = pl.program_id(1)
    q_width = q_ref.shape[1]

    @pl.when(place == 0)
    def _():
        k_rows[...] = k_ref[...].T

    queries = side_by_side(q_ref[...], group)
    starts = starts_ref[...]

    def step(masked, index, carry):
        high, total, mixed = carry
        first = pl.multiple_of(index * wide, wide)
        scores = (
            jnp.dot(k_rows[pl.ds(first, wide), :], queries, preferred_element_type=F32)
            * LOG2_SCALE
        )
        if masked:
            seen = visible_mask(index, wide, first, place * q_width, starts)
            scores = jnp.where(jnp.concatenate([seen] * group, axis=1), scores, NEGATIVE)
        new_high = jnp.maximum(high, jnp.max(scores, axis=0, keepdims=True))
        weights = jnp.exp2(scores - new_high)
        fade = jnp.exp2(high - new_high)
        total = total * fade + jnp.sum(weights, axis=0, keepdims=True)
        mixed = mixed * fade + jnp.dot(
            v_ref[:, pl.ds(first, wide)], weights.astype(BF16), preferred_element_type=F32
        )
        return new_high, total, mixed

    columns = group * q_width
    high, total, mixed = three_loops(
        ranges,
        place,
        step,
        (
            jnp.full((1, columns), NEGATIVE, F32),
            jnp.zeros((1, columns), F32),
            jnp.zeros((HEAD, columns), F32),
        ),
    )
    mixed = (mixed / total).astype(BF16)
    stat = high + jnp.log2(total)
    for g in range(group):
        span = slice(g * q_width, (g + 1) * q_width)
        o_ref[g * HEAD : (g + 1) * HEAD, :] = mixed[:, span]
        stat_ref[0, g : g + 1, :] = stat[:, span]


def backward_kernel(
    ranges, q_ref, k_ref, v_ref, o_ref, g_ref, stat_ref, starts_ref,
    dq_ref, dk_ref, dv_ref, k_rows, v_rows, dk_sum, dv_sum, *, group, wide,
):
    place = pl.program_id(1)
    q_width = q_ref.shape[1]

    @pl.when(place == 0)
    def _():
        k_rows[...] = k_ref[...].T
        v_rows[...] = v_ref[...].T
        dk_sum[...] = jnp.zeros_like(dk_sum)
        dv_sum[...] = jnp.zeros_like(dv_sum)

    queries = side_by_side(q_ref[...], group)
    grads = side_by_side(g_ref[...], group)
    outs = side_by_side(o_ref[...], group)
    inner = jnp.sum(grads.astype(F32) * outs.astype(F32), axis=0, keepdims=True)
    stat = jnp.concatenate([stat_ref[0, g : g + 1, :] for g in range(group)], axis=1)
    starts = starts_ref[...]

    def step(masked, index, dq):
        first = pl.multiple_of(index * wide, wide)
        span = pl.ds(first, wide)
        scores = jnp.dot(k_rows[span, :], queries, preferred_element_type=F32) * LOG2_SCALE
        chances = jnp.exp2(scores - stat)
        if masked:
            seen = visible_mask(index, wide, first, place * q_width, starts)
            chances = jnp.where(jnp.concatenate([seen] * group, axis=1), chances, 0.0)
        slopes = jnp.dot(v_rows[span, :], grads, preferred_element_type=F32)
        pull = (chances * (slopes - inner)).astype(BF16)
        dv_sum[:, span] += dot(grads, chances.astype(BF16), 1, 1)
        dk_sum[:, span] += dot(queries, pull, 1, 1)
        return dq + jnp.dot(k_ref[:, span], pull, preferred_element_type=F32)

    dq = three_loops(ranges, place, step, jnp.zeros((HEAD, group * q_width), F32))
    dq = (dq * SCALE).astype(BF16)
    for g in range(group):
        dq_ref[g * HEAD : (g + 1) * HEAD, :] = dq[:, g * q_width : (g + 1) * q_width]

    @pl.when(place == pl.num_programs(1) - 1)
    def _():
        dk_ref[...] = (dk_sum[...] * SCALE).astype(BF16)
        dv_ref[...] = dv_sum[...].astype(BF16)


def block_ranges(starts, q_width, wide):
    length = starts.shape[1]
    count = length // q_width
    first_query = jnp.arange(count, dtype=jnp.int32) * q_width
    low = starts[0, ::q_width] // wide
    full_low = (starts[0, q_width - 1 :: q_width] + wide - 1) // wide
    full_high = (first_query + 1) // wide
    full_high = first_query // wide
    high = (first_query + q_width) // wide
    full_low = jnp.clip(full_low, low, jnp.maximum(full_high, low))
    full_high = jnp.maximum(full_high, full_low)
    return jnp.stack([low, full_low, full_high, high], axis=1)


def attention_specs(head, group, length, q_width):
    per_query = pl.BlockSpec((group * HEAD, q_width), lambda h, i, r: (head, i))
    per_head = pl.BlockSpec((HEAD, length), lambda h, i, r: (head, 0))
    out_query = pl.BlockSpec((group * HEAD, q_width), lambda h, i, r: (0, i))
    out_head = pl.BlockSpec((HEAD, length), lambda h, i, r: (0, 0))
    stat = pl.BlockSpec((1, group, q_width), lambda h, i, r: (0, 0, i))
    starts = pl.BlockSpec((1, q_width), lambda h, i, r: (0, i))
    return per_query, per_head, out_query, out_head, stat, starts


def attend_forward(head, q_t, k_t, v_t, starts):
    length = q_t.shape[1]
    group = q_t.shape[0] // k_t.shape[0]
    q_width, wide = forward_blocks(length)
    per_query, per_head, out_query, _, stat, start_spec = attention_specs(
        head, group, length, q_width
    )
    pairs = group * length * length // 2
    return pl.pallas_call(
        functools.partial(forward_kernel, group=group, wide=wide),
        out_shape=(
            jax.ShapeDtypeStruct((group * HEAD, length), BF16),
            jax.ShapeDtypeStruct((1, group, length), F32),
        ),
        grid_spec=pltpu.PrefetchScalarGridSpec(
            num_scalar_prefetch=1,
            grid=(1, length // q_width),
            in_specs=[per_query, per_head, per_head, start_spec],
            out_specs=(out_query, stat),
            scratch_shapes=[pltpu.VMEM((length, HEAD), BF16)],
        ),
        compiler_params=pltpu.CompilerParams(
            dimension_semantics=("arbitrary", "arbitrary"), vmem_limit_bytes=40 << 20
        ),
        cost_estimate=pl.CostEstimate(
            flops=pairs * HEAD * 4, transcendentals=0, bytes_accessed=group * length * 512
        ),
        name="attend_forward",
    )(block_ranges(starts, q_width, wide), q_t, k_t, v_t, starts)


def attend_backward(head, q_t, k_t, v_t, o_h, g_h, stat_h, starts):
    length = q_t.shape[1]
    group = q_t.shape[0] // k_t.shape[0]
    q_width, wide = backward_blocks(length)
    per_query, per_head, out_query, out_head, stat, start_spec = attention_specs(
        head, group, length, q_width
    )
    pairs = group * length * length // 2
    return pl.pallas_call(
        functools.partial(backward_kernel, group=group, wide=wide),
        out_shape=(
            jax.ShapeDtypeStruct((group * HEAD, length), BF16),
            jax.ShapeDtypeStruct((HEAD, length), BF16),
            jax.ShapeDtypeStruct((HEAD, length), BF16),
        ),
        grid_spec=pltpu.PrefetchScalarGridSpec(
            num_scalar_prefetch=1,
            grid=(1, length // q_width),
            in_specs=[per_query, per_head, per_head, out_query, out_query, stat, start_spec],
            out_specs=(out_query, out_head, out_head),
            scratch_shapes=[
                pltpu.VMEM((length, HEAD), BF16),
                pltpu.VMEM((length, HEAD), BF16),
                pltpu.VMEM((HEAD, length), F32),
                pltpu.VMEM((HEAD, length), F32),
            ],
        ),
        compiler_params=pltpu.CompilerParams(
            dimension_semantics=("arbitrary", "arbitrary"), vmem_limit_bytes=40 << 20
        ),
        cost_estimate=pl.CostEstimate(
            flops=pairs * HEAD * 10, transcendentals=0, bytes_accessed=group * length * 1024
        ),
        name="attend_backward",
    )(block_ranges(starts, q_width, wide), q_t, k_t, v_t, o_h, g_h, stat_h, starts)


class Place:
    def __init__(self):
        self.quarters = lax.axis_size("chip")
        self.reps = 2 * self.quarters
        self.shards = lax.axis_size("shard")
        self.chips = self.shards // 4
        self.core = lax.axis_index("core")
        self.quarter = lax.axis_index("chip")
        self.shard = lax.axis_index("shard")
        self.stream = self.shard // self.chips
        self.batch = self.stream // 2
        self.source = self.quarter * 2 + self.stream % 2
        self.chip = self.shard % self.chips

    def across(self, array, key):
        return lax.ppermute(array, "chip", [(i, i ^ key) for i in range(self.quarters)])

    def swap(self, array):
        return lax.ppermute(array, "core", [(0, 1), (1, 0)])

    def moves(self, turn, home):
        pairs = []
        for quarter in range(self.quarters):
            for core in range(2):
                for shard in range(self.shards):
                    batch = turn ^ (shard & 1)
                    member = shard // 2
                    stream = 2 * batch + core
                    start = (quarter * 2 + core) * self.shards + shard
                    end = (
                        (quarter * 2 + member % 2) * self.shards
                        + stream * self.chips
                        + member // 2
                    )
                    if start != end:
                        pairs.append((end, start) if home else (start, end))
        return pairs

    def stays(self, turn):
        batch = turn ^ (self.shard & 1)
        member = self.shard // 2
        end = (2 * batch + self.core) * self.chips + member // 2
        return (member % 2 == self.core) & (end == self.shard)

    def leaving(self, array):
        odd = self.shard % 2 == 1
        return [jnp.where(odd, array[1 - turn], array[turn]) for turn in range(2)]

    def send_streams(self, array):
        return [
            lax.ppermute(part, BOTH, self.moves(turn, False))
            for turn, part in enumerate(self.leaving(array))
        ]

    def join_streams(self, array, got):
        got = [
            jnp.where(self.stays(turn), part, got[turn])
            for turn, part in enumerate(self.leaving(array))
        ]
        swapped = self.batch == 1
        return jnp.concatenate(
            [jnp.where(swapped, got[1], got[0]), jnp.where(swapped, got[0], got[1])], axis=0
        )

    def to_streams(self, array):
        return self.join_streams(array, self.send_streams(array))

    def to_homes(self, array):
        half = array.shape[0] // 2
        swapped = self.batch == 1
        parts = [array[:half], array[half:]]
        got = [
            jnp.where(swapped, parts[1 - turn], parts[turn]) for turn in range(2)
        ]
        got = [
            jnp.where(
                self.stays(turn), part, lax.ppermute(part, BOTH, self.moves(turn, True))
            )
            for turn, part in enumerate(got)
        ]
        odd = self.shard % 2 == 1
        return jnp.stack([jnp.where(odd, got[1], got[0]), jnp.where(odd, got[0], got[1])])

    def ordered(self, mine, other, axis):
        return jnp.where(
            self.core == 0,
            jnp.concatenate([mine, other], axis=axis),
            jnp.concatenate([other, mine], axis=axis),
        )

    def halves(self, array, axis):
        size = array.shape[axis] // 2
        mine = lax.dynamic_slice_in_dim(array, self.core * size, size, axis)
        other = lax.dynamic_slice_in_dim(array, (1 - self.core) * size, size, axis)
        return mine, other

    def head_order(self, pieces, heads):
        if self.chips == 1:
            return jnp.concatenate(pieces, axis=0)
        stacked = jnp.stack([p.reshape(self.chips, -1, p.shape[1]) for p in pieces], axis=1)
        return stacked.reshape(-1, pieces[0].shape[1])

    def chip_exchange(self, array, split, join):
        if self.chips == 1:
            return array
        size = array.shape[split] // self.chips
        width = array.shape[join]
        shape = list(array.shape)
        shape[split] = size
        shape[join] = width * self.chips
        result = jnp.zeros(shape, array.dtype)
        for step in range(self.chips):
            other = self.chip ^ step
            piece = lax.dynamic_slice_in_dim(array, other * size, size, split)
            if step:
                piece = lax.ppermute(
                    piece, "shard", [(i, i ^ step) for i in range(self.shards)]
                )
            result = lax.dynamic_update_slice_in_dim(result, piece, other * width, join)
        return result

    def along(self, array, step):
        return lax.ppermute(
            array, "shard", [(i, (i + step) % self.shards) for i in range(self.shards)]
        )

    def fetch_along(self, own):
        piece = lax.dynamic_index_in_dim(own, self.quarter, 1, keepdims=False)
        return [self.along(piece, step) for step in range(1, self.shards)]

    def fetch_across(self, got):
        got = jnp.stack(got)
        return [got] + [self.across(got, key) for key in range(1, self.quarters)]

    def assemble(self, own, found, widths):
        parts, quarters, rows, _ = own.shape
        shards = self.shards
        places = jnp.stack([self.shard, self.quarter]).astype(jnp.int32)
        edges = [sum(widths[:n]) for n in range(len(widths) + 1)]

        def kernel(places_ref, own_ref, *refs):
            found_refs, out_refs, sem = refs[:quarters], refs[quarters:-1], refs[-1]
            shard, quarter = places_ref[0], places_ref[1]
            copies = []
            for n, out_ref in enumerate(out_refs):
                span = pl.ds(edges[n], widths[n])
                for part in range(parts):
                    copies.append((own_ref.at[part, :, :, span], out_ref.at[part, shard]))
                    for key in range(quarters):
                        for step in range(1, shards):
                            where = (shard - step + shards) % shards
                            copies.append(
                                (
                                    found_refs[key].at[step - 1, part, :, span],
                                    out_ref.at[part, where, quarter ^ key],
                                )
                            )
            copies = [
                pltpu.make_async_copy(source, end, sem.at[n])
                for n, (source, end) in enumerate(copies)
            ]
            for copy in copies:
                copy.start()
            for copy in copies:
                copy.wait()

        whole = pl.pallas_call(
            kernel,
            out_shape=tuple(
                jax.ShapeDtypeStruct((parts, shards, quarters, rows, width), own.dtype)
                for width in widths
            ),
            in_specs=[pl.BlockSpec(memory_space=pltpu.SMEM)]
            + [pl.BlockSpec(memory_space=pl.ANY)] * (quarters + 1),
            out_specs=tuple(pl.BlockSpec(memory_space=pltpu.VMEM) for _ in widths),
            scratch_shapes=[
                pltpu.SemaphoreType.DMA((len(widths) * parts * (1 + quarters * (shards - 1)),))
            ],
            compiler_params=pltpu.CompilerParams(vmem_limit_bytes=24 << 20),
            cost_estimate=pl.CostEstimate(
                flops=0, transcendentals=0, bytes_accessed=own.size * shards * 4
            ),
            name="assemble",
        )(places, own, *found)
        return [part.reshape(parts * shards * quarters * rows, -1) for part in whole]

    def gather_experts(self, w_gate, w_up):
        which = self.quarter * 2 + self.core

        def part(weight):
            size = weight.shape[1] // self.reps
            piece = lax.dynamic_slice_in_dim(weight, which * size, size, 1)
            return piece.reshape(-1, weight.shape[2])

        piece = jnp.concatenate([part(w_gate), part(w_up)], axis=0)
        return lax.all_gather(piece, ("shard", "chip", "core"), axis=0, tiled=False)

    def reduce_across(self, grad):
        got = lax.all_to_all(grad, "chip", 0, 0, tiled=True)
        return jnp.sum(got.astype(F32), axis=0).astype(BF16)

    def by_shard(self, held):
        return jnp.transpose(held.reshape(held.shape[0], self.shards, -1), (1, 0, 2))

    def reduce_along(self, held):
        total = lax.dynamic_index_in_dim(held, self.shard, 0, keepdims=False).astype(F32)
        for step in range(1, self.shards):
            give = lax.dynamic_index_in_dim(
                held, (self.shard + step) % self.shards, 0, keepdims=False
            )
            total = total + self.along(give, step).astype(F32)
        return total.astype(BF16)

    def scatter(self, held):
        return lax.psum_scatter(held, "shard", scatter_dimension=0, tiled=False)

    def gather(self, total):
        whole = lax.all_gather(total, PLANE, axis=0, tiled=False)
        return whole.reshape(self.quarters, 2, *total.shape)


def core_columns(packed, which, core, shards, experts):
    pieces, _, hidden = packed.shape
    rows = packed.shape[1] // 2
    part = hidden // shards // 2
    small = rows // experts
    if part % 128 or small % 16:
        parts = packed[:, which * rows : (which + 1) * rows]
        parts = parts.reshape(pieces, experts, small, shards, 2, part)
        parts = lax.dynamic_index_in_dim(parts, core, 4, keepdims=False)
        return jnp.transpose(parts, (0, 2, 1, 3, 4)).reshape(pieces * small, -1)
    group = 4

    def kernel(core_ref, *refs):
        out_ref = refs[-1]
        for shard in range(shards):
            for piece in range(group):
                for expert in range(experts):
                    column = (expert * shards + shard) * part
                    out_ref[piece * small : (piece + 1) * small, column : column + part] = refs[
                        shard
                    ][piece, expert * small : (expert + 1) * small, :]

    def columns(shard):
        return pl.BlockSpec((group, rows, part), lambda i, c: (i, which, 2 * shard + c[0]))

    return pl.pallas_call(
        kernel,
        out_shape=jax.ShapeDtypeStruct((pieces * small, experts * hidden // 2), packed.dtype),
        grid_spec=pltpu.PrefetchScalarGridSpec(
            num_scalar_prefetch=1,
            grid=(pieces // group,),
            in_specs=[columns(shard) for shard in range(shards)],
            out_specs=pl.BlockSpec(
                (group * small, experts * hidden // 2), lambda i, c: (i, 0)
            ),
        ),
        cost_estimate=pl.CostEstimate(
            flops=0, transcendentals=0, bytes_accessed=packed.size
        ),
        name="core_columns",
    )(core.astype(jnp.int32)[None], *([packed] * shards))


def spread_experts(summed, which, experts, shards):
    quarters, _, _, columns, rows = summed.shape
    hidden = 2 * columns * quarters // experts
    part = hidden // shards // 2
    if part % 128 or quarters != experts:
        piece = jnp.transpose(summed[:, :, which].astype(F32), (1, 0, 2, 3))
        piece = piece.reshape(2, experts, shards, part, rows)
        return jnp.transpose(piece, (1, 4, 2, 0, 3)).reshape(experts, rows, hidden)

    def kernel(in_ref, out_ref):
        for core in range(2):
            turned = in_ref[0, core, 0].astype(F32).T
            for shard in range(shards):
                first = (2 * shard + core) * part
                out_ref[0, :, first : first + part] = turned[:, shard * part : (shard + 1) * part]

    return pl.pallas_call(
        kernel,
        out_shape=jax.ShapeDtypeStruct((experts, rows, hidden), F32),
        grid=(experts,),
        in_specs=[pl.BlockSpec((1, 2, 1, columns, rows), lambda e: (e, 0, which, 0, 0))],
        out_specs=pl.BlockSpec((1, rows, hidden), lambda e: (e, 0, 0)),
        cost_estimate=pl.CostEstimate(
            flops=0, transcendentals=0, bytes_accessed=summed.size * 3
        ),
        name="spread_experts",
    )(summed)


def spread_rows(mine, other, quarter, core, widths):
    quarters, columns, rows = mine.shape
    rest = quarters * columns - sum(widths)
    places = jnp.stack([quarter, core]).astype(jnp.int32)

    def kernel(places_ref, mine_ref, other_ref, *out_refs):
        quarter, core = places_ref[0], places_ref[1]
        for side, ref in enumerate((mine_ref, other_ref)):
            at = core if side == 0 else 1 - core
            whole = jnp.concatenate(
                [ref[n ^ quarter].astype(F32) for n in range(quarters)], axis=0
            )
            first = 0
            for width, out_ref in zip(widths, out_refs):
                span = pl.ds(pl.multiple_of(at * width, 128), width)
                out_ref[:, span] = whole[first : first + width].T
                first += width
            if rest and side == 0:
                out_refs[-1][...] = whole[first:]
            elif rest:
                out_refs[-1][...] += whole[first:]

    shapes = [jax.ShapeDtypeStruct((rows, 2 * width), F32) for width in widths]
    if rest:
        shapes.append(jax.ShapeDtypeStruct((rest, rows), F32))
    return pl.pallas_call(
        kernel,
        out_shape=tuple(shapes),
        in_specs=[
            pl.BlockSpec(memory_space=pltpu.SMEM),
            pl.BlockSpec(memory_space=pltpu.VMEM),
            pl.BlockSpec(memory_space=pltpu.VMEM),
        ],
        out_specs=tuple(pl.BlockSpec(memory_space=pltpu.VMEM) for _ in shapes),
        compiler_params=pltpu.CompilerParams(vmem_limit_bytes=40 << 20),
        cost_estimate=pl.CostEstimate(
            flops=0, transcendentals=0, bytes_accessed=mine.size * 12
        ),
        name="spread_rows",
    )(places, mine, other)


def rms_scale(rows_in):
    return lax.rsqrt(jnp.mean(rows_in * rows_in, axis=-1, keepdims=True) + EPSILON)


def norm_back(rows_in, row_scale, gain_row, grad_normed):
    grad_gain = jnp.sum(grad_normed * rows_in * row_scale, axis=0)
    scaled = grad_normed * gain_row
    scale_cubed = row_scale * row_scale * row_scale
    grad_rows = row_scale * scaled - rows_in * scale_cubed * jnp.mean(
        scaled * rows_in, axis=-1, keepdims=True
    )
    return (grad_rows, grad_gain)


def local(
    tokens,
    cotangent,
    routes,
    lengths,
    attn_gain,
    w_query,
    w_key,
    w_value,
    w_out,
    moe_gain,
    w_router,
    w_gate,
    w_up,
    w_down,
):
    here = Place()
    core, shards, quarters = here.core, here.shards, here.quarters
    experts = w_gate.shape[0]
    features = tokens.shape[3]
    hidden_all = w_gate.shape[2]
    width_q = w_query.shape[1] // 2
    width_k = w_key.shape[1] // 2
    shard_rows = w_query.shape[0]
    rows_q = shard_rows // quarters
    hidden_part = hidden_all // shards // 2
    hidden_core = hidden_all // 2

    def columns_of(weight, width):
        return lax.dynamic_slice_in_dim(weight, core * width, width, 1)

    small = jnp.concatenate([attn_gain[:, None], moe_gain[:, None], w_router], axis=1)
    small = jnp.pad(small, ((0, 0), (0, 128 - small.shape[1])))
    own = jnp.concatenate(
        [
            columns_of(w_query, width_q),
            columns_of(w_key, width_k),
            columns_of(w_value, width_k),
            small,
            columns_of(w_out, features // 2),
        ],
        axis=1,
    ).reshape(1, quarters, rows_q, -1)
    got = here.fetch_along(own)

    tokens, own = together(tokens, own)
    x_own = here.to_streams(tokens[:, 0])
    rows = x_own.shape[0]
    w_gate, *got = together(w_gate, *got)
    packed = here.gather_experts(w_gate, w_up)
    own_down = lax.dynamic_slice_in_dim(w_down, core * hidden_part, hidden_part, 1).reshape(
        experts, quarters, hidden_part // quarters, features
    )
    found = here.fetch_across(got)
    routes, x_own = together(routes, x_own)
    route_own = here.to_streams(routes[:, 0])
    own_down, route_own = together(own_down, route_own)
    got_down = here.fetch_along(own_down)
    qkv_w, small_w, out_w = here.assemble(
        own, found, [width_q + 2 * width_k, 128, features // 2]
    )
    out_w = here.ordered(out_w, here.swap(out_w), 1)
    smalls = small_w[:, : 2 + experts].astype(F32)
    gain_one = smalls[:, 0][None, :]
    gain_two = smalls[:, 1][None, :]
    router_w = small_w[:, 2 : 2 + experts]

    x_wide = x_own.astype(F32)
    scale_one = rms_scale(x_wide)
    normed_own = (x_wide * scale_one * gain_one).astype(BF16)
    normed = here.ordered(normed_own, here.swap(normed_own), 0)
    route_all = jnp.concatenate([route_own, here.swap(route_own)], axis=0)
    qkv_t = dot(qkv_w, normed, 0, 1, BF16)
    q_t, k_t, v_t = qkv_t[:width_q], qkv_t[width_q : width_q + width_k], qkv_t[width_q + width_k :]
    q_t, k_t, v_t = (here.chip_exchange(part, 0, 1) for part in (q_t, k_t, v_t))
    length = q_t.shape[1]

    my_lengths = lax.dynamic_index_in_dim(
        lax.dynamic_index_in_dim(lengths, here.batch, 0, keepdims=False),
        here.source,
        0,
        keepdims=False,
    )
    ends = jnp.cumsum(my_lengths)[:-1]
    positions = jnp.arange(length, dtype=jnp.int32)
    starts = jnp.max(
        jnp.where(ends[:, None] <= positions[None, :], ends[:, None], 0), axis=0, keepdims=True
    ).astype(jnp.int32)
    heads = k_t.shape[0] // HEAD
    o_heads, stats, o_mine, o_got = [], [], [], []
    for head in range(heads):
        source = k_t
        if head == 0:
            source, route_all = together(k_t, route_all)
        else:
            source, stats[-1] = together(k_t, stats[-1])
        o_h, stat = attend_forward(head, q_t, source, v_t, starts)
        o_heads.append(o_h)
        stats.append(stat)
        if head == 1:
            *got_down, stats[-1] = together(*got_down, stats[-1])
            found_down = here.fetch_across(got_down)
        mine, other = here.halves(here.chip_exchange(o_h, 1, 0), 1)
        o_mine.append(mine)
        o_got.append(here.swap(other))
    o_own = here.ordered(
        here.head_order(o_mine, heads), here.head_order(o_got, heads), 0
    )
    gate_w = core_columns(packed, 0, core, shards, experts)
    up_w = core_columns(packed, 1, core, shards, experts)
    h_own = x_wide + dot(o_own, out_w, 0, 0)

    scale_two = rms_scale(h_own)
    b_own = (h_own * scale_two * gain_two).astype(BF16)
    b_all = jnp.concatenate([b_own, here.swap(b_own)], axis=0)
    cotangent, gate_w = together(cotangent, gate_w)
    dy_blocks = here.send_streams(cotangent[:, 0])

    logits = dot(b_all, router_w, 1, 0)
    route_hot = (
        route_all[:, :, None] == jnp.arange(experts, dtype=jnp.int32)[None, None, :]
    ).astype(F32)
    chosen = jnp.sum(logits[:, None, :] * route_hot, axis=2)
    gate_share = jax.nn.softmax(chosen, axis=1)
    shares = jnp.sum(gate_share[:, :, None] * route_hot, axis=1)
    share_wide = jnp.repeat(shares, hidden_core, axis=1)

    gate_v = dot(b_all, gate_w, 1, 0, BF16)
    *found_down, gate_v = together(*found_down, gate_v)
    down_w = here.assemble(own_down, found_down, [features])[0]
    up_v = dot(b_all, up_w, 1, 0, BF16)
    *dy_blocks, up_v = together(*dy_blocks, up_v)
    dy_own = here.join_streams(cotangent[:, 0], dy_blocks)
    dy_all = jnp.concatenate([dy_own, here.swap(dy_own)], axis=0)
    gate_f, up_f = gate_v.astype(F32), up_v.astype(F32)
    squashed = jax.nn.sigmoid(gate_f)
    mid = (gate_f * squashed * up_f * share_wide).astype(BF16)
    y_other = dot(mid[rows:], down_w, 1, 0, BF16)
    y_got = here.swap(y_other)
    y_own = dot(mid[:rows], down_w, 1, 0)
    block_own = (h_own + y_own + y_got.astype(F32)).astype(BF16)
    block_out = here.to_homes(block_own)

    slope = dot(dy_all, down_w, 1, 1)
    grad_down = dot(mid, dy_all, 0, 0, BF16)
    if quarters == experts:
        grad_down = grad_down.reshape(quarters, shards, hidden_part, features)
    else:
        grad_down = jnp.transpose(
            grad_down.reshape(experts, shards, hidden_part, quarters, features // quarters),
            (3, 1, 0, 2, 4),
        )
    held_down = here.reduce_across(grad_down)
    active = gate_f * squashed
    grad_share = jnp.sum((slope * active * up_f).reshape(2 * rows, experts, hidden_core), axis=2)
    scaled = slope * share_wide
    grad_gate_v = (scaled * up_f * squashed * (1.0 + gate_f * (1.0 - squashed))).astype(BF16)
    grad_up_v = (scaled * active).astype(BF16)
    share_got = here.swap(grad_share[rows:])
    grad_share = grad_share[:rows] + share_got

    def expert_grad(back):
        return dot(back, b_all, 0, 0, BF16).reshape(quarters, -1, features)

    grad_gate = expert_grad(grad_gate_v)
    grad_up = expert_grad(grad_up_v)
    grad_gate_v, grad_up_v, grad_gate, grad_up = together(
        grad_gate_v, grad_up_v, grad_gate, grad_up
    )
    db_other = (
        dot(grad_gate_v[rows:], gate_w, 1, 1) + dot(grad_up_v[rows:], up_w, 1, 1)
    ).astype(BF16)
    db_got = here.swap(db_other)
    db_got, held_down = together(db_got, held_down)
    db_own = dot(grad_gate_v[:rows], gate_w, 1, 1) + dot(grad_up_v[:rows], up_w, 1, 1)

    hot_own, share_own = route_hot[:rows], gate_share[:rows]
    grad_gates = jnp.sum(grad_share[:, None, :] * hot_own, axis=2)
    grad_chosen = share_own * (
        grad_gates - jnp.sum(share_own * grad_gates, axis=1, keepdims=True)
    )
    grad_logits = jnp.sum(grad_chosen[:, :, None] * hot_own, axis=1).astype(BF16)
    grad_router = dot(grad_logits, b_own, 0, 0)
    db = db_own + db_got.astype(F32) + dot(grad_logits, router_w, 1, 1)
    dh, grad_gain_two = norm_back(h_own, scale_two, gain_two, db)
    dh = dh + dy_own.astype(F32)
    dattn = dh.astype(BF16)

    dattn, grad_gate = together(dattn, grad_gate)
    held_gate = here.by_shard(here.reduce_across(grad_gate))
    do_t = dot(out_w, dattn, 1, 1, BF16)
    do_mine, do_other = here.halves(do_t, 0)
    do_t = here.ordered(do_mine, here.swap(do_other), 1)
    do_t = here.chip_exchange(do_t, 0, 1)
    grad_out = dot(dattn, o_own, 0, 1, BF16)
    out_mine, out_other = here.halves(grad_out, 0)
    grad_out = (out_mine.astype(F32) + here.swap(out_other).astype(F32)).astype(BF16)
    back_heads, back_rows, back_got = [], [], []
    for head in range(heads):
        g_h = do_t[head * o_heads[0].shape[0] : (head + 1) * o_heads[0].shape[0]]
        if head == 1:
            g_h, block_out, held_gate, grad_up, grad_out, back_heads[0] = together(
                g_h, block_out, held_gate, grad_up, grad_out, back_heads[0]
            )
            cut = grad_up.shape[1]
            held_both = here.reduce_across(
                jnp.concatenate([grad_up, grad_out.reshape(quarters, -1, features)], axis=1)
            )
        elif head:
            g_h, back_heads[-1] = together(g_h, back_heads[-1])
        parts = attend_backward(head, q_t, k_t, v_t, o_heads[head], g_h, stats[head], starts)
        parts = [here.chip_exchange(part, 1, 0) for part in parts]
        back_heads.append(parts)
        back_h = jnp.concatenate(parts, axis=0)
        mine, other = here.halves(back_h, 1)
        back_rows.append(mine)
        back_got.append(here.swap(other))

    def all_heads(which):
        return here.head_order([parts[which] for parts in back_heads], heads)

    back_t = jnp.concatenate([all_heads(0), all_heads(1), all_heads(2)], axis=0)
    qkv_w_got = here.swap(qkv_w)
    sizes = [parts.shape[0] for parts in back_heads[0]]

    def regroup(pieces):
        edges = [0, sizes[0], sizes[0] + sizes[1], sum(sizes)]
        return jnp.concatenate(
            [
                here.head_order([piece[edges[n] : edges[n + 1]] for piece in pieces], heads)
                for n in range(3)
            ],
            axis=0,
        )

    da = dot(regroup(back_rows), qkv_w, 0, 1) + dot(regroup(back_got), qkv_w_got, 0, 1)
    grad_qkv = dot(back_t, normed, 1, 0, BF16)
    dx, grad_gain_one = norm_back(x_wide, scale_one, gain_one, da)
    input_grad = here.to_homes((dx + dh).astype(BF16))

    grad_small = jnp.concatenate([grad_gain_one[None], grad_gain_two[None], grad_router], axis=0)
    grad_small = jnp.pad(grad_small, ((0, 64 - grad_small.shape[0]), (0, 0))).astype(BF16)
    grad_qkv = jnp.concatenate([grad_qkv, grad_small], axis=0).reshape(quarters, -1, features)
    grad_qkv, held_both = together(grad_qkv, held_both)
    held_up = here.by_shard(held_both[:cut])
    held_out = here.by_shard(held_both[cut:])
    held_qkv = here.by_shard(here.reduce_across(grad_qkv))
    sum_down = here.gather(here.scatter(held_down))
    sum_gate_up = here.gather(jnp.stack([here.scatter(held_gate), here.scatter(held_up)]))
    sum_out = here.gather(here.scatter(held_out))
    total = here.reduce_along(held_qkv)
    mine = jnp.stack([total] + [here.across(total, key) for key in range(1, quarters)])
    out_query, out_key, out_value, small_sum = spread_rows(
        mine, here.swap(mine), here.quarter, core, [width_q, width_k, width_k]
    )
    out_out = jnp.transpose(sum_out.astype(F32), (3, 1, 0, 2)).reshape(shard_rows, features)
    if quarters == experts:
        out_down = sum_down.astype(F32).reshape(experts, 2 * hidden_part, features)
    else:
        out_down = jnp.transpose(sum_down.astype(F32), (2, 1, 3, 0, 4)).reshape(
            experts, 2 * hidden_part, features
        )
    return (
        block_out[:, None],
        input_grad[:, None],
        small_sum[0],
        out_query,
        out_key,
        out_value,
        out_out,
        small_sum[1],
        small_sum[2 : 2 + experts].T,
        spread_experts(sum_gate_up, 0, experts, shards),
        spread_experts(sum_gate_up, 1, experts, shards),
        out_down,
    )


def solution(mesh):
    chips = mesh.shape["rep"] // 2
    mesh = jax.sharding.Mesh(
        mesh.devices.reshape(chips, 2, mesh.shape["shard"]), ("chip", "core", "shard")
    )
    in_specs = (
        P(None, PLANE, "shard", None),
        P(None, PLANE, "shard", None),
        P(None, PLANE, "shard", None),
        P(),
        P("shard"),
        P("shard", None),
        P("shard", None),
        P("shard", None),
        P("shard", None),
        P("shard"),
        P("shard", None),
        P(None, "shard", None),
        P(None, "shard", None),
        P(None, "shard", None),
    )
    out_specs = (
        P(None, PLANE, "shard", None),
        P(None, PLANE, "shard", None),
        P("shard"),
        P("shard", None),
        P("shard", None),
        P("shard", None),
        P("shard", None),
        P("shard"),
        P("shard", None),
        P(None, "shard", None),
        P(None, "shard", None),
        P(None, "shard", None),
    )
    return jax.shard_map(local, mesh=mesh, in_specs=in_specs, out_specs=out_specs, check_vma=False)
```

```python
import functools
import math

import jax
import jax.numpy as jnp
from jax import lax
from jax.experimental import pallas as pl
from jax.experimental.pallas import tpu as pltpu
from jax.sharding import PartitionSpec as P

HEAD = 64
EPSILON = 1e-05
NEGATIVE = -1e30
F32 = jnp.float32
BF16 = jnp.bfloat16
LOG2_SCALE = HEAD ** (-0.5) * math.log2(math.e)
SCALE = HEAD ** (-0.5)
PLANE = ("chip", "core")
BOTH = ("chip", "core", "shard")


SHORT = pl.CostEstimate(flops=1 << 20, transcendentals=0, bytes_accessed=1 << 20)


def together(*arrays):
    return lax.optimization_barrier(arrays)


def dot(left, right, left_dim, right_dim, kind=F32):
    return lax.dot_general(
        left, right, (((left_dim,), (right_dim,)), ((), ())), preferred_element_type=F32
    ).astype(kind)


def forward_blocks(length):
    return min(512, length), min(512, length)


def backward_blocks(length):
    return min(512, length), min(256, length)


def visible_mask(index, width, first_key, first_query, starts):
    rows = first_key + lax.broadcasted_iota(jnp.int32, (width, starts.shape[1]), 0)
    columns = first_query + lax.broadcasted_iota(jnp.int32, (1, starts.shape[1]), 1)
    return (rows >= starts) & (rows <= columns)


def side_by_side(block, group):
    return jnp.concatenate([block[g * HEAD : (g + 1) * HEAD, :] for g in range(group)], axis=1)


def three_loops(ranges, place, step, carry):
    low, full_low, full_high, high = (ranges[place, n] for n in range(4))
    carry = lax.fori_loop(low, full_low, functools.partial(step, True), carry)
    carry = lax.fori_loop(full_low, full_high, functools.partial(step, False), carry)
    return lax.fori_loop(full_high, high, functools.partial(step, True), carry)


def forward_kernel(ranges, *refs, group, wide):
    q_refs, (k_ref, v_ref, starts_ref, o_ref, stat_ref, k_rows) = refs[:group], refs[group:]
    place = pl.program_id(1)
    q_width = q_refs[0].shape[1]

    @pl.when(place == 0)
    def _():
        k_rows[...] = k_ref[...].T

    queries = jnp.concatenate([ref[...] for ref in q_refs], axis=1)
    starts = starts_ref[...]

    def step(masked, index, carry):
        high, total, mixed = carry
        first = pl.multiple_of(index * wide, wide)
        scores = (
            jnp.dot(k_rows[pl.ds(first, wide), :], queries, preferred_element_type=F32)
            * LOG2_SCALE
        )
        if masked:
            seen = visible_mask(index, wide, first, place * q_width, starts)
            scores = jnp.where(jnp.concatenate([seen] * group, axis=1), scores, NEGATIVE)
        new_high = jnp.maximum(high, jnp.max(scores, axis=0, keepdims=True))
        weights = jnp.exp2(scores - new_high)
        fade = jnp.exp2(high - new_high)
        total = total * fade + jnp.sum(weights, axis=0, keepdims=True)
        mixed = mixed * fade + jnp.dot(
            v_ref[:, pl.ds(first, wide)], weights.astype(BF16), preferred_element_type=F32
        )
        return new_high, total, mixed

    columns = group * q_width
    high, total, mixed = three_loops(
        ranges,
        place,
        step,
        (
            jnp.full((1, columns), NEGATIVE, F32),
            jnp.zeros((1, columns), F32),
            jnp.zeros((HEAD, columns), F32),
        ),
    )
    mixed = (mixed / total).astype(BF16)
    stat = high + jnp.log2(total)
    for g in range(group):
        span = slice(g * q_width, (g + 1) * q_width)
        o_ref[g * HEAD : (g + 1) * HEAD, :] = mixed[:, span]
        stat_ref[0, g : g + 1, :] = stat[:, span]


def backward_kernel(ranges, *refs, group, wide):
    q_refs, (k_ref, v_ref, o_ref, g_ref, stat_ref, starts_ref), (
        back_ref, k_rows, v_rows, dk_sum, dv_sum,
    ) = refs[:group], refs[group : group + 6], refs[group + 6 :]
    place = pl.program_id(1)
    q_width = q_refs[0].shape[1]

    @pl.when(place == 0)
    def _():
        k_rows[...] = k_ref[...].T
        v_rows[...] = v_ref[...].T
        dk_sum[...] = jnp.zeros_like(dk_sum)
        dv_sum[...] = jnp.zeros_like(dv_sum)

    queries = jnp.concatenate([ref[...] for ref in q_refs], axis=1)
    grads = side_by_side(g_ref[...], group)
    outs = side_by_side(o_ref[...], group)
    inner = jnp.sum(grads.astype(F32) * outs.astype(F32), axis=0, keepdims=True)
    stat = jnp.concatenate([stat_ref[0, g : g + 1, :] for g in range(group)], axis=1)
    starts = starts_ref[...]

    def step(masked, index, dq):
        first = pl.multiple_of(index * wide, wide)
        span = pl.ds(first, wide)
        scores = jnp.dot(k_rows[span, :], queries, preferred_element_type=F32) * LOG2_SCALE
        chances = jnp.exp2(scores - stat)
        if masked:
            seen = visible_mask(index, wide, first, place * q_width, starts)
            chances = jnp.where(jnp.concatenate([seen] * group, axis=1), chances, 0.0)
        slopes = jnp.dot(v_rows[span, :], grads, preferred_element_type=F32)
        pull = (chances * (slopes - inner)).astype(BF16)
        dv_sum[:, span] += dot(grads, chances.astype(BF16), 1, 1)
        dk_sum[:, span] += dot(queries, pull, 1, 1)
        return dq + jnp.dot(k_ref[:, span], pull, preferred_element_type=F32)

    dq = three_loops(ranges, place, step, jnp.zeros((HEAD, group * q_width), F32))
    dq = (dq * SCALE).astype(BF16)
    here = pl.ds(pl.multiple_of(place * q_width, q_width), q_width)
    for g in range(group):
        back_ref[g * HEAD : (g + 1) * HEAD, here] = dq[:, g * q_width : (g + 1) * q_width]

    @pl.when(place == pl.num_programs(1) - 1)
    def _():
        back_ref[group * HEAD : (group + 1) * HEAD, :] = (dk_sum[...] * SCALE).astype(BF16)
        back_ref[(group + 1) * HEAD :, :] = dv_sum[...].astype(BF16)


def block_ranges(starts, q_width, wide):
    length = starts.shape[1]
    count = length // q_width
    first_query = jnp.arange(count, dtype=jnp.int32) * q_width
    low = starts[0, ::q_width] // wide
    full_low = (starts[0, q_width - 1 :: q_width] + wide - 1) // wide
    full_high = (first_query + 1) // wide
    full_high = first_query // wide
    high = (first_query + q_width) // wide
    full_low = jnp.clip(full_low, low, jnp.maximum(full_high, low))
    full_high = jnp.maximum(full_high, full_low)
    return jnp.stack([low, full_low, full_high, high], axis=1)


def attention_specs(head, group, length, q_width):
    first = head * (group + 2)
    queries = [
        pl.BlockSpec((HEAD, q_width), lambda h, i, r, g=g: (first + g, i)) for g in range(group)
    ]
    keys = pl.BlockSpec((HEAD, length), lambda h, i, r: (first + group, 0))
    values = pl.BlockSpec((HEAD, length), lambda h, i, r: (first + group + 1, 0))
    per_query = pl.BlockSpec((group * HEAD, q_width), lambda h, i, r: (0, i))
    stat = pl.BlockSpec((1, group, q_width), lambda h, i, r: (0, 0, i))
    starts = pl.BlockSpec((1, q_width), lambda h, i, r: (0, i))
    return [*queries, keys, values], per_query, stat, starts


def attend_forward(head, group, qkv_t, starts, ranges):
    length = qkv_t.shape[1]
    q_width, wide = forward_blocks(length)
    rows, per_query, stat, start_spec = attention_specs(head, group, length, q_width)
    return pl.pallas_call(
        functools.partial(forward_kernel, group=group, wide=wide),
        out_shape=(
            jax.ShapeDtypeStruct((group * HEAD, length), BF16),
            jax.ShapeDtypeStruct((1, group, length), F32),
        ),
        grid_spec=pltpu.PrefetchScalarGridSpec(
            num_scalar_prefetch=1,
            grid=(1, length // q_width),
            in_specs=[*rows, start_spec],
            out_specs=(per_query, stat),
            scratch_shapes=[pltpu.VMEM((length, HEAD), BF16)],
        ),
        compiler_params=pltpu.CompilerParams(
            dimension_semantics=("arbitrary", "arbitrary"), vmem_limit_bytes=40 << 20
        ),
        cost_estimate=SHORT,
        name="attend_forward",
    )(ranges, *[qkv_t] * (group + 2), starts)


def attend_backward(head, group, qkv_t, o_h, g_h, stat_h, starts, ranges):
    length = qkv_t.shape[1]
    q_width, wide = backward_blocks(length)
    rows, per_query, stat, start_spec = attention_specs(head, group, length, q_width)
    count = (group + 2) * HEAD
    return pl.pallas_call(
        functools.partial(backward_kernel, group=group, wide=wide),
        out_shape=jax.ShapeDtypeStruct((count, length), BF16),
        grid_spec=pltpu.PrefetchScalarGridSpec(
            num_scalar_prefetch=1,
            grid=(1, length // q_width),
            in_specs=[*rows, per_query, per_query, stat, start_spec],
            out_specs=pl.BlockSpec((count, length), lambda h, i, r: (0, 0)),
            scratch_shapes=[
                pltpu.VMEM((length, HEAD), BF16),
                pltpu.VMEM((length, HEAD), BF16),
                pltpu.VMEM((HEAD, length), F32),
                pltpu.VMEM((HEAD, length), F32),
            ],
        ),
        compiler_params=pltpu.CompilerParams(
            dimension_semantics=("arbitrary", "arbitrary"), vmem_limit_bytes=40 << 20
        ),
        cost_estimate=SHORT,
        name="attend_backward",
    )(ranges, *[qkv_t] * (group + 2), o_h, g_h, stat_h, starts)


class Place:
    def __init__(self):
        self.quarters = lax.axis_size("chip")
        self.reps = 2 * self.quarters
        self.shards = lax.axis_size("shard")
        self.chips = self.shards // 4
        self.core = lax.axis_index("core")
        self.quarter = lax.axis_index("chip")
        self.shard = lax.axis_index("shard")
        self.stream = self.shard // self.chips
        self.batch = self.stream // 2
        self.source = self.quarter * 2 + self.stream % 2
        self.chip = self.shard % self.chips

    def across(self, array, key):
        return lax.ppermute(array, "chip", [(i, i ^ key) for i in range(self.quarters)])

    def swap(self, array):
        return lax.ppermute(array, "core", [(0, 1), (1, 0)])

    def moves(self, turn, home):
        pairs = []
        for quarter in range(self.quarters):
            for core in range(2):
                for shard in range(self.shards):
                    batch = turn ^ (shard & 1)
                    member = shard // 2
                    stream = 2 * batch + core
                    start = (quarter * 2 + core) * self.shards + shard
                    end = (
                        (quarter * 2 + member % 2) * self.shards
                        + stream * self.chips
                        + member // 2
                    )
                    if start != end:
                        pairs.append((end, start) if home else (start, end))
        return pairs

    def stays(self, turn):
        batch = turn ^ (self.shard & 1)
        member = self.shard // 2
        end = (2 * batch + self.core) * self.chips + member // 2
        return (member % 2 == self.core) & (end == self.shard)

    def leaving(self, array):
        odd = self.shard % 2 == 1
        return [jnp.where(odd, array[1 - turn], array[turn]) for turn in range(2)]

    def send_streams(self, array):
        return [
            lax.ppermute(part, BOTH, self.moves(turn, False))
            for turn, part in enumerate(self.leaving(array))
        ]

    def join_streams(self, array, got):
        got = [
            jnp.where(self.stays(turn), part, got[turn])
            for turn, part in enumerate(self.leaving(array))
        ]
        swapped = self.batch == 1
        return jnp.concatenate(
            [jnp.where(swapped, got[1], got[0]), jnp.where(swapped, got[0], got[1])], axis=0
        )

    def to_streams(self, array):
        return self.join_streams(array, self.send_streams(array))

    def send_homes(self, array):
        half = array.shape[0] // 2
        swapped = self.batch == 1
        parts = [array[:half], array[half:]]
        parts = [jnp.where(swapped, parts[1 - turn], parts[turn]) for turn in range(2)]
        got = [lax.ppermute(part, BOTH, self.moves(turn, True)) for turn, part in enumerate(parts)]
        return parts, got

    def join_homes(self, parts, got):
        got = [jnp.where(self.stays(turn), parts[turn], got[turn]) for turn in range(2)]
        odd = self.shard % 2 == 1
        return jnp.stack([jnp.where(odd, got[1], got[0]), jnp.where(odd, got[0], got[1])])

    def ordered(self, mine, other, axis):
        return jnp.where(
            self.core == 0,
            jnp.concatenate([mine, other], axis=axis),
            jnp.concatenate([other, mine], axis=axis),
        )

    def halves(self, array, axis):
        size = array.shape[axis] // 2
        mine = lax.dynamic_slice_in_dim(array, self.core * size, size, axis)
        other = lax.dynamic_slice_in_dim(array, (1 - self.core) * size, size, axis)
        return mine, other

    def head_order(self, pieces, heads):
        if self.chips == 1:
            return jnp.concatenate(pieces, axis=0)
        stacked = jnp.stack([p.reshape(self.chips, -1, p.shape[1]) for p in pieces], axis=1)
        return stacked.reshape(-1, pieces[0].shape[1])

    def chip_exchange(self, array, split, join):
        if self.chips == 1:
            return array
        size = array.shape[split] // self.chips
        width = array.shape[join]
        shape = list(array.shape)
        shape[split] = size
        shape[join] = width * self.chips
        result = jnp.zeros(shape, array.dtype)
        for step in range(self.chips):
            other = self.chip ^ step
            piece = lax.dynamic_slice_in_dim(array, other * size, size, split)
            if step:
                piece = lax.ppermute(
                    piece, "shard", [(i, i ^ step) for i in range(self.shards)]
                )
            result = lax.dynamic_update_slice_in_dim(result, piece, other * width, join)
        return result

    def along(self, array, step):
        return lax.ppermute(
            array, "shard", [(i, (i + step) % self.shards) for i in range(self.shards)]
        )

    def fetch_along(self, own):
        piece = lax.dynamic_index_in_dim(own, self.quarter, 1, keepdims=False)
        return [self.along(piece, step) for step in range(1, self.shards)]

    def fetch_across(self, got):
        got = jnp.stack(got)
        return [got] + [self.across(got, key) for key in range(1, self.quarters)]

    def assemble(self, own, found, widths):
        parts, quarters, rows, _ = own.shape
        shards = self.shards
        places = jnp.stack([self.shard, self.quarter]).astype(jnp.int32)
        edges = [sum(widths[:n]) for n in range(len(widths) + 1)]

        def kernel(places_ref, own_ref, *refs):
            found_refs, out_refs, sem = refs[:quarters], refs[quarters:-1], refs[-1]
            shard, quarter = places_ref[0], places_ref[1]
            copies = []
            for n, out_ref in enumerate(out_refs):
                span = pl.ds(edges[n], widths[n])
                for part in range(parts):
                    copies.append((own_ref.at[part, :, :, span], out_ref.at[part, shard]))
                    for key in range(quarters):
                        for step in range(1, shards):
                            where = (shard - step + shards) % shards
                            copies.append(
                                (
                                    found_refs[key].at[step - 1, part, :, span],
                                    out_ref.at[part, where, quarter ^ key],
                                )
                            )
            copies = [
                pltpu.make_async_copy(source, end, sem.at[n])
                for n, (source, end) in enumerate(copies)
            ]
            for copy in copies:
                copy.start()
            for copy in copies:
                copy.wait()

        whole = pl.pallas_call(
            kernel,
            out_shape=tuple(
                jax.ShapeDtypeStruct((parts, shards, quarters, rows, width), own.dtype)
                for width in widths
            ),
            in_specs=[pl.BlockSpec(memory_space=pltpu.SMEM)]
            + [pl.BlockSpec(memory_space=pl.ANY)] * (quarters + 1),
            out_specs=tuple(pl.BlockSpec(memory_space=pltpu.VMEM) for _ in widths),
            scratch_shapes=[
                pltpu.SemaphoreType.DMA((len(widths) * parts * (1 + quarters * (shards - 1)),))
            ],
            compiler_params=pltpu.CompilerParams(vmem_limit_bytes=24 << 20),
            cost_estimate=SHORT,
            name="assemble",
        )(places, own, *found)
        return [part.reshape(parts * shards * quarters * rows, -1) for part in whole]

    def gather_experts(self, w_gate, w_up):
        which = self.quarter * 2 + self.core

        def part(weight):
            size = weight.shape[1] // self.reps
            piece = lax.dynamic_slice_in_dim(weight, which * size, size, 1)
            return piece.reshape(-1, weight.shape[2])

        piece = jnp.concatenate([part(w_gate), part(w_up)], axis=0)
        return lax.all_gather(piece, ("shard", "chip", "core"), axis=0, tiled=False)

    def exchange(self, grad):
        return lax.all_to_all(grad, "chip", 0, 0, tiled=True)

    def reduce_along(self, held):
        total = lax.dynamic_index_in_dim(held, self.shard, 0, keepdims=False).astype(F32)
        for step in range(1, self.shards):
            give = lax.dynamic_index_in_dim(
                held, (self.shard + step) % self.shards, 0, keepdims=False
            )
            total = total + self.along(give, step).astype(F32)
        return total.astype(BF16)

    def scatter(self, held):
        return lax.psum_scatter(held, "shard", scatter_dimension=0, tiled=False)

    def gather(self, total):
        whole = lax.all_gather(total, PLANE, axis=0, tiled=False)
        return whole.reshape(self.quarters, 2, *total.shape)


def core_columns(packed, which, core, shards, experts):
    pieces, _, hidden = packed.shape
    rows = packed.shape[1] // 2
    part = hidden // shards // 2
    small = rows // experts
    if part % 128 or small % 16:
        parts = packed[:, which * rows : (which + 1) * rows]
        parts = parts.reshape(pieces, experts, small, shards, 2, part)
        parts = lax.dynamic_index_in_dim(parts, core, 4, keepdims=False)
        return jnp.transpose(parts, (0, 2, 1, 3, 4)).reshape(pieces * small, -1)
    group = 4

    def kernel(core_ref, *refs):
        out_ref = refs[-1]
        for shard in range(shards):
            for piece in range(group):
                for expert in range(experts):
                    column = (expert * shards + shard) * part
                    out_ref[piece * small : (piece + 1) * small, column : column + part] = refs[
                        shard
                    ][piece, expert * small : (expert + 1) * small, :]

    def columns(shard):
        return pl.BlockSpec((group, rows, part), lambda i, c: (i, which, 2 * shard + c[0]))

    return pl.pallas_call(
        kernel,
        out_shape=jax.ShapeDtypeStruct((pieces * small, experts * hidden // 2), packed.dtype),
        grid_spec=pltpu.PrefetchScalarGridSpec(
            num_scalar_prefetch=1,
            grid=(pieces // group,),
            in_specs=[columns(shard) for shard in range(shards)],
            out_specs=pl.BlockSpec(
                (group * small, experts * hidden // 2), lambda i, c: (i, 0)
            ),
        ),
        cost_estimate=SHORT,
        name="core_columns",
    )(core.astype(jnp.int32)[None], *([packed] * shards))


def spread_experts(summed, experts, shards, hidden):
    quarters, _, _, rows = summed.shape
    columns = experts * hidden // 2 // quarters
    part = hidden // shards // 2
    if part % 128 or quarters != experts:
        piece = jnp.transpose(summed[:, :, :columns].astype(F32), (1, 0, 2, 3))
        piece = piece.reshape(2, experts, shards, part, rows)
        return jnp.transpose(piece, (1, 4, 2, 0, 3)).reshape(experts, rows, hidden)

    def kernel(in_ref, out_ref):
        for core in range(2):
            turned = in_ref[0, core].astype(F32).T
            for shard in range(shards):
                first = (2 * shard + core) * part
                out_ref[0, :, first : first + part] = turned[:, shard * part : (shard + 1) * part]

    return pl.pallas_call(
        kernel,
        out_shape=jax.ShapeDtypeStruct((experts, rows, hidden), F32),
        grid=(experts,),
        in_specs=[pl.BlockSpec((1, 2, columns, rows), lambda e: (e, 0, 0, 0))],
        out_specs=pl.BlockSpec((1, rows, hidden), lambda e: (e, 0, 0)),
        cost_estimate=SHORT,
        name="spread_experts",
    )(summed)


def attention_columns(core, w_query, w_key, w_value, small, w_out):
    rows = w_query.shape[0]
    width_q, width_k, width_out = (w.shape[1] // 2 for w in (w_query, w_key, w_out))
    heads = width_k // HEAD
    part = width_q // heads
    total = width_q + 2 * width_k + small.shape[1] + width_out

    def kernel(core_ref, q_ref, k_ref, v_ref, small_ref, o_ref, out_ref):
        def half(ref, width):
            return ref[:, pl.ds(pl.multiple_of(core_ref[0] * width, 128), width)]

        query, key, value = half(q_ref, width_q), half(k_ref, width_k), half(v_ref, width_k)
        pieces = []
        for head in range(heads):
            span = slice(head * HEAD, (head + 1) * HEAD)
            pieces += [query[:, head * part : (head + 1) * part], key[:, span], value[:, span]]
        first = width_q + 2 * width_k
        out_ref[:, :first] = jnp.concatenate(pieces, axis=1)
        out_ref[:, first : first + small.shape[1]] = small_ref[...]
        out_ref[:, first + small.shape[1] :] = half(o_ref, width_out)

    return pl.pallas_call(
        kernel,
        out_shape=jax.ShapeDtypeStruct((rows, total), w_query.dtype),
        in_specs=[pl.BlockSpec(memory_space=pltpu.SMEM)]
        + [pl.BlockSpec(memory_space=pltpu.VMEM)] * 5,
        out_specs=pl.BlockSpec(memory_space=pltpu.VMEM),
        cost_estimate=SHORT,
        name="attention_columns",
    )(core.astype(jnp.int32)[None], w_query, w_key, w_value, small, w_out)


def spread_rows(mine, other, quarter, core, heads, group):
    quarters, columns, rows = mine.shape
    each = (group + 2) * HEAD
    own = heads * each // quarters
    rest = columns - own
    widths = [heads * group * HEAD, heads * HEAD, heads * HEAD]
    edges = [0, group * HEAD, (group + 1) * HEAD, each]
    places = jnp.stack([quarter, core]).astype(jnp.int32)

    def kernel(places_ref, mine_ref, other_ref, *out_refs):
        quarter, core = places_ref[0], places_ref[1]
        smalls = jnp.zeros((rest, rows), F32)
        for side, ref in enumerate((mine_ref, other_ref)):
            at = core if side == 0 else 1 - core
            whole = jnp.concatenate(
                [ref[n ^ quarter, :own].astype(F32) for n in range(quarters)], axis=0
            )
            for n in range(quarters):
                smalls = smalls + ref[n, own:].astype(F32)
            for n, (width, out_ref) in enumerate(zip(widths, out_refs)):
                span = pl.ds(pl.multiple_of(at * width, 128), width)
                picked = [
                    whole[head * each + edges[n] : head * each + edges[n + 1]]
                    for head in range(heads)
                ]
                out_ref[:, span] = jnp.concatenate(picked, axis=0).T
        out_refs[-1][...] = smalls

    shapes = [jax.ShapeDtypeStruct((rows, 2 * width), F32) for width in widths]
    shapes.append(jax.ShapeDtypeStruct((rest, rows), F32))
    return pl.pallas_call(
        kernel,
        out_shape=tuple(shapes),
        in_specs=[
            pl.BlockSpec(memory_space=pltpu.SMEM),
            pl.BlockSpec(memory_space=pltpu.VMEM),
            pl.BlockSpec(memory_space=pltpu.VMEM),
        ],
        out_specs=tuple(pl.BlockSpec(memory_space=pltpu.VMEM) for _ in shapes),
        compiler_params=pltpu.CompilerParams(vmem_limit_bytes=40 << 20),
        cost_estimate=SHORT,
        name="spread_rows",
    )(places, mine, other)


def spread_out(summed, first):
    quarters, _, columns, rows = summed.shape
    width = quarters * (columns - first)

    def kernel(in_ref, out_ref):
        for core in range(2):
            whole = jnp.concatenate(
                [in_ref[n, core, first:].astype(F32) for n in range(quarters)], axis=0
            )
            out_ref[:, core * width : (core + 1) * width] = whole.T

    return pl.pallas_call(
        kernel,
        out_shape=jax.ShapeDtypeStruct((rows, 2 * width), F32),
        in_specs=[pl.BlockSpec(memory_space=pltpu.VMEM)],
        out_specs=pl.BlockSpec(memory_space=pltpu.VMEM),
        compiler_params=pltpu.CompilerParams(vmem_limit_bytes=40 << 20),
        cost_estimate=SHORT,
        name="spread_out",
    )(summed)


def full_block(array):
    return pl.BlockSpec(array.shape, lambda i: (0, 0), pipeline_mode=pl.Buffered(1))


def row_block(rows, columns):
    return pl.BlockSpec((rows, columns), lambda i: (i, 0))


def experts_forward(b_all, gate_w, up_w, shares):
    count, features = b_all.shape
    columns = gate_w.shape[1]
    experts = shares.shape[1]
    width = columns // experts
    tile = min(256, count)

    def kernel(b_ref, gate_w_ref, up_w_ref, share_ref, gate_ref, up_ref, mid_ref):
        rows = b_ref[...]
        for expert in range(experts):
            span = slice(expert * width, (expert + 1) * width)
            gate = jnp.dot(rows, gate_w_ref[:, span], preferred_element_type=F32).astype(BF16)
            up = jnp.dot(rows, up_w_ref[:, span], preferred_element_type=F32).astype(BF16)
            gate_ref[:, span] = gate
            up_ref[:, span] = up
            gate, up = gate.astype(F32), up.astype(F32)
            share = share_ref[:, expert : expert + 1]
            mid_ref[:, span] = (gate * jax.nn.sigmoid(gate) * up * share).astype(BF16)

    return pl.pallas_call(
        kernel,
        out_shape=(jax.ShapeDtypeStruct((count, columns), BF16),) * 3,
        grid=(count // tile,),
        in_specs=[
            row_block(tile, features),
            full_block(gate_w),
            full_block(up_w),
            row_block(tile, experts),
        ],
        out_specs=(row_block(tile, columns),) * 3,
        compiler_params=pltpu.CompilerParams(vmem_limit_bytes=48 << 20),
        cost_estimate=SHORT,
        name="experts_forward",
    )(b_all, gate_w, up_w, shares)


def experts_backward(dy_all, down_w, gate_v, up_v, shares):
    count, features = dy_all.shape
    columns = gate_v.shape[1]
    experts = shares.shape[1]
    width = columns // experts
    tile = min(256, count)

    def kernel(dy_ref, down_ref, gate_ref, up_ref, share_ref, dgate_ref, dup_ref, dshare_ref):
        rows = dy_ref[...]
        sums = []
        for expert in range(experts):
            span = slice(expert * width, (expert + 1) * width)
            slope = dot(rows, down_ref[span, :], 1, 1)
            gate, up = gate_ref[:, span].astype(F32), up_ref[:, span].astype(F32)
            squashed = jax.nn.sigmoid(gate)
            active = gate * squashed
            sums.append(jnp.sum(slope * active * up, axis=1, keepdims=True))
            scaled = slope * share_ref[:, expert : expert + 1]
            dgate_ref[:, span] = (
                scaled * up * squashed * (1.0 + gate * (1.0 - squashed))
            ).astype(BF16)
            dup_ref[:, span] = (scaled * active).astype(BF16)
        dshare_ref[...] = jnp.concatenate(sums, axis=1)

    return pl.pallas_call(
        kernel,
        out_shape=(
            jax.ShapeDtypeStruct((count, columns), BF16),
            jax.ShapeDtypeStruct((count, columns), BF16),
            jax.ShapeDtypeStruct((count, experts), F32),
        ),
        grid=(count // tile,),
        in_specs=[
            row_block(tile, features),
            full_block(down_w),
            row_block(tile, columns),
            row_block(tile, columns),
            row_block(tile, experts),
        ],
        out_specs=(
            row_block(tile, columns),
            row_block(tile, columns),
            row_block(tile, experts),
        ),
        compiler_params=pltpu.CompilerParams(vmem_limit_bytes=48 << 20),
        cost_estimate=SHORT,
        name="experts_backward",
    )(dy_all, down_w, gate_v, up_v, shares)


def sum_parts(parts, shards):
    count, rows, features = parts.shape
    width = features // shards
    if width % 128:
        held = jnp.sum(parts.astype(F32), axis=0).astype(BF16)
        return jnp.transpose(held.reshape(rows, shards, width), (1, 0, 2))

    def kernel(in_ref, out_ref):
        total = in_ref[0].astype(F32)
        for n in range(1, count):
            total = total + in_ref[n].astype(F32)
        out_ref[0] = total.astype(BF16)

    return pl.pallas_call(
        kernel,
        out_shape=jax.ShapeDtypeStruct((shards, rows, width), BF16),
        grid=(shards,),
        in_specs=[pl.BlockSpec((count, rows, width), lambda i: (0, 0, i))],
        out_specs=pl.BlockSpec((1, rows, width), lambda i: (i, 0, 0)),
        cost_estimate=SHORT,
        name="sum_parts",
    )(parts)


def rms_scale(rows_in):
    return lax.rsqrt(jnp.mean(rows_in * rows_in, axis=-1, keepdims=True) + EPSILON)


def norm_back(rows_in, row_scale, gain_row, grad_normed):
    grad_gain = jnp.sum(grad_normed * rows_in * row_scale, axis=0)
    scaled = grad_normed * gain_row
    scale_cubed = row_scale * row_scale * row_scale
    grad_rows = row_scale * scaled - rows_in * scale_cubed * jnp.mean(
        scaled * rows_in, axis=-1, keepdims=True
    )
    return (grad_rows, grad_gain)


def local(
    tokens,
    cotangent,
    routes,
    lengths,
    attn_gain,
    w_query,
    w_key,
    w_value,
    w_out,
    moe_gain,
    w_router,
    w_gate,
    w_up,
    w_down,
):
    here = Place()
    core, shards, quarters = here.core, here.shards, here.quarters
    experts = w_gate.shape[0]
    features = tokens.shape[3]
    hidden_all = w_gate.shape[2]
    width_q = w_query.shape[1] // 2
    width_k = w_key.shape[1] // 2
    shard_rows = w_query.shape[0]
    rows_q = shard_rows // quarters
    hidden_part = hidden_all // shards // 2
    hidden_core = hidden_all // 2

    small = jnp.concatenate([attn_gain[:, None], moe_gain[:, None], w_router], axis=1)
    small = jnp.pad(small, ((0, 0), (0, 128 - small.shape[1])))
    own = attention_columns(core, w_query, w_key, w_value, small, w_out)
    own = own.reshape(1, quarters, rows_q, -1)
    got = here.fetch_along(own)

    length = tokens.shape[2] * shards
    my_lengths = lax.dynamic_index_in_dim(
        lax.dynamic_index_in_dim(lengths, here.batch, 0, keepdims=False),
        here.source,
        0,
        keepdims=False,
    )
    ends = jnp.cumsum(my_lengths)[:-1]
    positions = jnp.arange(length, dtype=jnp.int32)
    starts = jnp.max(
        jnp.where(ends[:, None] <= positions[None, :], ends[:, None], 0), axis=0, keepdims=True
    ).astype(jnp.int32)
    forward_ranges = block_ranges(starts, *forward_blocks(length))
    backward_ranges = block_ranges(starts, *backward_blocks(length))
    x_blocks = here.send_streams(tokens[:, 0])
    found = here.fetch_across(got)
    starts, forward_ranges, backward_ranges, *held = together(
        starts, forward_ranges, backward_ranges, *x_blocks, *found
    )
    x_blocks, found = held[:2], held[2:]
    x_own = here.join_streams(tokens[:, 0], x_blocks)
    rows = x_own.shape[0]
    w_gate, routes, x_own = together(w_gate, routes, x_own)
    packed = here.gather_experts(w_gate, w_up)
    own_down = lax.dynamic_slice_in_dim(w_down, core * hidden_part, hidden_part, 1).reshape(
        experts, quarters, hidden_part // quarters, features
    )
    route_own = here.to_streams(routes[:, 0])
    own_down, route_own = together(own_down, route_own)
    got_down = here.fetch_along(own_down)
    qkv_w, small_w, out_w = here.assemble(
        own, found, [width_q + 2 * width_k, 128, features // 2]
    )
    out_w = here.ordered(out_w, here.swap(out_w), 1)
    smalls = small_w[:, : 2 + experts].astype(F32)
    gain_one = smalls[:, 0][None, :]
    gain_two = smalls[:, 1][None, :]
    router_w = small_w[:, 2 : 2 + experts]

    x_wide = x_own.astype(F32)
    scale_one = rms_scale(x_wide)
    normed_own = (x_wide * scale_one * gain_one).astype(BF16)
    normed = here.ordered(normed_own, here.swap(normed_own), 0)
    route_all = jnp.concatenate([route_own, here.swap(route_own)], axis=0)
    qkv_t = dot(qkv_w, normed, 0, 1, BF16)
    qkv_t = here.chip_exchange(qkv_t, 0, 1)
    group = width_q // width_k
    heads = width_k // HEAD // here.chips
    o_heads, stats, o_mine, o_got = [], [], [], []
    for head in range(heads):
        source = qkv_t
        if head == 0:
            source, route_all = together(qkv_t, route_all)
        else:
            source, stats[-1] = together(qkv_t, stats[-1])
        o_h, stat = attend_forward(head, group, source, starts, forward_ranges)
        o_heads.append(o_h)
        stats.append(stat)
        if head == 1:
            *got_down, stats[-1] = together(*got_down, stats[-1])
            found_down = here.fetch_across(got_down)
        mine, other = here.halves(here.chip_exchange(o_h, 1, 0), 1)
        o_mine.append(mine)
        o_got.append(here.swap(other))
    o_own = here.ordered(
        here.head_order(o_mine, heads), here.head_order(o_got, heads), 0
    )
    cotangent, packed = together(cotangent, packed)
    dy_blocks = here.send_streams(cotangent[:, 0])
    gate_w = core_columns(packed, 0, core, shards, experts)
    up_w = core_columns(packed, 1, core, shards, experts)
    h_own = x_wide + dot(o_own, out_w, 0, 0)

    scale_two = rms_scale(h_own)
    b_own = (h_own * scale_two * gain_two).astype(BF16)
    b_all = jnp.concatenate([b_own, here.swap(b_own)], axis=0)

    logits = dot(b_all, router_w, 1, 0)
    route_hot = (
        route_all[:, :, None] == jnp.arange(experts, dtype=jnp.int32)[None, None, :]
    ).astype(F32)
    chosen = jnp.sum(logits[:, None, :] * route_hot, axis=2)
    gate_share = jax.nn.softmax(chosen, axis=1)
    shares = jnp.sum(gate_share[:, :, None] * route_hot, axis=1)

    gate_v, up_v, mid = experts_forward(b_all, gate_w, up_w, shares)
    *found_down, mid = together(*found_down, mid)
    *dy_blocks, mid = together(*dy_blocks, mid)
    dy_own = here.join_streams(cotangent[:, 0], dy_blocks)
    dy_all = jnp.concatenate([dy_own, here.swap(dy_own)], axis=0)
    down_w = here.assemble(own_down, found_down, [features])[0]
    y_other = dot(mid[rows:], down_w, 1, 0, BF16)
    y_got = here.swap(y_other)
    y_own = dot(mid[:rows], down_w, 1, 0)
    block_own = (h_own + y_own + y_got.astype(F32)).astype(BF16)
    block_out = here.join_homes(*here.send_homes(block_own))

    grad_down = dot(mid, dy_all, 0, 0, BF16)
    if quarters == experts:
        grad_down = grad_down.reshape(quarters, shards, hidden_part, features)
    else:
        grad_down = jnp.transpose(
            grad_down.reshape(experts, shards, hidden_part, quarters, features // quarters),
            (3, 1, 0, 2, 4),
        )
    dy_all, down_w, grad_down = together(dy_all, down_w, grad_down)
    got_grad_down = here.exchange(grad_down)
    grad_gate_v, grad_up_v, grad_share = experts_backward(dy_all, down_w, gate_v, up_v, shares)
    share_got = here.swap(grad_share[rows:])
    grad_share = grad_share[:rows] + share_got

    def expert_grad(back):
        return dot(back, b_all, 0, 0, BF16).reshape(quarters, -1, features)

    grad_gate = expert_grad(grad_gate_v)
    grad_up = expert_grad(grad_up_v)
    grad_gate_v, grad_up_v, grad_gate, grad_up, got_grad_down = together(
        grad_gate_v, grad_up_v, grad_gate, grad_up, got_grad_down
    )
    held_down = jnp.sum(got_grad_down.astype(F32), axis=0).astype(BF16)
    db_other = (
        dot(grad_gate_v[rows:], gate_w, 1, 1) + dot(grad_up_v[rows:], up_w, 1, 1)
    ).astype(BF16)
    db_got = here.swap(db_other)
    got_grad_gate = here.exchange(grad_gate)
    db_own = dot(grad_gate_v[:rows], gate_w, 1, 1) + dot(grad_up_v[:rows], up_w, 1, 1)

    hot_own, share_own = route_hot[:rows], gate_share[:rows]
    grad_gates = jnp.sum(grad_share[:, None, :] * hot_own, axis=2)
    grad_chosen = share_own * (
        grad_gates - jnp.sum(share_own * grad_gates, axis=1, keepdims=True)
    )
    grad_logits = jnp.sum(grad_chosen[:, :, None] * hot_own, axis=1).astype(BF16)
    grad_router = dot(grad_logits, b_own, 0, 0)
    db = db_own + db_got.astype(F32) + dot(grad_logits, router_w, 1, 1)
    dh, grad_gain_two = norm_back(h_own, scale_two, gain_two, db)
    dh = dh + dy_own.astype(F32)
    dattn = dh.astype(BF16)

    qkv_w_got = here.swap(qkv_w)
    do_t = dot(out_w, dattn, 1, 1, BF16)
    do_mine, do_other = here.halves(do_t, 0)
    do_t = here.ordered(do_mine, here.swap(do_other), 1)
    do_t = here.chip_exchange(do_t, 0, 1)
    grad_out = dot(dattn, o_own, 0, 1, BF16)
    out_mine, out_other = here.halves(grad_out, 0)
    grad_out = (out_mine.astype(F32) + here.swap(out_other).astype(F32)).astype(BF16)
    back_heads, back_rows, back_got = [], [], []
    for head in range(heads):
        g_h = do_t[head * o_heads[0].shape[0] : (head + 1) * o_heads[0].shape[0]]
        if head == 0:
            g_h, grad_out, qkv_w_got = together(g_h, grad_out, qkv_w_got)
        elif head == 1:
            g_h, block_out, got_grad_gate, grad_out, back_heads[0] = together(
                g_h, block_out, got_grad_gate, grad_out, back_heads[0]
            )
            got_grad_out = here.exchange(grad_out.reshape(quarters, -1, features))
            total_gate = here.scatter(sum_parts(got_grad_gate, shards))
        else:
            g_h, back_heads[-1] = together(g_h, back_heads[-1])
        if head == heads // 2:
            g_h, got_grad_out, grad_up = together(g_h, got_grad_out, grad_up)
            got_grad_up = here.exchange(grad_up)
            total_out = here.scatter(sum_parts(got_grad_out, shards))
        back_h = attend_backward(
            head, group, qkv_t, o_heads[head], g_h, stats[head], starts, backward_ranges
        )
        back_h = here.chip_exchange(back_h, 1, 0)
        back_heads.append(back_h)
        mine, other = here.halves(back_h, 1)
        back_rows.append(mine)
        back_got.append(here.swap(other))

    grad_qkv = jnp.stack(
        [
            dot(back_h, normed, 1, 0, BF16).reshape(here.chips, -1, features)
            for back_h in back_heads
        ],
        axis=1,
    ).reshape(quarters, -1, features)
    grad_qkv, got_grad_up = together(grad_qkv, got_grad_up)
    total_up = here.scatter(sum_parts(got_grad_up, shards))
    got_grad_qkv = here.exchange(grad_qkv)
    da = dot(here.head_order(back_rows, heads), qkv_w, 0, 1) + dot(
        here.head_order(back_got, heads), qkv_w_got, 0, 1
    )
    da, got_grad_qkv = together(da, got_grad_qkv)
    dx, grad_gain_one = norm_back(x_wide, scale_one, gain_one, da)
    dx_rows = (dx + dh).astype(BF16)

    grad_small = jnp.concatenate([grad_gain_one[None], grad_gain_two[None], grad_router], axis=0)
    grad_small = jnp.pad(grad_small, ((0, 16 - grad_small.shape[0]), (0, 0))).astype(BF16)
    grad_small = jnp.transpose(grad_small.reshape(16, shards, shard_rows), (1, 0, 2))
    held_qkv = sum_parts(got_grad_qkv, shards)
    held_qkv, total_up, total_out = together(held_qkv, total_up, total_out)
    held_qkv = jnp.concatenate([held_qkv, grad_small], axis=1)
    total = here.reduce_along(held_qkv)
    total, dx_rows = together(total, dx_rows)
    input_grad = here.join_homes(*here.send_homes(dx_rows))
    sum_down = here.gather(here.scatter(held_down))
    sum_gate = here.gather(total_gate)
    sum_up_out = here.gather(jnp.concatenate([total_up, total_out], axis=0))
    cut = total_up.shape[0]
    mine = jnp.stack([total] + [here.across(total, key) for key in range(1, quarters)])
    out_query, out_key, out_value, small_sum = spread_rows(
        mine, here.swap(mine), here.quarter, core, width_k // HEAD, group
    )
    if (features // 2) % 128 or (features // 2 // quarters) % 16:
        out_out = sum_up_out[:, :, cut:].astype(F32)
        out_out = jnp.transpose(out_out, (3, 1, 0, 2)).reshape(shard_rows, features)
    else:
        out_out = spread_out(sum_up_out, cut)
    if quarters == experts:
        out_down = sum_down.astype(F32).reshape(experts, 2 * hidden_part, features)
    else:
        out_down = jnp.transpose(sum_down.astype(F32), (2, 1, 3, 0, 4)).reshape(
            experts, 2 * hidden_part, features
        )
    return (
        block_out[:, None],
        input_grad[:, None],
        small_sum[0],
        out_query,
        out_key,
        out_value,
        out_out,
        small_sum[1],
        small_sum[2 : 2 + experts].T,
        spread_experts(sum_gate, experts, shards, hidden_all),
        spread_experts(sum_up_out, experts, shards, hidden_all),
        out_down,
    )


def solution(mesh):
    chips = mesh.shape["rep"] // 2
    mesh = jax.sharding.Mesh(
        mesh.devices.reshape(chips, 2, mesh.shape["shard"]), ("chip", "core", "shard")
    )
    in_specs = (
        P(None, PLANE, "shard", None),
        P(None, PLANE, "shard", None),
        P(None, PLANE, "shard", None),
        P(),
        P("shard"),
        P("shard", None),
        P("shard", None),
        P("shard", None),
        P("shard", None),
        P("shard"),
        P("shard", None),
        P(None, "shard", None),
        P(None, "shard", None),
        P(None, "shard", None),
    )
    out_specs = (
        P(None, PLANE, "shard", None),
        P(None, PLANE, "shard", None),
        P("shard"),
        P("shard", None),
        P("shard", None),
        P("shard", None),
        P("shard", None),
        P("shard"),
        P("shard", None),
        P(None, "shard", None),
        P(None, "shard", None),
        P(None, "shard", None),
    )
    return jax.shard_map(local, mesh=mesh, in_specs=in_specs, out_specs=out_specs, check_vma=False)
```

```python
import functools
import math

import jax
import jax.numpy as jnp
from jax import lax
from jax.experimental import pallas as pl
from jax.experimental.pallas import tpu as pltpu
from jax.sharding import PartitionSpec as P

HEAD = 64
EPSILON = 1e-05
NEGATIVE = -1e30
F32 = jnp.float32
BF16 = jnp.bfloat16
LOG2_SCALE = HEAD ** (-0.5) * math.log2(math.e)
SCALE = HEAD ** (-0.5)
PLANE = ("chip", "core")
BOTH = ("chip", "core", "shard")


SHORT = pl.CostEstimate(flops=1 << 20, transcendentals=0, bytes_accessed=1 << 20)


def together(*arrays):
    return lax.optimization_barrier(arrays)


def dot(left, right, left_dim, right_dim, kind=F32):
    return lax.dot_general(
        left, right, (((left_dim,), (right_dim,)), ((), ())), preferred_element_type=F32
    ).astype(kind)


def forward_blocks(length):
    return min(512, length), min(512, length)


def backward_blocks(length):
    return min(256, length), min(256, length)


def visible_mask(index, width, first_key, first_query, starts):
    rows = first_key + lax.broadcasted_iota(jnp.int32, (width, starts.shape[1]), 0)
    columns = first_query + lax.broadcasted_iota(jnp.int32, (1, starts.shape[1]), 1)
    return (rows >= starts) & (rows <= columns)


def side_by_side(block, group):
    return jnp.concatenate([block[g * HEAD : (g + 1) * HEAD, :] for g in range(group)], axis=1)


def three_loops(ranges, place, step, carry):
    low, full_low, full_high, high = (ranges[place, n] for n in range(4))
    carry = lax.fori_loop(low, full_low, functools.partial(step, True), carry)
    carry = lax.fori_loop(full_low, full_high, functools.partial(step, False), carry)
    return lax.fori_loop(full_high, high, functools.partial(step, True), carry)


def forward_kernel(ranges, *refs, group, wide):
    q_refs, (k_ref, v_ref, starts_ref, o_ref, stat_ref, k_rows) = refs[:group], refs[group:]
    place = pl.program_id(1)
    q_width = q_refs[0].shape[1]

    @pl.when(place == 0)
    def _():
        k_rows[...] = k_ref[...].T

    queries = jnp.concatenate([ref[...] for ref in q_refs], axis=1)
    starts = starts_ref[...]

    def step(masked, index, carry):
        high, total, mixed = carry
        first = pl.multiple_of(index * wide, wide)
        scores = (
            jnp.dot(k_rows[pl.ds(first, wide), :], queries, preferred_element_type=F32)
            * LOG2_SCALE
        )
        if masked:
            seen = visible_mask(index, wide, first, place * q_width, starts)
            scores = jnp.where(jnp.concatenate([seen] * group, axis=1), scores, NEGATIVE)
        new_high = jnp.maximum(high, jnp.max(scores, axis=0, keepdims=True))
        weights = jnp.exp2(scores - new_high)
        fade = jnp.exp2(high - new_high)
        total = total * fade + jnp.sum(weights, axis=0, keepdims=True)
        mixed = mixed * fade + jnp.dot(
            v_ref[:, pl.ds(first, wide)], weights.astype(BF16), preferred_element_type=F32
        )
        return new_high, total, mixed

    columns = group * q_width
    high, total, mixed = three_loops(
        ranges,
        place,
        step,
        (
            jnp.full((1, columns), NEGATIVE, F32),
            jnp.zeros((1, columns), F32),
            jnp.zeros((HEAD, columns), F32),
        ),
    )
    mixed = (mixed / total).astype(BF16)
    stat = high + jnp.log2(total)
    for g in range(group):
        span = slice(g * q_width, (g + 1) * q_width)
        o_ref[g * HEAD : (g + 1) * HEAD, :] = mixed[:, span]
        stat_ref[0, g : g + 1, :] = stat[:, span]


def backward_kernel(ranges, *refs, group, wide):
    q_refs, (k_ref, v_ref, o_ref, g_ref, stat_ref, starts_ref), (
        back_ref, k_rows, v_rows, dk_sum, dv_sum,
    ) = refs[:group], refs[group : group + 6], refs[group + 6 :]
    place = pl.program_id(1)
    q_width = q_refs[0].shape[1]

    @pl.when(place == 0)
    def _():
        k_rows[...] = k_ref[...].T
        v_rows[...] = v_ref[...].T
        dk_sum[...] = jnp.zeros_like(dk_sum)
        dv_sum[...] = jnp.zeros_like(dv_sum)

    queries = jnp.concatenate([ref[...] for ref in q_refs], axis=1)
    grads = side_by_side(g_ref[...], group)
    outs = side_by_side(o_ref[...], group)
    inner = jnp.sum(grads.astype(F32) * outs.astype(F32), axis=0, keepdims=True)
    stat = jnp.concatenate([stat_ref[0, g : g + 1, :] for g in range(group)], axis=1)
    starts = starts_ref[...]

    def step(masked, index, dq):
        first = pl.multiple_of(index * wide, wide)
        span = pl.ds(first, wide)
        scores = jnp.dot(k_rows[span, :], queries, preferred_element_type=F32) * LOG2_SCALE
        chances = jnp.exp2(scores - stat)
        if masked:
            seen = visible_mask(index, wide, first, place * q_width, starts)
            chances = jnp.where(jnp.concatenate([seen] * group, axis=1), chances, 0.0)
        slopes = jnp.dot(v_rows[span, :], grads, preferred_element_type=F32)
        pull = (chances * (slopes - inner)).astype(BF16)
        dv_sum[:, span] += dot(grads, chances.astype(BF16), 1, 1)
        dk_sum[:, span] += dot(queries, pull, 1, 1)
        return dq + jnp.dot(k_ref[:, span], pull, preferred_element_type=F32)

    dq = three_loops(ranges, place, step, jnp.zeros((HEAD, group * q_width), F32))
    dq = (dq * SCALE).astype(BF16)
    here = pl.ds(pl.multiple_of(place * q_width, q_width), q_width)
    for g in range(group):
        back_ref[g * HEAD : (g + 1) * HEAD, here] = dq[:, g * q_width : (g + 1) * q_width]

    @pl.when(place == pl.num_programs(1) - 1)
    def _():
        back_ref[group * HEAD : (group + 1) * HEAD, :] = (dk_sum[...] * SCALE).astype(BF16)
        back_ref[(group + 1) * HEAD :, :] = dv_sum[...].astype(BF16)


def block_ranges(starts, q_width, wide):
    length = starts.shape[1]
    count = length // q_width
    first_query = jnp.arange(count, dtype=jnp.int32) * q_width
    low = starts[0, ::q_width] // wide
    full_low = (starts[0, q_width - 1 :: q_width] + wide - 1) // wide
    full_high = (first_query + 1) // wide
    full_high = first_query // wide
    high = (first_query + q_width) // wide
    full_low = jnp.clip(full_low, low, jnp.maximum(full_high, low))
    full_high = jnp.maximum(full_high, full_low)
    return jnp.stack([low, full_low, full_high, high], axis=1)


def attention_specs(head, group, length, q_width):
    first = head * (group + 2)
    queries = [
        pl.BlockSpec((HEAD, q_width), lambda h, i, r, g=g: (first + g, i)) for g in range(group)
    ]
    keys = pl.BlockSpec((HEAD, length), lambda h, i, r: (first + group, 0))
    values = pl.BlockSpec((HEAD, length), lambda h, i, r: (first + group + 1, 0))
    per_query = pl.BlockSpec((group * HEAD, q_width), lambda h, i, r: (0, i))
    stat = pl.BlockSpec((1, group, q_width), lambda h, i, r: (0, 0, i))
    starts = pl.BlockSpec((1, q_width), lambda h, i, r: (0, i))
    return [*queries, keys, values], per_query, stat, starts


def attend_forward(head, group, qkv_t, starts, ranges):
    length = qkv_t.shape[1]
    q_width, wide = forward_blocks(length)
    rows, per_query, stat, start_spec = attention_specs(head, group, length, q_width)
    return pl.pallas_call(
        functools.partial(forward_kernel, group=group, wide=wide),
        out_shape=(
            jax.ShapeDtypeStruct((group * HEAD, length), BF16),
            jax.ShapeDtypeStruct((1, group, length), F32),
        ),
        grid_spec=pltpu.PrefetchScalarGridSpec(
            num_scalar_prefetch=1,
            grid=(1, length // q_width),
            in_specs=[*rows, start_spec],
            out_specs=(per_query, stat),
            scratch_shapes=[pltpu.VMEM((length, HEAD), BF16)],
        ),
        compiler_params=pltpu.CompilerParams(
            dimension_semantics=("arbitrary", "arbitrary"), vmem_limit_bytes=40 << 20
        ),
        cost_estimate=SHORT,
        name="attend_forward",
    )(ranges, *[qkv_t] * (group + 2), starts)


def attend_backward(head, group, qkv_t, o_h, g_h, stat_h, starts, ranges):
    length = qkv_t.shape[1]
    q_width, wide = backward_blocks(length)
    rows, per_query, stat, start_spec = attention_specs(head, group, length, q_width)
    count = (group + 2) * HEAD
    return pl.pallas_call(
        functools.partial(backward_kernel, group=group, wide=wide),
        out_shape=jax.ShapeDtypeStruct((count, length), BF16),
        grid_spec=pltpu.PrefetchScalarGridSpec(
            num_scalar_prefetch=1,
            grid=(1, length // q_width),
            in_specs=[*rows, per_query, per_query, stat, start_spec],
            out_specs=pl.BlockSpec((count, length), lambda h, i, r: (0, 0)),
            scratch_shapes=[
                pltpu.VMEM((length, HEAD), BF16),
                pltpu.VMEM((length, HEAD), BF16),
                pltpu.VMEM((HEAD, length), F32),
                pltpu.VMEM((HEAD, length), F32),
            ],
        ),
        compiler_params=pltpu.CompilerParams(
            dimension_semantics=("arbitrary", "arbitrary"), vmem_limit_bytes=40 << 20
        ),
        cost_estimate=SHORT,
        name="attend_backward",
    )(ranges, *[qkv_t] * (group + 2), o_h, g_h, stat_h, starts)


class Place:
    def __init__(self):
        self.quarters = lax.axis_size("chip")
        self.reps = 2 * self.quarters
        self.shards = lax.axis_size("shard")
        self.chips = self.shards // 4
        self.core = lax.axis_index("core")
        self.quarter = lax.axis_index("chip")
        self.shard = lax.axis_index("shard")
        self.stream = self.shard // self.chips
        self.batch = self.stream // 2
        self.source = self.quarter * 2 + self.stream % 2
        self.chip = self.shard % self.chips

    def across(self, array, key):
        return lax.ppermute(array, "chip", [(i, i ^ key) for i in range(self.quarters)])

    def swap(self, array):
        return lax.ppermute(array, "core", [(0, 1), (1, 0)])

    def moves(self, turn, home):
        pairs = []
        for quarter in range(self.quarters):
            for core in range(2):
                for shard in range(self.shards):
                    batch = turn ^ (shard & 1)
                    member = shard // 2
                    stream = 2 * batch + core
                    start = (quarter * 2 + core) * self.shards + shard
                    end = (
                        (quarter * 2 + member % 2) * self.shards
                        + stream * self.chips
                        + member // 2
                    )
                    if start != end:
                        pairs.append((end, start) if home else (start, end))
        return pairs

    def stays(self, turn):
        batch = turn ^ (self.shard & 1)
        member = self.shard // 2
        end = (2 * batch + self.core) * self.chips + member // 2
        return (member % 2 == self.core) & (end == self.shard)

    def leaving(self, array):
        odd = self.shard % 2 == 1
        return [jnp.where(odd, array[1 - turn], array[turn]) for turn in range(2)]

    def send_streams(self, array):
        return [
            lax.ppermute(part, BOTH, self.moves(turn, False))
            for turn, part in enumerate(self.leaving(array))
        ]

    def join_streams(self, array, got):
        got = [
            jnp.where(self.stays(turn), part, got[turn])
            for turn, part in enumerate(self.leaving(array))
        ]
        swapped = self.batch == 1
        return jnp.concatenate(
            [jnp.where(swapped, got[1], got[0]), jnp.where(swapped, got[0], got[1])], axis=0
        )

    def to_streams(self, array):
        return self.join_streams(array, self.send_streams(array))

    def send_homes(self, array):
        half = array.shape[0] // 2
        swapped = self.batch == 1
        parts = [array[:half], array[half:]]
        parts = [jnp.where(swapped, parts[1 - turn], parts[turn]) for turn in range(2)]
        got = [lax.ppermute(part, BOTH, self.moves(turn, True)) for turn, part in enumerate(parts)]
        return parts, got

    def join_homes(self, parts, got):
        got = [jnp.where(self.stays(turn), parts[turn], got[turn]) for turn in range(2)]
        odd = self.shard % 2 == 1
        return jnp.stack([jnp.where(odd, got[1], got[0]), jnp.where(odd, got[0], got[1])])

    def ordered(self, mine, other, axis):
        return jnp.where(
            self.core == 0,
            jnp.concatenate([mine, other], axis=axis),
            jnp.concatenate([other, mine], axis=axis),
        )

    def halves(self, array, axis):
        size = array.shape[axis] // 2
        mine = lax.dynamic_slice_in_dim(array, self.core * size, size, axis)
        other = lax.dynamic_slice_in_dim(array, (1 - self.core) * size, size, axis)
        return mine, other

    def head_order(self, pieces, heads):
        if self.chips == 1:
            return jnp.concatenate(pieces, axis=0)
        stacked = jnp.stack([p.reshape(self.chips, -1, p.shape[1]) for p in pieces], axis=1)
        return stacked.reshape(-1, pieces[0].shape[1])

    def chip_exchange(self, array, split, join):
        if self.chips == 1:
            return array
        size = array.shape[split] // self.chips
        width = array.shape[join]
        shape = list(array.shape)
        shape[split] = size
        shape[join] = width * self.chips
        result = jnp.zeros(shape, array.dtype)
        for step in range(self.chips):
            other = self.chip ^ step
            piece = lax.dynamic_slice_in_dim(array, other * size, size, split)
            if step:
                piece = lax.ppermute(
                    piece, "shard", [(i, i ^ step) for i in range(self.shards)]
                )
            result = lax.dynamic_update_slice_in_dim(result, piece, other * width, join)
        return result

    def along(self, array, step):
        return lax.ppermute(
            array, "shard", [(i, (i + step) % self.shards) for i in range(self.shards)]
        )

    def fetch_along(self, own):
        piece = lax.dynamic_index_in_dim(own, self.quarter, 1, keepdims=False)
        return [self.along(piece, step) for step in range(1, self.shards)]

    def fetch_across(self, got):
        got = jnp.stack(got)
        return [got] + [self.across(got, key) for key in range(1, self.quarters)]

    def assemble(self, own, found, widths):
        parts, quarters, rows, _ = own.shape
        shards = self.shards
        places = jnp.stack([self.shard, self.quarter]).astype(jnp.int32)
        edges = [sum(widths[:n]) for n in range(len(widths) + 1)]

        def kernel(places_ref, own_ref, *refs):
            found_refs, out_refs, sem = refs[:quarters], refs[quarters:-1], refs[-1]
            shard, quarter = places_ref[0], places_ref[1]
            copies = []
            for n, out_ref in enumerate(out_refs):
                span = pl.ds(edges[n], widths[n])
                for part in range(parts):
                    copies.append((own_ref.at[part, :, :, span], out_ref.at[part, shard]))
                    for key in range(quarters):
                        for step in range(1, shards):
                            where = (shard - step + shards) % shards
                            copies.append(
                                (
                                    found_refs[key].at[step - 1, part, :, span],
                                    out_ref.at[part, where, quarter ^ key],
                                )
                            )
            copies = [
                pltpu.make_async_copy(source, end, sem.at[n])
                for n, (source, end) in enumerate(copies)
            ]
            for copy in copies:
                copy.start()
            for copy in copies:
                copy.wait()

        whole = pl.pallas_call(
            kernel,
            out_shape=tuple(
                jax.ShapeDtypeStruct((parts, shards, quarters, rows, width), own.dtype)
                for width in widths
            ),
            in_specs=[pl.BlockSpec(memory_space=pltpu.SMEM)]
            + [pl.BlockSpec(memory_space=pl.ANY)] * (quarters + 1),
            out_specs=tuple(pl.BlockSpec(memory_space=pltpu.VMEM) for _ in widths),
            scratch_shapes=[
                pltpu.SemaphoreType.DMA((len(widths) * parts * (1 + quarters * (shards - 1)),))
            ],
            compiler_params=pltpu.CompilerParams(vmem_limit_bytes=24 << 20),
            cost_estimate=SHORT,
            name="assemble",
        )(places, own, *found)
        return [part.reshape(parts * shards * quarters * rows, -1) for part in whole]

    def gather_experts(self, w_gate, w_up):
        which = self.quarter * 2 + self.core

        def part(weight):
            size = weight.shape[1] // self.reps
            piece = lax.dynamic_slice_in_dim(weight, which * size, size, 1)
            return piece.reshape(-1, weight.shape[2])

        piece = jnp.concatenate([part(w_gate), part(w_up)], axis=0)
        return lax.all_gather(piece, ("shard", "chip", "core"), axis=0, tiled=False)

    def exchange(self, grad):
        return lax.all_to_all(grad, "chip", 0, 0, tiled=True)

    def reduce_along(self, held):
        total = lax.dynamic_index_in_dim(held, self.shard, 0, keepdims=False).astype(F32)
        for step in range(1, self.shards):
            give = lax.dynamic_index_in_dim(
                held, (self.shard + step) % self.shards, 0, keepdims=False
            )
            total = total + self.along(give, step).astype(F32)
        return total.astype(BF16)

    def scatter(self, held):
        return lax.psum_scatter(held, "shard", scatter_dimension=0, tiled=False)

    def gather(self, total):
        whole = lax.all_gather(total, PLANE, axis=0, tiled=False)
        return whole.reshape(self.quarters, 2, *total.shape)


def core_columns(packed, which, core, shards, experts):
    pieces, _, hidden = packed.shape
    rows = packed.shape[1] // 2
    part = hidden // shards // 2
    small = rows // experts
    if part % 128 or small % 16:
        parts = packed[:, which * rows : (which + 1) * rows]
        parts = parts.reshape(pieces, experts, small, shards, 2, part)
        parts = lax.dynamic_index_in_dim(parts, core, 4, keepdims=False)
        return jnp.transpose(parts, (0, 2, 1, 3, 4)).reshape(pieces * small, -1)
    group = 4

    def kernel(core_ref, *refs):
        out_ref = refs[-1]
        for shard in range(shards):
            for piece in range(group):
                for expert in range(experts):
                    column = (expert * shards + shard) * part
                    out_ref[piece * small : (piece + 1) * small, column : column + part] = refs[
                        shard
                    ][piece, expert * small : (expert + 1) * small, :]

    def columns(shard):
        return pl.BlockSpec((group, rows, part), lambda i, c: (i, which, 2 * shard + c[0]))

    return pl.pallas_call(
        kernel,
        out_shape=jax.ShapeDtypeStruct((pieces * small, experts * hidden // 2), packed.dtype),
        grid_spec=pltpu.PrefetchScalarGridSpec(
            num_scalar_prefetch=1,
            grid=(pieces // group,),
            in_specs=[columns(shard) for shard in range(shards)],
            out_specs=pl.BlockSpec(
                (group * small, experts * hidden // 2), lambda i, c: (i, 0)
            ),
        ),
        cost_estimate=SHORT,
        name="core_columns",
    )(core.astype(jnp.int32)[None], *([packed] * shards))


def spread_experts(summed, experts, shards, hidden):
    quarters, _, _, rows = summed.shape
    columns = experts * hidden // 2 // quarters
    part = hidden // shards // 2
    if part % 128 or quarters != experts:
        piece = jnp.transpose(summed[:, :, :columns].astype(F32), (1, 0, 2, 3))
        piece = piece.reshape(2, experts, shards, part, rows)
        return jnp.transpose(piece, (1, 4, 2, 0, 3)).reshape(experts, rows, hidden)

    def kernel(in_ref, out_ref):
        for core in range(2):
            turned = in_ref[0, core].astype(F32).T
            for shard in range(shards):
                first = (2 * shard + core) * part
                out_ref[0, :, first : first + part] = turned[:, shard * part : (shard + 1) * part]

    return pl.pallas_call(
        kernel,
        out_shape=jax.ShapeDtypeStruct((experts, rows, hidden), F32),
        grid=(experts,),
        in_specs=[pl.BlockSpec((1, 2, columns, rows), lambda e: (e, 0, 0, 0))],
        out_specs=pl.BlockSpec((1, rows, hidden), lambda e: (e, 0, 0)),
        cost_estimate=SHORT,
        name="spread_experts",
    )(summed)


def attention_columns(core, w_query, w_key, w_value, small, w_out):
    rows = w_query.shape[0]
    width_q, width_k, width_out = (w.shape[1] // 2 for w in (w_query, w_key, w_out))
    heads = width_k // HEAD
    part = width_q // heads
    total = width_q + 2 * width_k + small.shape[1] + width_out

    def kernel(core_ref, q_ref, k_ref, v_ref, small_ref, o_ref, out_ref):
        def half(ref, width):
            return ref[:, pl.ds(pl.multiple_of(core_ref[0] * width, 128), width)]

        query, key, value = half(q_ref, width_q), half(k_ref, width_k), half(v_ref, width_k)
        pieces = []
        for head in range(heads):
            span = slice(head * HEAD, (head + 1) * HEAD)
            pieces += [query[:, head * part : (head + 1) * part], key[:, span], value[:, span]]
        first = width_q + 2 * width_k
        out_ref[:, :first] = jnp.concatenate(pieces, axis=1)
        out_ref[:, first : first + small.shape[1]] = small_ref[...]
        out_ref[:, first + small.shape[1] :] = half(o_ref, width_out)

    return pl.pallas_call(
        kernel,
        out_shape=jax.ShapeDtypeStruct((rows, total), w_query.dtype),
        in_specs=[pl.BlockSpec(memory_space=pltpu.SMEM)]
        + [pl.BlockSpec(memory_space=pltpu.VMEM)] * 5,
        out_specs=pl.BlockSpec(memory_space=pltpu.VMEM),
        cost_estimate=SHORT,
        name="attention_columns",
    )(core.astype(jnp.int32)[None], w_query, w_key, w_value, small, w_out)


def spread_rows(mine, other, quarter, core, heads, group):
    quarters, columns, rows = mine.shape
    each = (group + 2) * HEAD
    own = heads * each // quarters
    rest = columns - own
    widths = [heads * group * HEAD, heads * HEAD, heads * HEAD]
    edges = [0, group * HEAD, (group + 1) * HEAD, each]
    places = jnp.stack([quarter, core]).astype(jnp.int32)

    def kernel(places_ref, mine_ref, other_ref, *out_refs):
        quarter, core = places_ref[0], places_ref[1]
        smalls = jnp.zeros((rest, rows), F32)
        for side, ref in enumerate((mine_ref, other_ref)):
            at = core if side == 0 else 1 - core
            whole = jnp.concatenate(
                [ref[n ^ quarter, :own].astype(F32) for n in range(quarters)], axis=0
            )
            for n in range(quarters):
                smalls = smalls + ref[n, own:].astype(F32)
            for n, (width, out_ref) in enumerate(zip(widths, out_refs)):
                span = pl.ds(pl.multiple_of(at * width, 128), width)
                picked = [
                    whole[head * each + edges[n] : head * each + edges[n + 1]]
                    for head in range(heads)
                ]
                out_ref[:, span] = jnp.concatenate(picked, axis=0).T
        out_refs[-1][...] = smalls

    shapes = [jax.ShapeDtypeStruct((rows, 2 * width), F32) for width in widths]
    shapes.append(jax.ShapeDtypeStruct((rest, rows), F32))
    return pl.pallas_call(
        kernel,
        out_shape=tuple(shapes),
        in_specs=[
            pl.BlockSpec(memory_space=pltpu.SMEM),
            pl.BlockSpec(memory_space=pltpu.VMEM),
            pl.BlockSpec(memory_space=pltpu.VMEM),
        ],
        out_specs=tuple(pl.BlockSpec(memory_space=pltpu.VMEM) for _ in shapes),
        compiler_params=pltpu.CompilerParams(vmem_limit_bytes=40 << 20),
        cost_estimate=SHORT,
        name="spread_rows",
    )(places, mine, other)


def spread_out(summed, first):
    quarters, _, columns, rows = summed.shape
    width = quarters * (columns - first)

    def kernel(in_ref, out_ref):
        for core in range(2):
            whole = jnp.concatenate(
                [in_ref[n, core, first:].astype(F32) for n in range(quarters)], axis=0
            )
            out_ref[:, core * width : (core + 1) * width] = whole.T

    return pl.pallas_call(
        kernel,
        out_shape=jax.ShapeDtypeStruct((rows, 2 * width), F32),
        in_specs=[pl.BlockSpec(memory_space=pltpu.VMEM)],
        out_specs=pl.BlockSpec(memory_space=pltpu.VMEM),
        compiler_params=pltpu.CompilerParams(vmem_limit_bytes=40 << 20),
        cost_estimate=SHORT,
        name="spread_out",
    )(summed)


def full_block(array):
    return pl.BlockSpec(array.shape, lambda i: (0, 0), pipeline_mode=pl.Buffered(1))


def row_block(rows, columns):
    return pl.BlockSpec((rows, columns), lambda i: (i, 0))


def experts_forward(b_all, gate_w, up_w, shares):
    count, features = b_all.shape
    columns = gate_w.shape[1]
    experts = shares.shape[1]
    width = columns // experts
    tile = min(256, count)

    def kernel(b_ref, gate_w_ref, up_w_ref, share_ref, gate_ref, up_ref, mid_ref):
        rows = b_ref[...]
        for expert in range(experts):
            span = slice(expert * width, (expert + 1) * width)
            gate = jnp.dot(rows, gate_w_ref[:, span], preferred_element_type=F32).astype(BF16)
            up = jnp.dot(rows, up_w_ref[:, span], preferred_element_type=F32).astype(BF16)
            gate_ref[:, span] = gate
            up_ref[:, span] = up
            gate, up = gate.astype(F32), up.astype(F32)
            share = share_ref[:, expert : expert + 1]
            mid_ref[:, span] = (gate * jax.nn.sigmoid(gate) * up * share).astype(BF16)

    return pl.pallas_call(
        kernel,
        out_shape=(jax.ShapeDtypeStruct((count, columns), BF16),) * 3,
        grid=(count // tile,),
        in_specs=[
            row_block(tile, features),
            full_block(gate_w),
            full_block(up_w),
            row_block(tile, experts),
        ],
        out_specs=(row_block(tile, columns),) * 3,
        compiler_params=pltpu.CompilerParams(vmem_limit_bytes=48 << 20),
        cost_estimate=SHORT,
        name="experts_forward",
    )(b_all, gate_w, up_w, shares)


def experts_backward(dy_all, down_w, gate_v, up_v, shares):
    count, features = dy_all.shape
    columns = gate_v.shape[1]
    experts = shares.shape[1]
    width = columns // experts
    tile = min(256, count)

    def kernel(dy_ref, down_ref, gate_ref, up_ref, share_ref, dgate_ref, dup_ref, dshare_ref):
        rows = dy_ref[...]
        sums = []
        for expert in range(experts):
            span = slice(expert * width, (expert + 1) * width)
            slope = dot(rows, down_ref[span, :], 1, 1)
            gate, up = gate_ref[:, span].astype(F32), up_ref[:, span].astype(F32)
            squashed = jax.nn.sigmoid(gate)
            active = gate * squashed
            sums.append(jnp.sum(slope * active * up, axis=1, keepdims=True))
            scaled = slope * share_ref[:, expert : expert + 1]
            dgate_ref[:, span] = (
                scaled * up * squashed * (1.0 + gate * (1.0 - squashed))
            ).astype(BF16)
            dup_ref[:, span] = (scaled * active).astype(BF16)
        dshare_ref[...] = jnp.concatenate(sums, axis=1)

    return pl.pallas_call(
        kernel,
        out_shape=(
            jax.ShapeDtypeStruct((count, columns), BF16),
            jax.ShapeDtypeStruct((count, columns), BF16),
            jax.ShapeDtypeStruct((count, experts), F32),
        ),
        grid=(count // tile,),
        in_specs=[
            row_block(tile, features),
            full_block(down_w),
            row_block(tile, columns),
            row_block(tile, columns),
            row_block(tile, experts),
        ],
        out_specs=(
            row_block(tile, columns),
            row_block(tile, columns),
            row_block(tile, experts),
        ),
        compiler_params=pltpu.CompilerParams(vmem_limit_bytes=48 << 20),
        cost_estimate=SHORT,
        name="experts_backward",
    )(dy_all, down_w, gate_v, up_v, shares)


def sum_parts(parts, shards):
    count, rows, features = parts.shape
    width = features // shards
    if width % 128:
        held = jnp.sum(parts.astype(F32), axis=0).astype(BF16)
        return jnp.transpose(held.reshape(rows, shards, width), (1, 0, 2))

    def kernel(in_ref, out_ref):
        total = in_ref[0].astype(F32)
        for n in range(1, count):
            total = total + in_ref[n].astype(F32)
        out_ref[0] = total.astype(BF16)

    return pl.pallas_call(
        kernel,
        out_shape=jax.ShapeDtypeStruct((shards, rows, width), BF16),
        grid=(shards,),
        in_specs=[pl.BlockSpec((count, rows, width), lambda i: (0, 0, i))],
        out_specs=pl.BlockSpec((1, rows, width), lambda i: (i, 0, 0)),
        cost_estimate=SHORT,
        name="sum_parts",
    )(parts)


def rms_scale(rows_in):
    return lax.rsqrt(jnp.mean(rows_in * rows_in, axis=-1, keepdims=True) + EPSILON)


def norm_back(rows_in, row_scale, gain_row, grad_normed):
    grad_gain = jnp.sum(grad_normed * rows_in * row_scale, axis=0)
    scaled = grad_normed * gain_row
    scale_cubed = row_scale * row_scale * row_scale
    grad_rows = row_scale * scaled - rows_in * scale_cubed * jnp.mean(
        scaled * rows_in, axis=-1, keepdims=True
    )
    return (grad_rows, grad_gain)


def local(
    tokens,
    cotangent,
    routes,
    lengths,
    attn_gain,
    w_query,
    w_key,
    w_value,
    w_out,
    moe_gain,
    w_router,
    w_gate,
    w_up,
    w_down,
):
    here = Place()
    core, shards, quarters = here.core, here.shards, here.quarters
    experts = w_gate.shape[0]
    features = tokens.shape[3]
    hidden_all = w_gate.shape[2]
    width_q = w_query.shape[1] // 2
    width_k = w_key.shape[1] // 2
    shard_rows = w_query.shape[0]
    rows_q = shard_rows // quarters
    hidden_part = hidden_all // shards // 2
    hidden_core = hidden_all // 2

    small = jnp.concatenate([attn_gain[:, None], moe_gain[:, None], w_router], axis=1)
    small = jnp.pad(small, ((0, 0), (0, 128 - small.shape[1])))
    own = attention_columns(core, w_query, w_key, w_value, small, w_out)
    own = own.reshape(1, quarters, rows_q, -1)
    got = here.fetch_along(own)

    length = tokens.shape[2] * shards
    my_lengths = lax.dynamic_index_in_dim(
        lax.dynamic_index_in_dim(lengths, here.batch, 0, keepdims=False),
        here.source,
        0,
        keepdims=False,
    )
    ends = jnp.cumsum(my_lengths)[:-1]
    positions = jnp.arange(length, dtype=jnp.int32)
    starts = jnp.max(
        jnp.where(ends[:, None] <= positions[None, :], ends[:, None], 0), axis=0, keepdims=True
    ).astype(jnp.int32)
    forward_ranges = block_ranges(starts, *forward_blocks(length))
    backward_ranges = block_ranges(starts, *backward_blocks(length))
    x_blocks = here.send_streams(tokens[:, 0])
    found = here.fetch_across(got)
    starts, forward_ranges, backward_ranges, *held = together(
        starts, forward_ranges, backward_ranges, *x_blocks, *found
    )
    x_blocks, found = held[:2], held[2:]
    x_own = here.join_streams(tokens[:, 0], x_blocks)
    x_other = here.swap(x_own)
    rows = x_own.shape[0]
    w_gate, routes, x_own = together(w_gate, routes, x_own)
    packed = here.gather_experts(w_gate, w_up)
    own_down = lax.dynamic_slice_in_dim(w_down, core * hidden_part, hidden_part, 1).reshape(
        experts, quarters, hidden_part // quarters, features
    )
    route_own = here.to_streams(routes[:, 0])
    own_down, route_own = together(own_down, route_own)
    got_down = here.fetch_along(own_down)
    qkv_w, small_w, out_w = here.assemble(
        own, found, [width_q + 2 * width_k, 128, features // 2]
    )
    out_w = here.ordered(out_w, here.swap(out_w), 1)
    smalls = small_w[:, : 2 + experts].astype(F32)
    gain_one = smalls[:, 0][None, :]
    gain_two = smalls[:, 1][None, :]
    router_w = small_w[:, 2 : 2 + experts]

    x_wide = x_own.astype(F32)
    scale_one = rms_scale(x_wide)
    x_all = here.ordered(x_own, x_other, 0).astype(F32)
    normed = (x_all * rms_scale(x_all) * gain_one).astype(BF16)
    route_all = jnp.concatenate([route_own, here.swap(route_own)], axis=0)
    qkv_t = dot(qkv_w, normed, 0, 1, BF16)
    qkv_t = here.chip_exchange(qkv_t, 0, 1)
    group = width_q // width_k
    heads = width_k // HEAD // here.chips
    o_heads, stats, o_mine, o_got = [], [], [], []
    for head in range(heads):
        source = qkv_t
        if head == 0:
            source, route_all = together(qkv_t, route_all)
        else:
            source, stats[-1] = together(qkv_t, stats[-1])
        o_h, stat = attend_forward(head, group, source, starts, forward_ranges)
        o_heads.append(o_h)
        stats.append(stat)
        if head == 1:
            *got_down, stats[-1] = together(*got_down, stats[-1])
            found_down = here.fetch_across(got_down)
        mine, other = here.halves(here.chip_exchange(o_h, 1, 0), 1)
        o_mine.append(mine)
        o_got.append(here.swap(other))
    o_own = here.ordered(
        here.head_order(o_mine, heads), here.head_order(o_got, heads), 0
    )
    h_own = x_wide + dot(o_own, out_w, 0, 0)

    scale_two = rms_scale(h_own)
    b_own = (h_own * scale_two * gain_two).astype(BF16)
    b_all = jnp.concatenate([b_own, here.swap(b_own)], axis=0)

    logits = dot(b_all, router_w, 1, 0)
    route_hot = (
        route_all[:, :, None] == jnp.arange(experts, dtype=jnp.int32)[None, None, :]
    ).astype(F32)
    chosen = jnp.sum(logits[:, None, :] * route_hot, axis=2)
    gate_share = jax.nn.softmax(chosen, axis=1)
    shares = jnp.sum(gate_share[:, :, None] * route_hot, axis=1)
    packed, b_all, shares = together(packed, b_all, shares)
    cotangent, packed = together(cotangent, packed)
    dy_blocks = here.send_streams(cotangent[:, 0])
    gate_w = core_columns(packed, 0, core, shards, experts)
    up_w = core_columns(packed, 1, core, shards, experts)

    gate_v, up_v, mid = experts_forward(b_all, gate_w, up_w, shares)
    *found_down, mid = together(*found_down, mid)
    *dy_blocks, mid = together(*dy_blocks, mid)
    dy_own = here.join_streams(cotangent[:, 0], dy_blocks)
    dy_all = jnp.concatenate([dy_own, here.swap(dy_own)], axis=0)
    down_w = here.assemble(own_down, found_down, [features])[0]
    y_other = dot(mid[rows:], down_w, 1, 0, BF16)
    y_got = here.swap(y_other)
    y_own = dot(mid[:rows], down_w, 1, 0)
    block_own = (h_own + y_own + y_got.astype(F32)).astype(BF16)
    block_out = here.join_homes(*here.send_homes(block_own))

    grad_down = dot(mid, dy_all, 0, 0, BF16)
    if quarters == experts:
        grad_down = grad_down.reshape(quarters, shards, hidden_part, features)
    else:
        grad_down = jnp.transpose(
            grad_down.reshape(experts, shards, hidden_part, quarters, features // quarters),
            (3, 1, 0, 2, 4),
        )
    dy_all, down_w, grad_down = together(dy_all, down_w, grad_down)
    got_grad_down = here.exchange(grad_down)
    grad_gate_v, grad_up_v, grad_share = experts_backward(dy_all, down_w, gate_v, up_v, shares)
    share_got = here.swap(grad_share[rows:])
    grad_share = grad_share[:rows] + share_got

    def expert_grad(back):
        return dot(back, b_all, 0, 0, BF16).reshape(quarters, -1, features)

    grad_gate = expert_grad(grad_gate_v)
    grad_up = expert_grad(grad_up_v)
    grad_gate_v, grad_up_v, grad_gate, grad_up, got_grad_down = together(
        grad_gate_v, grad_up_v, grad_gate, grad_up, got_grad_down
    )
    held_down = jnp.sum(got_grad_down.astype(F32), axis=0).astype(BF16)
    db_other = (
        dot(grad_gate_v[rows:], gate_w, 1, 1) + dot(grad_up_v[rows:], up_w, 1, 1)
    ).astype(BF16)
    db_got = here.swap(db_other)
    got_grad_gate = here.exchange(grad_gate)
    db_own = dot(grad_gate_v[:rows], gate_w, 1, 1) + dot(grad_up_v[:rows], up_w, 1, 1)

    hot_own, share_own = route_hot[:rows], gate_share[:rows]
    grad_gates = jnp.sum(grad_share[:, None, :] * hot_own, axis=2)
    grad_chosen = share_own * (
        grad_gates - jnp.sum(share_own * grad_gates, axis=1, keepdims=True)
    )
    grad_logits = jnp.sum(grad_chosen[:, :, None] * hot_own, axis=1).astype(BF16)
    grad_router = dot(grad_logits, b_own, 0, 0)
    db = db_own + db_got.astype(F32) + dot(grad_logits, router_w, 1, 1)
    dh, grad_gain_two = norm_back(h_own, scale_two, gain_two, db)
    dh = dh + dy_own.astype(F32)
    dattn = dh.astype(BF16)

    qkv_w_got = here.swap(qkv_w)
    do_t = dot(out_w, dattn, 1, 1, BF16)
    do_mine, do_other = here.halves(do_t, 0)
    do_t = here.ordered(do_mine, here.swap(do_other), 1)
    do_t = here.chip_exchange(do_t, 0, 1)
    grad_out = dot(dattn, o_own, 0, 1, BF16)
    out_mine, out_other = here.halves(grad_out, 0)
    grad_out = (out_mine.astype(F32) + here.swap(out_other).astype(F32)).astype(BF16)
    sum_down = here.gather(here.scatter(held_down))
    back_heads, back_rows, back_got = [], [], []
    for head in range(heads):
        g_h = do_t[head * o_heads[0].shape[0] : (head + 1) * o_heads[0].shape[0]]
        if head == 0:
            g_h, grad_out, qkv_w_got = together(g_h, grad_out, qkv_w_got)
        elif head == 1:
            g_h, block_out, got_grad_gate, grad_out, back_heads[0] = together(
                g_h, block_out, got_grad_gate, grad_out, back_heads[0]
            )
            got_grad_out = here.exchange(grad_out.reshape(quarters, -1, features))
            total_gate = here.scatter(sum_parts(got_grad_gate, shards))
        else:
            g_h, back_heads[-1] = together(g_h, back_heads[-1])
        if head == heads // 2:
            g_h, got_grad_out, grad_up, total_gate = together(
                g_h, got_grad_out, grad_up, total_gate
            )
            sum_gate = here.gather(total_gate)
            got_grad_up = here.exchange(grad_up)
            total_out = here.scatter(sum_parts(got_grad_out, shards))
        back_h = attend_backward(
            head, group, qkv_t, o_heads[head], g_h, stats[head], starts, backward_ranges
        )
        back_h = here.chip_exchange(back_h, 1, 0)
        back_heads.append(back_h)
        mine, other = here.halves(back_h, 1)
        back_rows.append(mine)
        back_got.append(here.swap(other))

    grad_qkv = jnp.stack(
        [
            dot(back_h, normed, 1, 0, BF16).reshape(here.chips, -1, features)
            for back_h in back_heads
        ],
        axis=1,
    ).reshape(quarters, -1, features)
    grad_qkv, got_grad_up = together(grad_qkv, got_grad_up)
    total_up = here.scatter(sum_parts(got_grad_up, shards))
    got_grad_qkv = here.exchange(grad_qkv)
    da = dot(here.head_order(back_rows, heads), qkv_w, 0, 1) + dot(
        here.head_order(back_got, heads), qkv_w_got, 0, 1
    )
    dx, grad_gain_one = norm_back(x_wide, scale_one, gain_one, da)
    dx_parts, dx_blocks = here.send_homes((dx + dh).astype(BF16))
    got_grad_qkv, dx_blocks[0] = together(got_grad_qkv, dx_blocks[0])

    grad_small = jnp.concatenate([grad_gain_one[None], grad_gain_two[None], grad_router], axis=0)
    grad_small = jnp.pad(grad_small, ((0, 16 - grad_small.shape[0]), (0, 0))).astype(BF16)
    grad_small = jnp.transpose(grad_small.reshape(16, shards, shard_rows), (1, 0, 2))
    held_qkv = sum_parts(got_grad_qkv, shards)
    held_qkv, total_up, total_out = together(held_qkv, total_up, total_out)
    held_qkv = jnp.concatenate([held_qkv, grad_small], axis=1)
    total = here.reduce_along(held_qkv)
    total, dx_blocks[1] = together(total, dx_blocks[1])
    input_grad = here.join_homes(dx_parts, dx_blocks)
    sum_up_out = here.gather(jnp.concatenate([total_up, total_out], axis=0))
    cut = total_up.shape[0]
    mine = jnp.stack([total] + [here.across(total, key) for key in range(1, quarters)])
    out_query, out_key, out_value, small_sum = spread_rows(
        mine, here.swap(mine), here.quarter, core, width_k // HEAD, group
    )
    if (features // 2) % 128 or (features // 2 // quarters) % 16:
        out_out = sum_up_out[:, :, cut:].astype(F32)
        out_out = jnp.transpose(out_out, (3, 1, 0, 2)).reshape(shard_rows, features)
    else:
        out_out = spread_out(sum_up_out, cut)
    if quarters == experts:
        out_down = sum_down.astype(F32).reshape(experts, 2 * hidden_part, features)
    else:
        out_down = jnp.transpose(sum_down.astype(F32), (2, 1, 3, 0, 4)).reshape(
            experts, 2 * hidden_part, features
        )
    return (
        block_out[:, None],
        input_grad[:, None],
        small_sum[0],
        out_query,
        out_key,
        out_value,
        out_out,
        small_sum[1],
        small_sum[2 : 2 + experts].T,
        spread_experts(sum_gate, experts, shards, hidden_all),
        spread_experts(sum_up_out, experts, shards, hidden_all),
        out_down,
    )


def solution(mesh):
    chips = mesh.shape["rep"] // 2
    mesh = jax.sharding.Mesh(
        mesh.devices.reshape(chips, 2, mesh.shape["shard"]), ("chip", "core", "shard")
    )
    in_specs = (
        P(None, PLANE, "shard", None),
        P(None, PLANE, "shard", None),
        P(None, PLANE, "shard", None),
        P(),
        P("shard"),
        P("shard", None),
        P("shard", None),
        P("shard", None),
        P("shard", None),
        P("shard"),
        P("shard", None),
        P(None, "shard", None),
        P(None, "shard", None),
        P(None, "shard", None),
    )
    out_specs = (
        P(None, PLANE, "shard", None),
        P(None, PLANE, "shard", None),
        P("shard"),
        P("shard", None),
        P("shard", None),
        P("shard", None),
        P("shard", None),
        P("shard"),
        P("shard", None),
        P(None, "shard", None),
        P(None, "shard", None),
        P(None, "shard", None),
    )
    return jax.shard_map(local, mesh=mesh, in_specs=in_specs, out_specs=out_specs, check_vma=False)
```

```python
import functools
import math

import jax
import jax.numpy as jnp
from jax import lax
from jax.experimental import pallas as pl
from jax.experimental.pallas import tpu as pltpu
from jax.sharding import PartitionSpec as P

HEAD = 64
EPSILON = 1e-05
NEGATIVE = -1e30
F32 = jnp.float32
BF16 = jnp.bfloat16
LOG2_SCALE = HEAD ** (-0.5) * math.log2(math.e)
SCALE = HEAD ** (-0.5)
PLANE = ("chip", "core")
BOTH = ("chip", "core", "shard")


SHORT = pl.CostEstimate(flops=1 << 20, transcendentals=0, bytes_accessed=1 << 20)


def together(*arrays):
    return lax.optimization_barrier(arrays)


def dot(left, right, left_dim, right_dim, kind=F32):
    return lax.dot_general(
        left, right, (((left_dim,), (right_dim,)), ((), ())), preferred_element_type=F32
    ).astype(kind)


def forward_blocks(length):
    return min(512, length), min(512, length)


def backward_blocks(length):
    return min(256, length), min(256, length)


def visible_mask(index, width, first_key, first_query, starts):
    rows = first_key + lax.broadcasted_iota(jnp.int32, (width, starts.shape[1]), 0)
    columns = first_query + lax.broadcasted_iota(jnp.int32, (1, starts.shape[1]), 1)
    return (rows >= starts) & (rows <= columns)


def side_by_side(block, group):
    return jnp.concatenate([block[g * HEAD : (g + 1) * HEAD, :] for g in range(group)], axis=1)


def three_loops(ranges, place, step, carry):
    low, full_low, full_high, high = (ranges[place, n] for n in range(4))
    carry = lax.fori_loop(low, full_low, functools.partial(step, True), carry)
    carry = lax.fori_loop(full_low, full_high, functools.partial(step, False), carry)
    return lax.fori_loop(full_high, high, functools.partial(step, True), carry)


def forward_kernel(ranges, *refs, group, wide):
    q_refs, (k_ref, v_ref, starts_ref, o_ref, stat_ref, k_rows) = refs[:group], refs[group:]
    place = pl.program_id(1)
    q_width = q_refs[0].shape[1]

    @pl.when(place == 0)
    def _():
        k_rows[...] = k_ref[...].T

    queries = jnp.concatenate([ref[...] for ref in q_refs], axis=1)
    starts = starts_ref[...]

    def step(masked, index, carry):
        high, total, mixed = carry
        first = pl.multiple_of(index * wide, wide)
        scores = (
            jnp.dot(k_rows[pl.ds(first, wide), :], queries, preferred_element_type=F32)
            * LOG2_SCALE
        )
        if masked:
            seen = visible_mask(index, wide, first, place * q_width, starts)
            scores = jnp.where(jnp.concatenate([seen] * group, axis=1), scores, NEGATIVE)
        new_high = jnp.maximum(high, jnp.max(scores, axis=0, keepdims=True))
        weights = jnp.exp2(scores - new_high)
        fade = jnp.exp2(high - new_high)
        total = total * fade + jnp.sum(weights, axis=0, keepdims=True)
        mixed = mixed * fade + jnp.dot(
            v_ref[:, pl.ds(first, wide)], weights.astype(BF16), preferred_element_type=F32
        )
        return new_high, total, mixed

    columns = group * q_width
    high, total, mixed = three_loops(
        ranges,
        place,
        step,
        (
            jnp.full((1, columns), NEGATIVE, F32),
            jnp.zeros((1, columns), F32),
            jnp.zeros((HEAD, columns), F32),
        ),
    )
    mixed = (mixed / total).astype(BF16)
    stat = high + jnp.log2(total)
    for g in range(group):
        span = slice(g * q_width, (g + 1) * q_width)
        o_ref[g * HEAD : (g + 1) * HEAD, :] = mixed[:, span]
        stat_ref[0, g : g + 1, :] = stat[:, span]


def backward_kernel(ranges, *refs, group, wide):
    q_refs, (k_ref, v_ref, o_ref, g_ref, stat_ref, starts_ref), (
        back_ref, k_rows, v_rows, dk_sum, dv_sum,
    ) = refs[:group], refs[group : group + 6], refs[group + 6 :]
    place = pl.program_id(1)
    q_width = q_refs[0].shape[1]

    @pl.when(place == 0)
    def _():
        k_rows[...] = k_ref[...].T
        v_rows[...] = v_ref[...].T
        dk_sum[...] = jnp.zeros_like(dk_sum)
        dv_sum[...] = jnp.zeros_like(dv_sum)

    queries = jnp.concatenate([ref[...] for ref in q_refs], axis=1)
    grads = side_by_side(g_ref[...], group)
    outs = side_by_side(o_ref[...], group)
    inner = jnp.sum(grads.astype(F32) * outs.astype(F32), axis=0, keepdims=True)
    stat = jnp.concatenate([stat_ref[0, g : g + 1, :] for g in range(group)], axis=1)
    starts = starts_ref[...]

    def step(masked, index, dq):
        first = pl.multiple_of(index * wide, wide)
        span = pl.ds(first, wide)
        scores = jnp.dot(k_rows[span, :], queries, preferred_element_type=F32) * LOG2_SCALE
        chances = jnp.exp2(scores - stat)
        if masked:
            seen = visible_mask(index, wide, first, place * q_width, starts)
            chances = jnp.where(jnp.concatenate([seen] * group, axis=1), chances, 0.0)
        slopes = jnp.dot(v_rows[span, :], grads, preferred_element_type=F32)
        pull = (chances * (slopes - inner)).astype(BF16)
        dv_sum[:, span] += dot(grads, chances.astype(BF16), 1, 1)
        dk_sum[:, span] += dot(queries, pull, 1, 1)
        return dq + jnp.dot(k_ref[:, span], pull, preferred_element_type=F32)

    dq = three_loops(ranges, place, step, jnp.zeros((HEAD, group * q_width), F32))
    dq = (dq * SCALE).astype(BF16)
    here = pl.ds(pl.multiple_of(place * q_width, q_width), q_width)
    for g in range(group):
        back_ref[g * HEAD : (g + 1) * HEAD, here] = dq[:, g * q_width : (g + 1) * q_width]

    @pl.when(place == pl.num_programs(1) - 1)
    def _():
        back_ref[group * HEAD : (group + 1) * HEAD, :] = (dk_sum[...] * SCALE).astype(BF16)
        back_ref[(group + 1) * HEAD :, :] = dv_sum[...].astype(BF16)


def block_ranges(starts, q_width, wide):
    length = starts.shape[1]
    count = length // q_width
    first_query = jnp.arange(count, dtype=jnp.int32) * q_width
    low = starts[0, ::q_width] // wide
    full_low = (starts[0, q_width - 1 :: q_width] + wide - 1) // wide
    full_high = (first_query + 1) // wide
    full_high = first_query // wide
    high = (first_query + q_width) // wide
    full_low = jnp.clip(full_low, low, jnp.maximum(full_high, low))
    full_high = jnp.maximum(full_high, full_low)
    return jnp.stack([low, full_low, full_high, high], axis=1)


def attention_specs(head, group, length, q_width):
    first = head * (group + 2)
    queries = [
        pl.BlockSpec((HEAD, q_width), lambda h, i, r, g=g: (first + g, i)) for g in range(group)
    ]
    keys = pl.BlockSpec((HEAD, length), lambda h, i, r: (first + group, 0))
    values = pl.BlockSpec((HEAD, length), lambda h, i, r: (first + group + 1, 0))
    per_query = pl.BlockSpec((group * HEAD, q_width), lambda h, i, r: (0, i))
    stat = pl.BlockSpec((1, group, q_width), lambda h, i, r: (0, 0, i))
    starts = pl.BlockSpec((1, q_width), lambda h, i, r: (0, i))
    return [*queries, keys, values], per_query, stat, starts


def attend_forward(head, group, qkv_t, starts, ranges):
    length = qkv_t.shape[1]
    q_width, wide = forward_blocks(length)
    rows, per_query, stat, start_spec = attention_specs(head, group, length, q_width)
    return pl.pallas_call(
        functools.partial(forward_kernel, group=group, wide=wide),
        out_shape=(
            jax.ShapeDtypeStruct((group * HEAD, length), BF16),
            jax.ShapeDtypeStruct((1, group, length), F32),
        ),
        grid_spec=pltpu.PrefetchScalarGridSpec(
            num_scalar_prefetch=1,
            grid=(1, length // q_width),
            in_specs=[*rows, start_spec],
            out_specs=(per_query, stat),
            scratch_shapes=[pltpu.VMEM((length, HEAD), BF16)],
        ),
        compiler_params=pltpu.CompilerParams(
            dimension_semantics=("arbitrary", "arbitrary"), vmem_limit_bytes=40 << 20
        ),
        cost_estimate=SHORT,
        name="attend_forward",
    )(ranges, *[qkv_t] * (group + 2), starts)


def attend_backward(head, group, qkv_t, o_h, g_h, stat_h, starts, ranges):
    length = qkv_t.shape[1]
    q_width, wide = backward_blocks(length)
    rows, per_query, stat, start_spec = attention_specs(head, group, length, q_width)
    count = (group + 2) * HEAD
    return pl.pallas_call(
        functools.partial(backward_kernel, group=group, wide=wide),
        out_shape=jax.ShapeDtypeStruct((count, length), BF16),
        grid_spec=pltpu.PrefetchScalarGridSpec(
            num_scalar_prefetch=1,
            grid=(1, length // q_width),
            in_specs=[*rows, per_query, per_query, stat, start_spec],
            out_specs=pl.BlockSpec((count, length), lambda h, i, r: (0, 0)),
            scratch_shapes=[
                pltpu.VMEM((length, HEAD), BF16),
                pltpu.VMEM((length, HEAD), BF16),
                pltpu.VMEM((HEAD, length), F32),
                pltpu.VMEM((HEAD, length), F32),
            ],
        ),
        compiler_params=pltpu.CompilerParams(
            dimension_semantics=("arbitrary", "arbitrary"), vmem_limit_bytes=40 << 20
        ),
        cost_estimate=SHORT,
        name="attend_backward",
    )(ranges, *[qkv_t] * (group + 2), o_h, g_h, stat_h, starts)


class Place:
    def __init__(self):
        self.quarters = lax.axis_size("chip")
        self.reps = 2 * self.quarters
        self.shards = lax.axis_size("shard")
        self.chips = self.shards // 4
        self.core = lax.axis_index("core")
        self.quarter = lax.axis_index("chip")
        self.shard = lax.axis_index("shard")
        self.stream = self.shard // self.chips
        self.batch = self.stream // 2
        self.source = self.quarter * 2 + self.stream % 2
        self.chip = self.shard % self.chips

    def across(self, array, key):
        return lax.ppermute(array, "chip", [(i, i ^ key) for i in range(self.quarters)])

    def swap(self, array):
        return lax.ppermute(array, "core", [(0, 1), (1, 0)])

    def moves(self, turn, home):
        pairs = []
        for quarter in range(self.quarters):
            for core in range(2):
                for shard in range(self.shards):
                    batch = turn ^ (shard & 1)
                    member = shard // 2
                    stream = 2 * batch + core
                    start = (quarter * 2 + core) * self.shards + shard
                    end = (
                        (quarter * 2 + member % 2) * self.shards
                        + stream * self.chips
                        + member // 2
                    )
                    if start != end:
                        pairs.append((end, start) if home else (start, end))
        return pairs

    def stays(self, turn):
        batch = turn ^ (self.shard & 1)
        member = self.shard // 2
        end = (2 * batch + self.core) * self.chips + member // 2
        return (member % 2 == self.core) & (end == self.shard)

    def leaving(self, array):
        odd = self.shard % 2 == 1
        return [jnp.where(odd, array[1 - turn], array[turn]) for turn in range(2)]

    def send_streams(self, array):
        return [
            lax.ppermute(part, BOTH, self.moves(turn, False))
            for turn, part in enumerate(self.leaving(array))
        ]

    def join_streams(self, array, got):
        got = [
            jnp.where(self.stays(turn), part, got[turn])
            for turn, part in enumerate(self.leaving(array))
        ]
        swapped = self.batch == 1
        return jnp.concatenate(
            [jnp.where(swapped, got[1], got[0]), jnp.where(swapped, got[0], got[1])], axis=0
        )

    def to_streams(self, array):
        return self.join_streams(array, self.send_streams(array))

    def send_homes(self, array):
        half = array.shape[0] // 2
        swapped = self.batch == 1
        parts = [array[:half], array[half:]]
        parts = [jnp.where(swapped, parts[1 - turn], parts[turn]) for turn in range(2)]
        got = [lax.ppermute(part, BOTH, self.moves(turn, True)) for turn, part in enumerate(parts)]
        return parts, got

    def join_homes(self, parts, got):
        got = [jnp.where(self.stays(turn), parts[turn], got[turn]) for turn in range(2)]
        odd = self.shard % 2 == 1
        return jnp.stack([jnp.where(odd, got[1], got[0]), jnp.where(odd, got[0], got[1])])

    def ordered(self, mine, other, axis):
        return jnp.where(
            self.core == 0,
            jnp.concatenate([mine, other], axis=axis),
            jnp.concatenate([other, mine], axis=axis),
        )

    def halves(self, array, axis):
        size = array.shape[axis] // 2
        mine = lax.dynamic_slice_in_dim(array, self.core * size, size, axis)
        other = lax.dynamic_slice_in_dim(array, (1 - self.core) * size, size, axis)
        return mine, other

    def head_order(self, pieces, heads):
        if self.chips == 1:
            return jnp.concatenate(pieces, axis=0)
        stacked = jnp.stack([p.reshape(self.chips, -1, p.shape[1]) for p in pieces], axis=1)
        return stacked.reshape(-1, pieces[0].shape[1])

    def chip_exchange(self, array, split, join):
        if self.chips == 1:
            return array
        size = array.shape[split] // self.chips
        width = array.shape[join]
        shape = list(array.shape)
        shape[split] = size
        shape[join] = width * self.chips
        result = jnp.zeros(shape, array.dtype)
        for step in range(self.chips):
            other = self.chip ^ step
            piece = lax.dynamic_slice_in_dim(array, other * size, size, split)
            if step:
                piece = lax.ppermute(
                    piece, "shard", [(i, i ^ step) for i in range(self.shards)]
                )
            result = lax.dynamic_update_slice_in_dim(result, piece, other * width, join)
        return result

    def along(self, array, step):
        return lax.ppermute(
            array, "shard", [(i, (i + step) % self.shards) for i in range(self.shards)]
        )

    def fetch_along(self, own):
        piece = lax.dynamic_index_in_dim(own, self.quarter, 1, keepdims=False)
        return [self.along(piece, step) for step in range(1, self.shards)]

    def fetch_across(self, got):
        got = jnp.stack(got)
        return [got] + [self.across(got, key) for key in range(1, self.quarters)]

    def assemble(self, own, found, widths):
        parts, quarters, rows, _ = own.shape
        shards = self.shards
        places = jnp.stack([self.shard, self.quarter]).astype(jnp.int32)
        edges = [sum(widths[:n]) for n in range(len(widths) + 1)]

        def kernel(places_ref, own_ref, *refs):
            found_refs, out_refs, sem = refs[:quarters], refs[quarters:-1], refs[-1]
            shard, quarter = places_ref[0], places_ref[1]
            copies = []
            for n, out_ref in enumerate(out_refs):
                span = pl.ds(edges[n], widths[n])
                for part in range(parts):
                    copies.append((own_ref.at[part, :, :, span], out_ref.at[part, shard]))
                    for key in range(quarters):
                        for step in range(1, shards):
                            where = (shard - step + shards) % shards
                            copies.append(
                                (
                                    found_refs[key].at[step - 1, part, :, span],
                                    out_ref.at[part, where, quarter ^ key],
                                )
                            )
            copies = [
                pltpu.make_async_copy(source, end, sem.at[n])
                for n, (source, end) in enumerate(copies)
            ]
            for copy in copies:
                copy.start()
            for copy in copies:
                copy.wait()

        whole = pl.pallas_call(
            kernel,
            out_shape=tuple(
                jax.ShapeDtypeStruct((parts, shards, quarters, rows, width), own.dtype)
                for width in widths
            ),
            in_specs=[pl.BlockSpec(memory_space=pltpu.SMEM)]
            + [pl.BlockSpec(memory_space=pl.ANY)] * (quarters + 1),
            out_specs=tuple(pl.BlockSpec(memory_space=pltpu.VMEM) for _ in widths),
            scratch_shapes=[
                pltpu.SemaphoreType.DMA((len(widths) * parts * (1 + quarters * (shards - 1)),))
            ],
            compiler_params=pltpu.CompilerParams(vmem_limit_bytes=24 << 20),
            cost_estimate=SHORT,
            name="assemble",
        )(places, own, *found)
        return [part.reshape(parts * shards * quarters * rows, -1) for part in whole]

    def gather_experts(self, w_gate, w_up):
        which = self.quarter * 2 + self.core

        def part(weight):
            size = weight.shape[1] // self.reps
            piece = lax.dynamic_slice_in_dim(weight, which * size, size, 1)
            return piece.reshape(-1, weight.shape[2])

        piece = jnp.concatenate([part(w_gate), part(w_up)], axis=0)
        return lax.all_gather(piece, ("shard", "chip", "core"), axis=0, tiled=False)

    def exchange(self, grad):
        return lax.all_to_all(grad, "chip", 0, 0, tiled=True)

    def reduce_along(self, held):
        total = lax.dynamic_index_in_dim(held, self.shard, 0, keepdims=False).astype(F32)
        for step in range(1, self.shards):
            give = lax.dynamic_index_in_dim(
                held, (self.shard + step) % self.shards, 0, keepdims=False
            )
            total = total + self.along(give, step).astype(F32)
        return total.astype(BF16)

    def scatter(self, held):
        return lax.psum_scatter(held, "shard", scatter_dimension=0, tiled=False)

    def gather(self, total):
        whole = lax.all_gather(total, PLANE, axis=0, tiled=False)
        return whole.reshape(self.quarters, 2, *total.shape)


def core_columns(packed, which, core, shards, experts):
    pieces, _, hidden = packed.shape
    rows = packed.shape[1] // 2
    part = hidden // shards // 2
    small = rows // experts
    if part % 128 or small % 16:
        parts = packed[:, which * rows : (which + 1) * rows]
        parts = parts.reshape(pieces, experts, small, shards, 2, part)
        parts = lax.dynamic_index_in_dim(parts, core, 4, keepdims=False)
        return jnp.transpose(parts, (0, 2, 1, 3, 4)).reshape(pieces * small, -1)
    group = 4

    def kernel(core_ref, *refs):
        out_ref = refs[-1]
        for shard in range(shards):
            for piece in range(group):
                for expert in range(experts):
                    column = (expert * shards + shard) * part
                    out_ref[piece * small : (piece + 1) * small, column : column + part] = refs[
                        shard
                    ][piece, expert * small : (expert + 1) * small, :]

    def columns(shard):
        return pl.BlockSpec((group, rows, part), lambda i, c: (i, which, 2 * shard + c[0]))

    return pl.pallas_call(
        kernel,
        out_shape=jax.ShapeDtypeStruct((pieces * small, experts * hidden // 2), packed.dtype),
        grid_spec=pltpu.PrefetchScalarGridSpec(
            num_scalar_prefetch=1,
            grid=(pieces // group,),
            in_specs=[columns(shard) for shard in range(shards)],
            out_specs=pl.BlockSpec(
                (group * small, experts * hidden // 2), lambda i, c: (i, 0)
            ),
        ),
        cost_estimate=SHORT,
        name="core_columns",
    )(core.astype(jnp.int32)[None], *([packed] * shards))


def spread_experts(summed, experts, shards, hidden):
    quarters, _, _, rows = summed.shape
    columns = experts * hidden // 2 // quarters
    part = hidden // shards // 2
    if part % 128 or quarters != experts:
        piece = jnp.transpose(summed[:, :, :columns].astype(F32), (1, 0, 2, 3))
        piece = piece.reshape(2, experts, shards, part, rows)
        return jnp.transpose(piece, (1, 4, 2, 0, 3)).reshape(experts, rows, hidden)

    def kernel(in_ref, out_ref):
        for core in range(2):
            turned = in_ref[0, core].astype(F32).T
            for shard in range(shards):
                first = (2 * shard + core) * part
                out_ref[0, :, first : first + part] = turned[:, shard * part : (shard + 1) * part]

    return pl.pallas_call(
        kernel,
        out_shape=jax.ShapeDtypeStruct((experts, rows, hidden), F32),
        grid=(experts,),
        in_specs=[pl.BlockSpec((1, 2, columns, rows), lambda e: (e, 0, 0, 0))],
        out_specs=pl.BlockSpec((1, rows, hidden), lambda e: (e, 0, 0)),
        cost_estimate=SHORT,
        name="spread_experts",
    )(summed)


def attention_columns(core, w_query, w_key, w_value, small, w_out):
    rows = w_query.shape[0]
    width_q, width_k, width_out = (w.shape[1] // 2 for w in (w_query, w_key, w_out))
    heads = width_k // HEAD
    part = width_q // heads
    total = width_q + 2 * width_k + small.shape[1] + width_out

    def kernel(core_ref, q_ref, k_ref, v_ref, small_ref, o_ref, out_ref):
        def half(ref, width):
            return ref[:, pl.ds(pl.multiple_of(core_ref[0] * width, 128), width)]

        query, key, value = half(q_ref, width_q), half(k_ref, width_k), half(v_ref, width_k)
        pieces = []
        for head in range(heads):
            span = slice(head * HEAD, (head + 1) * HEAD)
            pieces += [query[:, head * part : (head + 1) * part], key[:, span], value[:, span]]
        first = width_q + 2 * width_k
        out_ref[:, :first] = jnp.concatenate(pieces, axis=1)
        out_ref[:, first : first + small.shape[1]] = small_ref[...]
        out_ref[:, first + small.shape[1] :] = half(o_ref, width_out)

    return pl.pallas_call(
        kernel,
        out_shape=jax.ShapeDtypeStruct((rows, total), w_query.dtype),
        in_specs=[pl.BlockSpec(memory_space=pltpu.SMEM)]
        + [pl.BlockSpec(memory_space=pltpu.VMEM)] * 5,
        out_specs=pl.BlockSpec(memory_space=pltpu.VMEM),
        cost_estimate=SHORT,
        name="attention_columns",
    )(core.astype(jnp.int32)[None], w_query, w_key, w_value, small, w_out)


def spread_rows(mine, other, quarter, core, heads, group):
    quarters, columns, rows = mine.shape
    each = (group + 2) * HEAD
    own = heads * each // quarters
    rest = columns - own
    widths = [heads * group * HEAD, heads * HEAD, heads * HEAD]
    edges = [0, group * HEAD, (group + 1) * HEAD, each]
    places = jnp.stack([quarter, core]).astype(jnp.int32)

    def kernel(places_ref, mine_ref, other_ref, *out_refs):
        quarter, core = places_ref[0], places_ref[1]
        smalls = jnp.zeros((rest, rows), F32)
        for side, ref in enumerate((mine_ref, other_ref)):
            at = core if side == 0 else 1 - core
            whole = jnp.concatenate(
                [ref[n ^ quarter, :own].astype(F32) for n in range(quarters)], axis=0
            )
            for n in range(quarters):
                smalls = smalls + ref[n, own:].astype(F32)
            for n, (width, out_ref) in enumerate(zip(widths, out_refs)):
                span = pl.ds(pl.multiple_of(at * width, 128), width)
                picked = [
                    whole[head * each + edges[n] : head * each + edges[n + 1]]
                    for head in range(heads)
                ]
                out_ref[:, span] = jnp.concatenate(picked, axis=0).T
        out_refs[-1][...] = smalls

    shapes = [jax.ShapeDtypeStruct((rows, 2 * width), F32) for width in widths]
    shapes.append(jax.ShapeDtypeStruct((rest, rows), F32))
    return pl.pallas_call(
        kernel,
        out_shape=tuple(shapes),
        in_specs=[
            pl.BlockSpec(memory_space=pltpu.SMEM),
            pl.BlockSpec(memory_space=pltpu.VMEM),
            pl.BlockSpec(memory_space=pltpu.VMEM),
        ],
        out_specs=tuple(pl.BlockSpec(memory_space=pltpu.VMEM) for _ in shapes),
        compiler_params=pltpu.CompilerParams(vmem_limit_bytes=40 << 20),
        cost_estimate=SHORT,
        name="spread_rows",
    )(places, mine, other)


def spread_out(summed, first):
    quarters, _, columns, rows = summed.shape
    width = quarters * (columns - first)

    def kernel(in_ref, out_ref):
        for core in range(2):
            whole = jnp.concatenate(
                [in_ref[n, core, first:].astype(F32) for n in range(quarters)], axis=0
            )
            out_ref[:, core * width : (core + 1) * width] = whole.T

    return pl.pallas_call(
        kernel,
        out_shape=jax.ShapeDtypeStruct((rows, 2 * width), F32),
        in_specs=[pl.BlockSpec(memory_space=pltpu.VMEM)],
        out_specs=pl.BlockSpec(memory_space=pltpu.VMEM),
        compiler_params=pltpu.CompilerParams(vmem_limit_bytes=40 << 20),
        cost_estimate=SHORT,
        name="spread_out",
    )(summed)


def full_block(array):
    return pl.BlockSpec(array.shape, lambda i: (0, 0), pipeline_mode=pl.Buffered(1))


def row_block(rows, columns):
    return pl.BlockSpec((rows, columns), lambda i: (i, 0))


def experts_forward(b_all, gate_w, up_w, shares):
    count, features = b_all.shape
    columns = gate_w.shape[1]
    experts = shares.shape[1]
    width = columns // experts
    tile = min(256, count)

    def kernel(b_ref, gate_w_ref, up_w_ref, share_ref, gate_ref, up_ref, mid_ref):
        rows = b_ref[...]
        for expert in range(experts):
            span = slice(expert * width, (expert + 1) * width)
            gate = jnp.dot(rows, gate_w_ref[:, span], preferred_element_type=F32).astype(BF16)
            up = jnp.dot(rows, up_w_ref[:, span], preferred_element_type=F32).astype(BF16)
            gate_ref[:, span] = gate
            up_ref[:, span] = up
            gate, up = gate.astype(F32), up.astype(F32)
            share = share_ref[:, expert : expert + 1]
            mid_ref[:, span] = (gate * jax.nn.sigmoid(gate) * up * share).astype(BF16)

    return pl.pallas_call(
        kernel,
        out_shape=(jax.ShapeDtypeStruct((count, columns), BF16),) * 3,
        grid=(count // tile,),
        in_specs=[
            row_block(tile, features),
            full_block(gate_w),
            full_block(up_w),
            row_block(tile, experts),
        ],
        out_specs=(row_block(tile, columns),) * 3,
        compiler_params=pltpu.CompilerParams(vmem_limit_bytes=48 << 20),
        cost_estimate=SHORT,
        name="experts_forward",
    )(b_all, gate_w, up_w, shares)


def experts_backward(dy_all, down_w, gate_v, up_v, shares):
    count, features = dy_all.shape
    columns = gate_v.shape[1]
    experts = shares.shape[1]
    width = columns // experts
    tile = min(256, count)

    def kernel(dy_ref, down_ref, gate_ref, up_ref, share_ref, dgate_ref, dup_ref, dshare_ref):
        rows = dy_ref[...]
        sums = []
        for expert in range(experts):
            span = slice(expert * width, (expert + 1) * width)
            slope = dot(rows, down_ref[span, :], 1, 1)
            gate, up = gate_ref[:, span].astype(F32), up_ref[:, span].astype(F32)
            squashed = jax.nn.sigmoid(gate)
            active = gate * squashed
            sums.append(jnp.sum(slope * active * up, axis=1, keepdims=True))
            scaled = slope * share_ref[:, expert : expert + 1]
            dgate_ref[:, span] = (
                scaled * up * squashed * (1.0 + gate * (1.0 - squashed))
            ).astype(BF16)
            dup_ref[:, span] = (scaled * active).astype(BF16)
        dshare_ref[...] = jnp.concatenate(sums, axis=1)

    return pl.pallas_call(
        kernel,
        out_shape=(
            jax.ShapeDtypeStruct((count, columns), BF16),
            jax.ShapeDtypeStruct((count, columns), BF16),
            jax.ShapeDtypeStruct((count, experts), F32),
        ),
        grid=(count // tile,),
        in_specs=[
            row_block(tile, features),
            full_block(down_w),
            row_block(tile, columns),
            row_block(tile, columns),
            row_block(tile, experts),
        ],
        out_specs=(
            row_block(tile, columns),
            row_block(tile, columns),
            row_block(tile, experts),
        ),
        compiler_params=pltpu.CompilerParams(vmem_limit_bytes=48 << 20),
        cost_estimate=SHORT,
        name="experts_backward",
    )(dy_all, down_w, gate_v, up_v, shares)


def sum_parts(parts, shards):
    count, rows, features = parts.shape
    width = features // shards
    if width % 128:
        held = jnp.sum(parts.astype(F32), axis=0).astype(BF16)
        return jnp.transpose(held.reshape(rows, shards, width), (1, 0, 2))

    def kernel(in_ref, out_ref):
        total = in_ref[0].astype(F32)
        for n in range(1, count):
            total = total + in_ref[n].astype(F32)
        out_ref[0] = total.astype(BF16)

    return pl.pallas_call(
        kernel,
        out_shape=jax.ShapeDtypeStruct((shards, rows, width), BF16),
        grid=(shards,),
        in_specs=[pl.BlockSpec((count, rows, width), lambda i: (0, 0, i))],
        out_specs=pl.BlockSpec((1, rows, width), lambda i: (i, 0, 0)),
        cost_estimate=SHORT,
        name="sum_parts",
    )(parts)


def rms_scale(rows_in):
    return lax.rsqrt(jnp.mean(rows_in * rows_in, axis=-1, keepdims=True) + EPSILON)


def norm_back(rows_in, row_scale, gain_row, grad_normed):
    grad_gain = jnp.sum(grad_normed * rows_in * row_scale, axis=0)
    scaled = grad_normed * gain_row
    scale_cubed = row_scale * row_scale * row_scale
    grad_rows = row_scale * scaled - rows_in * scale_cubed * jnp.mean(
        scaled * rows_in, axis=-1, keepdims=True
    )
    return (grad_rows, grad_gain)


def local(
    tokens,
    cotangent,
    routes,
    lengths,
    attn_gain,
    w_query,
    w_key,
    w_value,
    w_out,
    moe_gain,
    w_router,
    w_gate,
    w_up,
    w_down,
):
    here = Place()
    core, shards, quarters = here.core, here.shards, here.quarters
    experts = w_gate.shape[0]
    features = tokens.shape[3]
    hidden_all = w_gate.shape[2]
    width_q = w_query.shape[1] // 2
    width_k = w_key.shape[1] // 2
    shard_rows = w_query.shape[0]
    rows_q = shard_rows // quarters
    hidden_part = hidden_all // shards // 2
    hidden_core = hidden_all // 2

    small = jnp.concatenate([attn_gain[:, None], moe_gain[:, None], w_router], axis=1)
    small = jnp.pad(small, ((0, 0), (0, 128 - small.shape[1])))
    own = attention_columns(core, w_query, w_key, w_value, small, w_out)
    own = own.reshape(1, quarters, rows_q, -1)
    got = here.fetch_along(own)

    length = tokens.shape[2] * shards
    my_lengths = lax.dynamic_index_in_dim(
        lax.dynamic_index_in_dim(lengths, here.batch, 0, keepdims=False),
        here.source,
        0,
        keepdims=False,
    )
    ends = jnp.cumsum(my_lengths)[:-1]
    positions = jnp.arange(length, dtype=jnp.int32)
    starts = jnp.max(
        jnp.where(ends[:, None] <= positions[None, :], ends[:, None], 0), axis=0, keepdims=True
    ).astype(jnp.int32)
    forward_ranges = block_ranges(starts, *forward_blocks(length))
    backward_ranges = block_ranges(starts, *backward_blocks(length))
    x_blocks = here.send_streams(tokens[:, 0])
    found = here.fetch_across(got)
    starts, forward_ranges, backward_ranges, *held = together(
        starts, forward_ranges, backward_ranges, *x_blocks, *found
    )
    x_blocks, found = held[:2], held[2:]
    x_own = here.join_streams(tokens[:, 0], x_blocks)
    x_other = here.swap(x_own)
    rows = x_own.shape[0]
    w_gate, routes, x_own = together(w_gate, routes, x_own)
    packed = here.gather_experts(w_gate, w_up)
    own_down = lax.dynamic_slice_in_dim(w_down, core * hidden_part, hidden_part, 1).reshape(
        experts, quarters, hidden_part // quarters, features
    )
    route_own = here.to_streams(routes[:, 0])
    own_down, route_own = together(own_down, route_own)
    got_down = here.fetch_along(own_down)
    qkv_w, small_w, out_w = here.assemble(
        own, found, [width_q + 2 * width_k, 128, features // 2]
    )
    out_w = here.ordered(out_w, here.swap(out_w), 1)
    smalls = small_w[:, : 2 + experts].astype(F32)
    gain_one = smalls[:, 0][None, :]
    gain_two = smalls[:, 1][None, :]
    router_w = small_w[:, 2 : 2 + experts]

    x_wide = x_own.astype(F32)
    scale_one = rms_scale(x_wide)
    x_all = here.ordered(x_own, x_other, 0).astype(F32)
    normed = (x_all * rms_scale(x_all) * gain_one).astype(BF16)
    route_all = jnp.concatenate([route_own, here.swap(route_own)], axis=0)
    qkv_t = dot(qkv_w, normed, 0, 1, BF16)
    qkv_t = here.chip_exchange(qkv_t, 0, 1)
    group = width_q // width_k
    heads = width_k // HEAD // here.chips
    o_heads, stats, o_mine, o_got = [], [], [], []
    for head in range(heads):
        source = qkv_t
        if head == 0:
            source, route_all = together(qkv_t, route_all)
        else:
            source, stats[-1] = together(qkv_t, stats[-1])
        o_h, stat = attend_forward(head, group, source, starts, forward_ranges)
        o_heads.append(o_h)
        stats.append(stat)
        if head == 1:
            *got_down, stats[-1] = together(*got_down, stats[-1])
            found_down = here.fetch_across(got_down)
        mine, other = here.halves(here.chip_exchange(o_h, 1, 0), 1)
        o_mine.append(mine)
        o_got.append(here.swap(other))
    o_own = here.ordered(
        here.head_order(o_mine, heads), here.head_order(o_got, heads), 0
    )
    h_own = x_wide + dot(o_own, out_w, 0, 0)

    scale_two = rms_scale(h_own)
    b_own = (h_own * scale_two * gain_two).astype(BF16)
    b_all = jnp.concatenate([b_own, here.swap(b_own)], axis=0)

    logits = dot(b_all, router_w, 1, 0)
    route_hot = (
        route_all[:, :, None] == jnp.arange(experts, dtype=jnp.int32)[None, None, :]
    ).astype(F32)
    chosen = jnp.sum(logits[:, None, :] * route_hot, axis=2)
    gate_share = jax.nn.softmax(chosen, axis=1)
    shares = jnp.sum(gate_share[:, :, None] * route_hot, axis=1)
    dy_parts = here.leaving(cotangent[:, 0])
    packed, b_all, shares, *dy_parts = together(packed, b_all, shares, *dy_parts)
    dy_blocks = [
        lax.ppermute(part, BOTH, here.moves(turn, False)) for turn, part in enumerate(dy_parts)
    ]
    gate_w = core_columns(packed, 0, core, shards, experts)
    up_w = core_columns(packed, 1, core, shards, experts)

    gate_v, up_v, mid = experts_forward(b_all, gate_w, up_w, shares)
    *found_down, mid = together(*found_down, mid)
    *dy_blocks, mid = together(*dy_blocks, mid)
    dy_own = here.join_streams(cotangent[:, 0], dy_blocks)
    dy_all = jnp.concatenate([dy_own, here.swap(dy_own)], axis=0)
    down_w = here.assemble(own_down, found_down, [features])[0]
    y_other = dot(mid[rows:], down_w, 1, 0, BF16)
    y_got = here.swap(y_other)
    y_own = dot(mid[:rows], down_w, 1, 0)
    block_own = (h_own + y_own + y_got.astype(F32)).astype(BF16)
    block_out = here.join_homes(*here.send_homes(block_own))

    grad_down = dot(mid, dy_all, 0, 0, BF16)
    if quarters == experts:
        grad_down = grad_down.reshape(quarters, shards, hidden_part, features)
    else:
        grad_down = jnp.transpose(
            grad_down.reshape(experts, shards, hidden_part, quarters, features // quarters),
            (3, 1, 0, 2, 4),
        )
    dy_all, down_w, grad_down = together(dy_all, down_w, grad_down)
    got_grad_down = here.exchange(grad_down)
    grad_gate_v, grad_up_v, grad_share = experts_backward(dy_all, down_w, gate_v, up_v, shares)
    share_got = here.swap(grad_share[rows:])
    grad_share = grad_share[:rows] + share_got

    def expert_grad(back):
        return dot(back, b_all, 0, 0, BF16).reshape(quarters, -1, features)

    grad_gate = expert_grad(grad_gate_v)
    grad_up = expert_grad(grad_up_v)
    grad_gate_v, grad_up_v, grad_gate, grad_up, got_grad_down = together(
        grad_gate_v, grad_up_v, grad_gate, grad_up, got_grad_down
    )
    held_down = jnp.sum(got_grad_down.astype(F32), axis=0).astype(BF16)
    db_other = (
        dot(grad_gate_v[rows:], gate_w, 1, 1) + dot(grad_up_v[rows:], up_w, 1, 1)
    ).astype(BF16)
    db_got = here.swap(db_other)
    got_grad_gate = here.exchange(grad_gate)
    db_own = dot(grad_gate_v[:rows], gate_w, 1, 1) + dot(grad_up_v[:rows], up_w, 1, 1)

    hot_own, share_own = route_hot[:rows], gate_share[:rows]
    grad_gates = jnp.sum(grad_share[:, None, :] * hot_own, axis=2)
    grad_chosen = share_own * (
        grad_gates - jnp.sum(share_own * grad_gates, axis=1, keepdims=True)
    )
    grad_logits = jnp.sum(grad_chosen[:, :, None] * hot_own, axis=1).astype(BF16)
    grad_router = dot(grad_logits, b_own, 0, 0)
    db = db_own + db_got.astype(F32) + dot(grad_logits, router_w, 1, 1)
    dh, grad_gain_two = norm_back(h_own, scale_two, gain_two, db)
    dh = dh + dy_own.astype(F32)
    dattn = dh.astype(BF16)

    qkv_w_got = here.swap(qkv_w)
    do_t = dot(out_w, dattn, 1, 1, BF16)
    do_mine, do_other = here.halves(do_t, 0)
    do_t = here.ordered(do_mine, here.swap(do_other), 1)
    do_t = here.chip_exchange(do_t, 0, 1)
    grad_out = dot(dattn, o_own, 0, 1, BF16)
    out_mine, out_other = here.halves(grad_out, 0)
    grad_out = (out_mine.astype(F32) + here.swap(out_other).astype(F32)).astype(BF16)
    sum_down = here.gather(here.scatter(held_down))
    back_heads, back_rows, back_got = [], [], []
    for head in range(heads):
        g_h = do_t[head * o_heads[0].shape[0] : (head + 1) * o_heads[0].shape[0]]
        if head == 0:
            g_h, grad_out, qkv_w_got = together(g_h, grad_out, qkv_w_got)
        elif head == 1:
            g_h, block_out, got_grad_gate, grad_out, back_heads[0] = together(
                g_h, block_out, got_grad_gate, grad_out, back_heads[0]
            )
            got_grad_out = here.exchange(grad_out.reshape(quarters, -1, features))
            total_gate = here.scatter(sum_parts(got_grad_gate, shards))
        else:
            g_h, back_heads[-1] = together(g_h, back_heads[-1])
        if head == heads // 2:
            g_h, got_grad_out, grad_up, total_gate = together(
                g_h, got_grad_out, grad_up, total_gate
            )
            sum_gate = here.gather(total_gate)
            got_grad_up = here.exchange(grad_up)
            total_out = here.scatter(sum_parts(got_grad_out, shards))
        back_h = attend_backward(
            head, group, qkv_t, o_heads[head], g_h, stats[head], starts, backward_ranges
        )
        back_h = here.chip_exchange(back_h, 1, 0)
        back_heads.append(back_h)
        mine, other = here.halves(back_h, 1)
        back_rows.append(mine)
        back_got.append(here.swap(other))

    grad_qkv = jnp.stack(
        [
            dot(back_h, normed, 1, 0, BF16).reshape(here.chips, -1, features)
            for back_h in back_heads
        ],
        axis=1,
    ).reshape(quarters, -1, features)
    grad_qkv, got_grad_up = together(grad_qkv, got_grad_up)
    total_up = here.scatter(sum_parts(got_grad_up, shards))
    got_grad_qkv = here.exchange(grad_qkv)
    da = dot(here.head_order(back_rows, heads), qkv_w, 0, 1) + dot(
        here.head_order(back_got, heads), qkv_w_got, 0, 1
    )
    dx, grad_gain_one = norm_back(x_wide, scale_one, gain_one, da)
    dx_parts, dx_blocks = here.send_homes((dx + dh).astype(BF16))
    got_grad_qkv, dx_blocks[0] = together(got_grad_qkv, dx_blocks[0])

    grad_small = jnp.concatenate([grad_gain_one[None], grad_gain_two[None], grad_router], axis=0)
    grad_small = jnp.pad(grad_small, ((0, 16 - grad_small.shape[0]), (0, 0))).astype(BF16)
    grad_small = jnp.transpose(grad_small.reshape(16, shards, shard_rows), (1, 0, 2))
    held_qkv = sum_parts(got_grad_qkv, shards)
    held_qkv, total_up, total_out = together(held_qkv, total_up, total_out)
    held_qkv = jnp.concatenate([held_qkv, grad_small], axis=1)
    total = here.reduce_along(held_qkv)
    total, dx_blocks[1] = together(total, dx_blocks[1])
    input_grad = here.join_homes(dx_parts, dx_blocks)
    sum_up_out = here.gather(jnp.concatenate([total_up, total_out], axis=0))
    cut = total_up.shape[0]
    mine = jnp.stack([total] + [here.across(total, key) for key in range(1, quarters)])
    out_query, out_key, out_value, small_sum = spread_rows(
        mine, here.swap(mine), here.quarter, core, width_k // HEAD, group
    )
    if (features // 2) % 128 or (features // 2 // quarters) % 16:
        out_out = sum_up_out[:, :, cut:].astype(F32)
        out_out = jnp.transpose(out_out, (3, 1, 0, 2)).reshape(shard_rows, features)
    else:
        out_out = spread_out(sum_up_out, cut)
    if quarters == experts:
        out_down = sum_down.astype(F32).reshape(experts, 2 * hidden_part, features)
    else:
        out_down = jnp.transpose(sum_down.astype(F32), (2, 1, 3, 0, 4)).reshape(
            experts, 2 * hidden_part, features
        )
    return (
        block_out[:, None],
        input_grad[:, None],
        small_sum[0],
        out_query,
        out_key,
        out_value,
        out_out,
        small_sum[1],
        small_sum[2 : 2 + experts].T,
        spread_experts(sum_gate, experts, shards, hidden_all),
        spread_experts(sum_up_out, experts, shards, hidden_all),
        out_down,
    )


def solution(mesh):
    chips = mesh.shape["rep"] // 2
    mesh = jax.sharding.Mesh(
        mesh.devices.reshape(chips, 2, mesh.shape["shard"]), ("chip", "core", "shard")
    )
    in_specs = (
        P(None, PLANE, "shard", None),
        P(None, PLANE, "shard", None),
        P(None, PLANE, "shard", None),
        P(),
        P("shard"),
        P("shard", None),
        P("shard", None),
        P("shard", None),
        P("shard", None),
        P("shard"),
        P("shard", None),
        P(None, "shard", None),
        P(None, "shard", None),
        P(None, "shard", None),
    )
    out_specs = (
        P(None, PLANE, "shard", None),
        P(None, PLANE, "shard", None),
        P("shard"),
        P("shard", None),
        P("shard", None),
        P("shard", None),
        P("shard", None),
        P("shard"),
        P("shard", None),
        P(None, "shard", None),
        P(None, "shard", None),
        P(None, "shard", None),
    )
    return jax.shard_map(local, mesh=mesh, in_specs=in_specs, out_specs=out_specs, check_vma=False)
```
